32 devices in a mesh: elem: 8 (over z, x), crm: 4 (over y, core).
Axes of the slice: x: 2, y: 2, z: 4, core: 2. Of those that a mesh axis runs over, the one named last changes fastest.
Arguments:
- state: float32 [128, 64, 320], P('elem', 'crm'), may hold values from -6 to 6
- wind: float32 [128, 64, 128], P('elem', 'crm'), may hold values from -0.15 to 0.15
- dyn_mix: bfloat16 [320, 320], replicated, may hold values from -0.15625 to 0.15625
- owner: int32 [512, 1], P(('elem', 'crm')), may hold values from 0 to 3; in each aligned block of 16 rows (0 to 15, 16 to 31, ...) at most 4 rows name the same one
- crm_state: bfloat16 [512, 32, 320], P(('elem', 'crm')), may hold values from -6 to 6
- crm_mix: bfloat16 [320, 320], replicated, may hold values from -0.3125 to 0.3125
Outputs:
- dyn_state: float32 [128, 64, 320], P('elem', 'crm')
- crm_next: bfloat16 [512, 32, 320], P(('elem', 'crm'))
The draws below stay inside these ranges and needn't reach their ends.
Inputs may be any that keep to these rules, and one draw needn't show every extreme that they name: Within the 16 columns of one device (an aligned block) no owner is named more than 4 times, a bound that some block reaches.
All inputs are finite; a program needn't handle non-finite values.
Results may differ from the reference program's by a relative error of at most 0.0021.
Values sent between devices are 32-bit elements; how exact they have to be, the bound alone decides.
No kernel may reach another device: no remote copies, remote signals or barrier semaphores. Data moves between devices by JAX's collectives and lax.ppermute only.
A program may use at most 64 MiB of HBM per device.

```python
import math
import jax
import jax.numpy as jnp
import numpy as np
from jax import lax

LEV = 64
CRM_COLS = 32
SUB = 4
EXD = 4
EYD = 4
C = 320
COL_DEV = 16
CAP = 4
COLS = 512
SLOTS = 512
NXN = 128
NYN = 64
N_ELEM = 8
N_CRM = 4


def block_levels(own_key, extent, cuts, smallest, largest):
    def one(axis_at, blocks):
        draws = jax.random.uniform(jax.random.fold_in(jax.random.fold_in(own_key, 6), axis_at), (blocks,), jnp.float32, smallest / len(cuts), largest / len(cuts))
        return jnp.repeat(jnp.exp(draws), extent[axis_at] // blocks).reshape((-1,) + (1,) * (len(extent) - axis_at - 1))

    level = one(*cuts[0])
    for cut in cuts[1:]:
        level = level * one(*cut)
    return level


def assign_block(rng, own, number, rows, amount, top, most, slope):
    order = jax.random.permutation(rng, amount)
    crowded, ordinary = shares(amount, rows * top, most, slope, True), shares(amount, rows * top, most, slope, False)
    places = jnp.arange(amount)

    def named(tallies, offset_by):
        used = int((tallies > 0).sum())
        fixed = max(1, used // 4)
        shifted = fixed + (places - fixed + offset_by * (used - fixed)) % max(1, amount - fixed)
        return jnp.zeros((amount,), jnp.int32).at[order[jnp.where(places < fixed, places, shifted)]].set(jnp.asarray(tallies, jnp.int32))

    tallies = jnp.where(number % 4 == 0, named(crowded, number // 4), named(ordinary, number - number // 4 - 1))
    mixed = jax.random.permutation(jax.random.fold_in(own, 3), amount)
    source_of, receiver = mixed[0:amount // 2 * 2:2], mixed[1:amount // 2 * 2:2]
    slack = jnp.minimum(tallies[source_of] - 1, most - tallies[receiver]) // 2
    slack = jnp.where((source_of == order[0]) | (receiver == order[0]) | (tallies[receiver] == 0), 0, jnp.maximum(slack, 0))
    shifted = jax.random.randint(jax.random.fold_in(own, 4), (amount // 2,), 0, 1 << 20) % (slack + 1)
    tallies = tallies.at[source_of].add(-shifted).at[receiver].add(shifted)
    labels = jnp.searchsorted(jnp.cumsum(tallies), jnp.arange(rows * top), side="right").astype(jnp.int32)
    table = labels.reshape(top, rows).T
    table = table[jax.random.permutation(jax.random.fold_in(own, 1), rows)]
    offset_by = jax.random.randint(jax.random.fold_in(own, 2), (rows, 1), 0, top)
    return jnp.take_along_axis(table, (jnp.arange(top)[None, :] + offset_by) % top, axis=1)


def shares(count, total, bound, lean, full):
    weights = [(1 << 20) // math.isqrt(grade ** lean) + 1 for grade in range(1, count + 1)]
    largest = bound if full else min(bound, max(-(-total // count), total * weights[0] // sum(weights)))
    least = 1 if total - largest >= count - 1 else 0
    given, rest = [largest] + [least] * (count - 1), total - largest - least * (count - 1)
    while rest > 0:
        movable = [i for i in range(1, count) if given[i] < largest] or [i for i in range(1, count) if given[i] < bound]
        whole, budget = sum([weights[i] for i in movable]), rest
        for i in movable:
            extra = min(bound - given[i], max(1, budget * weights[i] // whole), rest)
            given[i] = given[i] + extra
            rest = rest - extra
    return np.array(given)


def noise(own_key, dims, scale, reach, split=(), kind=jnp.bfloat16):
    values = jax.random.normal(own_key, dims, jnp.float32) * scale
    if len(split) > 0:
        values = block_levels(own_key, dims, split, -0.22, 0.18) * values
    return jnp.clip(values, min=-reach, max=reach).astype(kind)


def setup_inputs(seed: int = 0) -> dict:
    streams_of = jax.random.split(jax.random.key(seed), 7)
    state = noise(streams_of[0], (NXN, NYN, C), 1.0, 6.0, ((0, 8), (1, 4)), jnp.float32)
    wind = jnp.clip(jax.random.uniform(streams_of[1], (NXN, NYN, 2 * LEV), jnp.float32, -0.15, 0.15) * block_levels(streams_of[1], (NXN, NYN, 2 * LEV), ((0, 8), (1, 4)), -0.4, 0.0), -0.15, 0.15)
    dyn_mix = noise(streams_of[2], (C, C), (4 * C) ** -0.5, 0.15625)
    owner_keys = jax.random.split(jax.random.fold_in(streams_of[3], 1), COLS // COL_DEV)
    owner_turns = jax.random.permutation(jax.random.fold_in(streams_of[3], 3), COLS // COL_DEV)
    owner = jax.vmap(lambda own, number: assign_block(jax.random.fold_in(streams_of[3], 2), own, number, COL_DEV, N_CRM, 1, CAP, 1))(owner_keys, owner_turns).reshape((COLS, 1))
    crm_state = noise(streams_of[4], (SLOTS, CRM_COLS, C), 1.0, 6.0, ((0, 32),))
    crm_mix = noise(streams_of[5], (C, C), C ** -0.5, 0.3125)
    return {"state": state, "wind": wind, "dyn_mix": dyn_mix, "owner": owner, "crm_state": crm_state, "crm_mix": crm_mix}


HIGHEST = lax.Precision.HIGHEST
CRM_STEP = 0.5
DIFFUSION = 0.2
RELAXATION = 1.0
COUPLING = 0.5

def gll_derivative():
    points = np.array([-1.0, -1.0 / np.sqrt(5.0), 1.0 / np.sqrt(5.0), 1.0])
    barycentric = np.array([1.0 / np.prod([points[node_index] - points[other_node] for other_node in range(4) if other_node != node_index]) for node_index in range(4)])
    derivative = np.zeros((4, 4))
    for node_index in range(4):
        for other_node in range(4):
            if other_node != node_index:
                derivative[node_index, other_node] = barycentric[other_node] / barycentric[node_index] / (points[node_index] - points[other_node])
        derivative[node_index, node_index] = -np.sum(derivative[node_index])
    return derivative

def dyn_rate(field, wind, dyn_mix):
    size_x, size_y, channels = field.shape
    levels = wind.shape[2] // 2
    derivative = jnp.asarray(gll_derivative(), field.dtype)
    along_x = jnp.einsum('ij,ajyc->aiyc', derivative, field.reshape(size_x // 4, 4, size_y, channels), precision=HIGHEST).reshape(field.shape)
    along_y = jnp.einsum('ij,xbjc->xbic', derivative, field.reshape(size_x, size_y // 4, 4, channels), precision=HIGHEST).reshape(field.shape)
    shaped = (size_x, size_y, channels // levels, levels)
    advect = wind[:, :, None, :levels] * along_x.reshape(shaped) + wind[:, :, None, levels:] * along_y.reshape(shaped)
    mixing = jnp.dot(field.astype(jnp.bfloat16).reshape(-1, channels), dyn_mix, preferred_element_type=jnp.float32).reshape(field.shape)
    return mixing - advect.reshape(field.shape)

def edge_average(padded, node_phase):
    inner_count = padded.shape[0] - 2
    position = (jnp.arange(inner_count) + node_phase) % 4
    upper_edge = (position == 3)[:, None, None]
    lower_edge = (position == 0)[:, None, None]
    middle = padded[1:-1]
    partner = jnp.where(upper_edge, padded[2:], padded[:-2])
    halfway = jnp.where(upper_edge | lower_edge, 0.5 * (middle + partner), middle)
    inner_y = halfway.shape[1] - 2
    position_y = (jnp.arange(inner_y) + node_phase) % 4
    upper_y = (position_y == 3)[None, :, None]
    lower_y = (position_y == 0)[None, :, None]
    middle_y = halfway[:, 1:-1]
    partner_y = jnp.where(upper_y, halfway[:, 2:], halfway[:, :-2])
    return jnp.where(upper_y | lower_y, 0.5 * (middle_y + partner_y), middle_y)

def column_forcing(field):
    size_x, size_y, channels = field.shape
    quadrature = np.array([1.0, 5.0, 5.0, 1.0]) / 6.0
    weights = jnp.asarray(np.outer(quadrature, quadrature) / 4.0, field.dtype)
    blocks = field.reshape(size_x // 4, 4, size_y // 4, 4, channels)
    return jnp.einsum('ij,aibjc->abc', weights, blocks, precision=HIGHEST)

def crm_run(states, forcing, crm_mix):
    current = states.astype(jnp.float32)
    slot_count, columns, channels = current.shape
    accumulated = jnp.zeros((slot_count, channels), jnp.float32)
    for substep in range(SUB):
        rounded = current.astype(jnp.bfloat16)
        mixing = jnp.dot(rounded.reshape(-1, channels), crm_mix, preferred_element_type=jnp.float32).reshape(current.shape)
        spread = jnp.roll(current, 1, axis=1) + jnp.roll(current, -1, axis=1) - 2.0 * current
        column_mean = lax.optimization_barrier(jnp.mean(current, axis=1))
        current = current + CRM_STEP * (jnp.tanh(mixing) + DIFFUSION * spread + RELAXATION * (forcing - column_mean)[:, None, :])
        accumulated = accumulated + (lax.optimization_barrier(jnp.mean(current, axis=1)) - forcing)
    return (current.astype(jnp.bfloat16), accumulated / SUB)

def wrap_pad(update):
    return jnp.pad(update, ((1, 1), (1, 1), (0, 0)), mode='wrap')

def reference(state, wind, dyn_mix, owner, crm_state, crm_mix):
    first = edge_average(wrap_pad(state + dyn_rate(state, wind, dyn_mix)), 0)
    second = edge_average(wrap_pad(state + dyn_rate(first, wind, dyn_mix)), 0)
    forcing_grid = column_forcing(second)
    grid_x, grid_y, channels = forcing_grid.shape
    devices = N_ELEM * N_CRM

    def to_columns(grid):
        return grid.reshape(N_ELEM, EXD, N_CRM, EYD, -1).transpose(0, 2, 1, 3, 4).reshape(devices * EXD * EYD, -1)

    def to_grid(column_rows):
        return column_rows.reshape(N_ELEM, N_CRM, EXD, EYD, -1).transpose(0, 2, 1, 3, 4).reshape(grid_x, grid_y, -1)
    forcing = to_columns(forcing_grid)
    owners = owner.reshape(devices, COL_DEV)
    onehot = (owners[:, :, None] == jnp.arange(N_CRM, dtype=jnp.int32)[None, None, :]).astype(jnp.int32)
    earlier = jnp.cumsum(onehot, axis=1) - onehot
    position_rank = lax.optimization_barrier(jnp.sum(earlier * onehot, axis=2))
    source = jnp.arange(devices, dtype=jnp.int32)
    target = (source // N_CRM)[:, None] * N_CRM + owners
    slot_index = (target * (N_CRM * CAP) + (source % N_CRM)[:, None] * CAP + position_rank).reshape(-1).astype(jnp.int32)
    gathered = jnp.take(crm_state, slot_index, axis=0).reshape(devices, COL_DEV, CRM_COLS, channels)

    def run_block(inputs):
        return crm_run(inputs[0], inputs[1], crm_mix)
    renewed, tendency = lax.map(run_block, (gathered, forcing.reshape(devices, COL_DEV, channels)))
    crm_next = crm_state.at[slot_index].set(renewed.reshape(-1, CRM_COLS, channels))
    tend_grid = to_grid(tendency.reshape(-1, channels))
    node_tend = jnp.repeat(jnp.repeat(tend_grid, 4, axis=0), 4, axis=1)
    coupled = second + COUPLING * node_tend
    third = edge_average(wrap_pad(coupled + dyn_rate(coupled, wind, dyn_mix)), 0)
    return (third, crm_next)
```

```python
import functools

import jax
import jax.numpy as jnp
import numpy as np
from jax import lax
from jax.experimental import pallas as pl
from jax.experimental.pallas import tpu as pltpu
from jax.sharding import PartitionSpec as P

SUB = 4
HIGHEST = lax.Precision.HIGHEST
CRM_STEP = 0.5
DIFFUSION = 0.2
COUPLING = 0.5
NODES = 4


def gll_derivative():
    points = np.array([-1.0, -1.0 / np.sqrt(5.0), 1.0 / np.sqrt(5.0), 1.0])
    barycentric = np.array(
        [
            1.0 / np.prod([points[i] - points[j] for j in range(NODES) if j != i])
            for i in range(NODES)
        ]
    )
    derivative = np.zeros((NODES, NODES))
    for i in range(NODES):
        for j in range(NODES):
            if j != i:
                derivative[i, j] = barycentric[j] / barycentric[i] / (points[i] - points[j])
        derivative[i, i] = -np.sum(derivative[i])
    return derivative


DERIV = [[float(value) for value in row] for row in gll_derivative().astype(np.float32)]
FIRST, LAST = DERIV[0][0], DERIV[3][3]
QUADRATURE = np.array([1.0, 5.0, 5.0, 1.0]) / 6.0


def lane_tiles(channels, width):
    return [(at, min(at + width, channels)) for at in range(0, channels, width)]


def winds(pair, levels):
    along_x, along_y = pair[:, :levels], pair[:, levels:]
    return (
        jnp.concatenate([along_x, along_x], axis=1),
        jnp.concatenate([along_y, along_y], axis=1),
    )


def full_winds(pair, levels, channels):
    along_x, along_y = winds(pair, levels)
    count = -(-channels // (2 * levels))
    return (
        jnp.concatenate([along_x] * count, axis=1)[:, :channels],
        jnp.concatenate([along_y] * count, axis=1)[:, :channels],
    )


def dx_rows(rows):
    out = []
    for i in range(NODES):
        total = None
        for j in range(NODES):
            if DERIV[i][j] != 0.0 and not (i == j and abs(DERIV[i][j]) < 1e-6):
                term = DERIV[i][j] * rows[j]
                total = term if total is None else total + term
        out.append(total)
    return out


def sublane_coefficients(rows, width):
    position = lax.broadcasted_iota(jnp.int32, (rows, width), 0) & 3
    table = []
    for shift in range(-3, 4):
        value = jnp.zeros((rows, width), jnp.float32)
        for at in range(NODES):
            if 0 <= at + shift < NODES:
                value = jnp.where(position == at, DERIV[at][at + shift], value)
        table.append(value)
    return table


def dsub(field, table):
    width = field.shape[1]
    blocks = []
    for at in range(0, field.shape[0], 8):
        part = field[at : at + 8]
        total = None
        for index, shift in enumerate(range(-3, 4)):
            moved = part if shift == 0 else pltpu.roll(part, (-shift) % 8, 0)
            term = table[index][:, :width] * moved
            total = term if total is None else total + term
        blocks.append(total)
    return blocks[0] if len(blocks) == 1 else jnp.concatenate(blocks, axis=0)


def sub_average(field):
    rows = field.shape[0]
    position = lax.broadcasted_iota(jnp.int32, field.shape, 0)
    phase = position & 3
    upper = (phase == 3) & (position < rows - 1)
    lower = (phase == 0) & (position > 0)
    ahead = pltpu.roll(field, rows - 1, 0)
    behind = pltpu.roll(field, 1, 0)
    partner = jnp.where(upper, ahead, jnp.where(lower, behind, field))
    return 0.5 * (field + partner)


def average_rows(ref, size_x, size_y):
    for at in range(NODES - 1, size_x - 1, NODES):
        low, high = pl.ds(at * size_y, size_y), pl.ds((at + 1) * size_y, size_y)
        mean = 0.5 * (ref[low, :] + ref[high, :])
        ref[low, :] = mean
        ref[high, :] = mean


def edge_rows(rows, first, last):
    position = lax.broadcasted_iota(jnp.int32, rows.shape, 0)
    count = rows.shape[0]
    return rows + jnp.where(
        position == 0, first, jnp.where(position == count - 1, last, 0.0)
    )


def local_update(base_ref, field_ref, mixed_ref, wind_ref, out_ref, size_x, size_y, levels, average):
    channels = field_ref.shape[1]
    table = sublane_coefficients(8, 2 * levels)
    for element in range(size_x // NODES):
        rows = [pl.ds((NODES * element + i) * size_y, size_y) for i in range(NODES)]
        wind = [winds(wind_ref[row, :], levels) for row in rows]
        for begin, end in lane_tiles(channels, 2 * levels):
            width = end - begin
            values = [field_ref[row, begin:end] for row in rows]
            slopes = dx_rows(values)
            for i in range(NODES):
                along_x, along_y = wind[i][0][:, :width], wind[i][1][:, :width]
                result = (
                    base_ref[rows[i], begin:end]
                    + mixed_ref[rows[i], begin:end]
                    - (along_x * slopes[i] + along_y * dsub(values[i], table))
                )
                out_ref[rows[i], begin:end] = sub_average(result) if average else result


def to_bf16(value):
    return value.astype(jnp.bfloat16)


def mix_all(field, mix):
    return jnp.dot(to_bf16(field), mix, preferred_element_type=jnp.float32)


def begin_kernel(size_x, size_y, levels, state, wind, mix, partial, to_left, to_right, mixed):
    channels = state.shape[1]
    mixed[...] = mix_all(state[...], mix[...])
    local_update(state, state, mixed, wind, partial, size_x, size_y, levels, True)
    average_rows(partial, size_x, size_y)
    for out, column, near, row in ((to_left, 0, 0, 0), (to_right, size_y - 1, size_y - NODES, 3)):
        slope = None
        for j in range(NODES):
            value = column_of(partial, near + j, size_x, size_y)
            term = DERIV[row][j] * value
            slope = term if slope is None else slope + term
        out[:, 0:channels] = column_of(partial, column, size_x, size_y)
        out[:, channels : 2 * channels] = slope
        out[:, 2 * channels : 3 * channels] = column_of(state, column, size_x, size_y)
        out[:, 3 * channels : 3 * channels + 2 * levels] = column_of(
            wind, column, size_x, size_y
        )


def column_of(ref, y, size_x, size_y):
    return jnp.concatenate(
        [ref[x * size_y + y : x * size_y + y + 1, :] for x in range(size_x)], axis=0
    )


def column_parts(message, channels, levels):
    return (
        message[:, 0:channels],
        message[:, channels : 2 * channels],
        message[:, 2 * channels : 3 * channels],
        message[:, 3 * channels : 3 * channels + 2 * levels],
    )


def turn_kernel(
    size_x, size_y, levels, partial, state, wind, from_left, from_right, to_up, to_down, field, line
):
    channels = state.shape[1]
    left_value, left_slope, left_state, left_wind = column_parts(from_left, channels, levels)
    right_value, right_slope, right_state, right_wind = column_parts(from_right, channels, levels)
    first_column = column_of(partial, 0, size_x, size_y)
    last_column = column_of(partial, size_y - 1, size_x, size_y)
    left_change = 0.5 * (left_value - first_column)
    right_change = 0.5 * (right_value - last_column)
    left_slope = left_slope - LAST * left_change
    right_slope = right_slope - FIRST * right_change
    for x in range(size_x):
        row = pl.ds(x * size_y, size_y)
        field[row, :] = edge_rows(
            partial[row, :], left_change[x : x + 1], right_change[x : x + 1]
        )
    span = 2 * channels + 2 * levels
    pieces = span // (2 * levels)
    for out, x, near, kind in ((to_up, 0, 0, 0), (to_down, size_x - 1, size_x - NODES, 3)):
        row = pl.ds(x * size_y, size_y)
        slope = None
        for j in range(NODES):
            term = DERIV[kind][j] * field[pl.ds((near + j) * size_y, size_y), :]
            slope = term if slope is None else slope + term
        along_x, _ = full_winds(wind[row, :], levels, channels)
        out[:, 0:channels] = field[row, :]
        out[:, channels : 2 * channels] = state[row, :] - along_x * slope
        out[:, 2 * channels : span] = wind[row, :]
        corners = (
            (left_slope, left_state, left_wind, slope[0:1]),
            (right_slope, right_state, right_wind, slope[size_y - 1 : size_y]),
        )
        for side, (side_slope, side_state, side_wind, corner_slope) in enumerate(corners):
            pair = side_wind[x : x + 1]
            corner_x, _ = full_winds(pair, levels, channels)
            line[side : side + 1, 0:channels] = side_slope[x : x + 1]
            line[side : side + 1, channels : 2 * channels] = (
                side_state[x : x + 1] - corner_x * corner_slope
            )
            line[side : side + 1, 2 * channels : span] = pair
            for piece in range(pieces):
                at = side * pieces + piece
                out[at : at + 1, span : span + 2 * levels] = line[
                    side : side + 1, piece * 2 * levels : (piece + 1) * 2 * levels
                ]
        used = 2 * pieces
        if used < size_y:
            out[used:size_y, span : span + 2 * levels] = jnp.zeros(
                (size_y - used, 2 * levels), jnp.float32
            )


def cloud_run(states, forcing, mix, tendency, columns, group):
    slots = forcing.shape[0]
    means = {}
    totals = {}
    for step in range(SUB):
        for begin in range(0, slots, group):
            span = pl.ds(begin * columns, group * columns)
            mixed = mix_all(states[span, :], mix[...])
            for slot in range(begin, begin + group):
                rows = pl.ds(slot * columns, columns)
                value = states[rows, :]
                push = forcing[slot : slot + 1, :]
                if step == 0:
                    mean = jnp.mean(value, axis=0, keepdims=True)
                else:
                    mean = means[slot]
                near = slice((slot - begin) * columns, (slot - begin + 1) * columns)
                spread = pltpu.roll(value, 1, 0) + pltpu.roll(value, columns - 1, 0) - 2.0 * value
                value = value + CRM_STEP * (
                    jnp.tanh(mixed[near]) + DIFFUSION * spread + (push - mean)
                )
                states[rows, :] = value
                mean = jnp.mean(value, axis=0, keepdims=True)
                means[slot] = mean
                totals[slot] = mean - push if step == 0 else totals[slot] + (mean - push)
    if tendency is not None:
        for slot in range(slots):
            tendency[slot : slot + 1, :] = totals[slot] / SUB


def home_kernel(
    size_x, size_y, levels, columns, groups, *refs
):
    (
        rank, field, state, wind, mix, cloud_mix, from_left, from_right, from_up, from_down,
        gather, spread, occupied, own_clouds,
    ) = refs[:14]
    clouds = refs[14 : 14 + groups - 1]
    out, to_left, to_right = refs[14 + groups - 1 : 17 + groups - 1]
    sends = refs[17 + groups - 1]
    mixed, work, total, reduced, forcing, tendency, cloud = refs[18 + groups - 1 :]
    channels = state.shape[1]
    slots = gather.shape[0]
    capacity = slots // groups
    span = 2 * channels + 2 * levels
    pieces = span // (2 * levels)
    last_row = pl.ds((size_x - 1) * size_y, size_y)
    first_row = pl.ds(0, size_y)
    cloud[pl.ds(0, capacity * columns), :] = (
        own_clouds[pl.ds(rank[0] * capacity * columns, capacity * columns), :].astype(jnp.float32)
    )
    for k in range(1, groups):
        cloud[pl.ds(k * capacity * columns, capacity * columns), :] = clouds[k - 1][...]
    up_change = 0.5 * (from_up[:, 0:channels] - field[first_row, :])
    down_change = 0.5 * (from_down[:, 0:channels] - field[last_row, :])
    work[...] = field[...]
    work[first_row, :] = field[first_row, :] + up_change
    work[last_row, :] = field[last_row, :] + down_change
    mixed[...] = mix_all(work[...], mix[...])
    local_update(state, work, mixed, wind, total, size_x, size_y, levels, True)
    table = sublane_coefficients(8, channels)
    corner = {}
    for name, message in (("up", from_up), ("down", from_down)):
        for side in range(2):
            line = jnp.concatenate(
                [
                    message[side * pieces + p : side * pieces + p + 1, span : span + 2 * levels]
                    for p in range(pieces)
                ],
                axis=1,
            )
            corner[name, side] = (
                line[:, 0:channels],
                line[:, channels : 2 * channels],
                line[:, 2 * channels : span],
            )
    side_slopes = []
    for side, (message, y, factor) in enumerate(
        ((from_left, 0, LAST), (from_right, size_y - 1, FIRST))
    ):
        value, slope, side_state, side_wind = column_parts(message, channels, levels)
        column = column_of(work, y, size_x, size_y)
        slope = slope - factor * (value - column_of(field, y, size_x, size_y))
        slope = edge_rows(
            slope,
            0.5 * (corner["up", side][0] - slope[0:1]),
            0.5 * (corner["down", side][0] - slope[size_x - 1 : size_x]),
        )
        side_slopes.append(slope)
        along_x, along_y = full_winds(side_wind, levels, channels)
        beyond = (
            side_state
            + column_of(mixed, y, size_x, size_y)
            - (along_x * dsub(column, table) + along_y * slope)
        )
        for x in range(size_x):
            at = slice(x * size_y + y, x * size_y + y + 1)
            total[at, :] = 0.5 * (total[at, :] + beyond[x : x + 1])
    for name, message, row, change, factor, x in (
        ("up", from_up, first_row, up_change, LAST, 0),
        ("down", from_down, last_row, down_change, FIRST, size_x - 1),
    ):
        along_x, along_y = full_winds(message[:, 2 * channels : span], levels, channels)
        slope_y = dsub(work[row, :], table)
        beyond = (
            message[:, channels : 2 * channels]
            + mixed[row, :]
            + factor * along_x * change
            - along_y * slope_y
        )
        beyond = sub_average(beyond)
        ends = []
        for side, y in ((0, 0), (1, size_y - 1)):
            _, part, pair = corner[name, side]
            corner_x, corner_y = full_winds(pair, levels, channels)
            value = (
                part
                + mixed[pl.ds(x * size_y + y, 1), :]
                + factor * corner_x * change[y : y + 1]
                - corner_y * side_slopes[side][x : x + 1]
            )
            ends.append(0.5 * (value - beyond[y : y + 1]))
        beyond = edge_rows(beyond, ends[0], ends[1])
        total[row, :] = 0.5 * (total[row, :] + beyond)
    average_rows(total, size_x, size_y)
    for element in range(size_x // NODES):
        value = None
        for i in range(NODES):
            term = float(QUADRATURE[i]) * total[pl.ds((NODES * element + i) * size_y, size_y), :]
            value = term if value is None else value + term
        reduced[pl.ds(element * size_y, size_y), :] = value
    forcing[...] = jnp.dot(
        gather[...], reduced[...], precision=HIGHEST, preferred_element_type=jnp.float32
    )
    mixed[...] = mix_all(total[...], mix[...])
    local_update(total, total, mixed, wind, work, size_x, size_y, levels, False)
    cloud_run(cloud, forcing, cloud_mix, tendency, columns, capacity if slots % 4 else 4)
    tend = tendency[...]
    change = COUPLING * (tend + mix_all(tend, mix[...]))
    reduced[...] = jnp.dot(
        spread[...], change, precision=HIGHEST, preferred_element_type=jnp.float32
    )
    for x in range(size_x):
        row = pl.ds(x * size_y, size_y)
        element = pl.ds((x // NODES) * size_y, size_y)
        out[row, :] = sub_average(work[row, :] + reduced[element, :])
    average_rows(out, size_x, size_y)
    for ref, y, block in ((to_left, 0, 1), (to_right, size_y - 1, groups - 1)):
        ref[0:size_x, 0:channels] = column_of(out, y, size_x, size_y)
        rows = pl.ds(block * capacity, capacity)
        ref[size_x : size_x + capacity, 0:channels] = forcing[rows, :]
        ref[size_x : size_x + capacity, channels : channels + 1] = occupied[rows, :]
    sends[:, 0:channels] = forcing[...]
    sends[:, channels : channels + 1] = occupied[...]


def last_turn_kernel(size_x, size_y, partial, from_left, from_right, to_up, to_down, field):
    channels = partial.shape[1]
    left = 0.5 * (
        from_left[0:size_x, 0:channels] - column_of(partial, 0, size_x, size_y)
    )
    right = 0.5 * (
        from_right[0:size_x, 0:channels] - column_of(partial, size_y - 1, size_x, size_y)
    )
    for x in range(size_x):
        row = pl.ds(x * size_y, size_y)
        field[row, :] = edge_rows(partial[row, :], left[x : x + 1], right[x : x + 1])
    to_up[...] = field[pl.ds(0, size_y), :]
    to_down[...] = field[pl.ds((size_x - 1) * size_y, size_y), :]


def finish_kernel(field, from_up, from_down, out):
    other = jnp.where(pl.program_id(0) == 0, from_up[...], from_down[...])
    out[...] = 0.5 * (field[...] + other)


def owner_kernel(columns, groups, *refs):
    rank, states, mix = refs[:3]
    forcings = refs[3 : 3 + groups]
    out, cloud, forcing = refs[3 + groups :]
    channels = states.shape[1]
    slots = forcing.shape[0]
    capacity = slots // groups
    block = capacity * columns
    for k in range(groups):
        place = lax.rem(rank[0] + k, groups)
        start = pl.multiple_of(place * block, block)
        cloud[pl.ds(k * block, block), :] = states[pl.ds(start, block), :].astype(jnp.float32)
        forcing[pl.ds(k * capacity, capacity), :] = forcings[k][:, 0:channels]
    cloud_run(cloud, forcing, mix, None, columns, capacity if slots % 4 else 4)
    for k in range(groups):
        place = lax.rem(rank[0] + k, groups)
        for slot in range(capacity):
            start = pl.multiple_of(place * block + slot * columns, columns)
            used = forcings[k][slot : slot + 1, channels : channels + 1] > 0.5
            rows = pl.ds((k * capacity + slot) * columns, columns)
            old = states[pl.ds(start, columns), :].astype(jnp.float32)
            out[pl.ds(start, columns), :] = to_bf16(jnp.where(used, cloud[rows, :], old))


def widen_kernel(groups, rank, states, *outs):
    block = outs[0].shape[0]
    for k in range(1, groups):
        place = lax.rem(rank[0] + k, groups)
        start = pl.multiple_of(place * block, block)
        outs[k - 1][...] = states[pl.ds(start, block), :].astype(jnp.float32)


VMEM = pltpu.MemorySpace.VMEM
SMEM = pltpu.MemorySpace.SMEM


def call(kernel, outs, scratch, *args, smem=()):
    specs = [
        pl.BlockSpec(memory_space=SMEM if index in smem else VMEM) for index in range(len(args))
    ]
    shapes = [jax.ShapeDtypeStruct(shape, dtype) for shape, dtype in outs]
    return pl.pallas_call(
        kernel,
        out_shape=shapes,
        in_specs=specs,
        out_specs=[pl.BlockSpec(memory_space=VMEM)] * len(shapes),
        scratch_shapes=[pltpu.VMEM(shape, dtype) for shape, dtype in scratch],
    )(*args)


def shift(value, axis, offset):
    count = lax.axis_size(axis)
    return lax.ppermute(value, axis, [(i, (i + offset) % count) for i in range(count)])


def on_device(state, wind, dyn_mix, owner, crm_state, crm_mix):
    f32 = jnp.float32
    size_x, size_y, channels = state.shape
    levels = wind.shape[2] // 2
    nodes = size_x * size_y
    groups = lax.axis_size("crm")
    slots, columns = crm_state.shape[:2]
    capacity = slots // groups
    elements_x, elements_y = size_x // NODES, size_y // NODES
    rank = lax.axis_index("crm").astype(jnp.int32).reshape(1)
    state = state.reshape(nodes, channels)
    wind = wind.reshape(nodes, 2 * levels)
    clouds = crm_state.reshape(slots * columns, channels)

    owners = owner[:, 0]
    onehot = (owners[:, None] == jnp.arange(groups, dtype=jnp.int32)[None, :]).astype(jnp.int32)
    earlier = jnp.cumsum(onehot, axis=0) - onehot
    position_rank = jnp.sum(earlier * onehot, axis=1)
    slot_index = ((rank[0] - owners) % groups) * capacity + position_rank
    selector = (slot_index[None, :] == jnp.arange(slots, dtype=jnp.int32)[:, None]).astype(f32)
    occupied = jnp.sum(selector, axis=1, keepdims=True)
    spread = jnp.repeat(selector, NODES, axis=1)
    weights = jnp.asarray(np.tile(QUADRATURE / 4.0, elements_x * elements_y), f32)
    gather = spread * weights[None, :]
    spread = spread.T

    column_message = ((size_x, 3 * channels + 2 * levels), f32)
    grid = ((nodes, channels), f32)
    partial, to_left, to_right = call(
        functools.partial(begin_kernel, size_x, size_y, levels),
        [grid, column_message, column_message],
        [grid],
        state, wind, dyn_mix,
    )
    from_right = shift(to_left, "crm", -1)
    from_left = shift(to_right, "crm", 1)
    block = ((capacity * columns, channels), f32)
    wide = call(
        functools.partial(widen_kernel, groups),
        [block] * (groups - 1), [], rank, clouds, smem=(0,),
    )
    arrived = [shift(wide[k - 1], "crm", k) for k in range(1, groups)]
    span = 2 * channels + 2 * levels
    row_message = ((size_y, span + 2 * levels), f32)
    to_up, to_down, field = call(
        functools.partial(turn_kernel, size_x, size_y, levels),
        [row_message, row_message, grid],
        [((8, span), f32)],
        partial, state, wind, from_left, from_right,
    )
    from_down = shift(to_up, "elem", -1)
    from_up = shift(to_down, "elem", 1)
    edge = ((size_x + capacity, channels + 1), f32)
    partial, to_left, to_right, sends = call(
        functools.partial(home_kernel, size_x, size_y, levels, columns, groups),
        [grid, edge, edge, ((slots, channels + 1), f32)],
        [
            grid, grid, grid,
            ((elements_x * size_y, channels), f32),
            ((slots, channels), f32),
            ((slots, channels), f32),
            ((slots * columns, channels), f32),
        ],
        rank, field, state, wind, dyn_mix, crm_mix, from_left, from_right, from_up, from_down,
        gather, spread, occupied, clouds, *arrived,
        smem=(0,),
    )
    from_right = shift(to_left, "crm", -1)
    from_left = shift(to_right, "crm", 1)
    blocks = [sends[k * capacity : (k + 1) * capacity] for k in range(groups)]
    forcings = [blocks[0], from_right[size_x:]]
    forcings += [shift(blocks[k], "crm", -k) for k in range(2, groups - 1)]
    forcings += [from_left[size_x:]]
    to_up, to_down, field = call(
        functools.partial(last_turn_kernel, size_x, size_y),
        [((size_y, channels), f32), ((size_y, channels), f32), grid],
        [],
        partial, from_left, from_right,
    )
    from_down = shift(to_up, "elem", -1)
    from_up = shift(to_down, "elem", 1)
    (crm_next,) = call(
        functools.partial(owner_kernel, columns, groups),
        [((slots * columns, channels), crm_state.dtype)],
        [((slots * columns, channels), f32), ((slots, channels), f32)],
        rank, clouds, crm_mix, *forcings,
        smem=(0,),
    )
    row = pl.BlockSpec((size_y, channels), lambda i: (i * (size_x - 1), 0))
    whole = pl.BlockSpec((size_y, channels), lambda i: (0, 0))
    third = pl.pallas_call(
        finish_kernel,
        grid=(2,),
        out_shape=jax.ShapeDtypeStruct((nodes, channels), f32),
        in_specs=[row, whole, whole],
        out_specs=row,
        input_output_aliases={0: 0},
    )(field, from_up, from_down)
    return (
        third.reshape(size_x, size_y, channels),
        crm_next.reshape(slots, columns, channels),
    )


def solution(mesh):
    return jax.shard_map(
        on_device,
        mesh=mesh,
        in_specs=(
            P("elem", "crm", None),
            P("elem", "crm", None),
            P(),
            P(("elem", "crm"), None),
            P(("elem", "crm"), None, None),
            P(),
        ),
        out_specs=(P("elem", "crm", None), P(("elem", "crm"), None, None)),
        check_vma=False,
    )
```

```python
import functools

import jax
import jax.numpy as jnp
import numpy as np
from jax import lax
from jax.experimental import pallas as pl
from jax.experimental.pallas import tpu as pltpu
from jax.sharding import PartitionSpec as P

SUB = 4
HIGHEST = lax.Precision.HIGHEST
CRM_STEP = 0.5
DIFFUSION = 0.2
COUPLING = 0.5
NODES = 4


def gll_derivative():
    points = np.array([-1.0, -1.0 / np.sqrt(5.0), 1.0 / np.sqrt(5.0), 1.0])
    barycentric = np.array(
        [
            1.0 / np.prod([points[i] - points[j] for j in range(NODES) if j != i])
            for i in range(NODES)
        ]
    )
    derivative = np.zeros((NODES, NODES))
    for i in range(NODES):
        for j in range(NODES):
            if j != i:
                derivative[i, j] = barycentric[j] / barycentric[i] / (points[i] - points[j])
        derivative[i, i] = -np.sum(derivative[i])
    return derivative


DERIV = [[float(value) for value in row] for row in gll_derivative().astype(np.float32)]
FIRST, LAST = DERIV[0][0], DERIV[3][3]
QUADRATURE = np.array([1.0, 5.0, 5.0, 1.0]) / 6.0


def lane_tiles(channels, width):
    return [(at, min(at + width, channels)) for at in range(0, channels, width)]


def winds(pair, levels):
    along_x, along_y = pair[:, :levels], pair[:, levels:]
    return (
        jnp.concatenate([along_x, along_x], axis=1),
        jnp.concatenate([along_y, along_y], axis=1),
    )


def full_winds(pair, levels, channels):
    along_x, along_y = winds(pair, levels)
    count = -(-channels // (2 * levels))
    return (
        jnp.concatenate([along_x] * count, axis=1)[:, :channels],
        jnp.concatenate([along_y] * count, axis=1)[:, :channels],
    )


def dx_rows(rows):
    out = []
    for i in range(NODES):
        total = None
        for j in range(NODES):
            if DERIV[i][j] != 0.0 and not (i == j and abs(DERIV[i][j]) < 1e-6):
                term = DERIV[i][j] * rows[j]
                total = term if total is None else total + term
        out.append(total)
    return out


def sublane_coefficients(rows, width):
    position = lax.broadcasted_iota(jnp.int32, (rows, width), 0) & 3
    table = []
    for shift in range(-3, 4):
        value = jnp.zeros((rows, width), jnp.float32)
        for at in range(NODES):
            if 0 <= at + shift < NODES:
                value = jnp.where(position == at, DERIV[at][at + shift], value)
        table.append(value)
    return table


def dsub(field, table):
    width = field.shape[1]
    blocks = []
    for at in range(0, field.shape[0], 8):
        part = field[at : at + 8]
        total = None
        for index, shift in enumerate(range(-3, 4)):
            moved = part if shift == 0 else pltpu.roll(part, (-shift) % 8, 0)
            term = table[index][:, :width] * moved
            total = term if total is None else total + term
        blocks.append(total)
    return blocks[0] if len(blocks) == 1 else jnp.concatenate(blocks, axis=0)


def sub_average(field):
    rows = field.shape[0]
    position = lax.broadcasted_iota(jnp.int32, field.shape, 0)
    phase = position & 3
    upper = (phase == 3) & (position < rows - 1)
    lower = (phase == 0) & (position > 0)
    ahead = pltpu.roll(field, rows - 1, 0)
    behind = pltpu.roll(field, 1, 0)
    partner = jnp.where(upper, ahead, jnp.where(lower, behind, field))
    return 0.5 * (field + partner)


def average_rows(ref, size_x, size_y):
    for at in range(NODES - 1, size_x - 1, NODES):
        low, high = pl.ds(at * size_y, size_y), pl.ds((at + 1) * size_y, size_y)
        mean = 0.5 * (ref[low, :] + ref[high, :])
        ref[low, :] = mean
        ref[high, :] = mean


def edge_rows(rows, first, last):
    position = lax.broadcasted_iota(jnp.int32, rows.shape, 0)
    count = rows.shape[0]
    return rows + jnp.where(
        position == 0, first, jnp.where(position == count - 1, last, 0.0)
    )


def local_update(base_ref, field_ref, mixed_ref, wind_ref, out_ref, size_x, size_y, levels, average):
    channels = field_ref.shape[1]
    table = sublane_coefficients(8, 2 * levels)
    for element in range(size_x // NODES):
        rows = [pl.ds((NODES * element + i) * size_y, size_y) for i in range(NODES)]
        wind = [winds(wind_ref[row, :], levels) for row in rows]
        for begin, end in lane_tiles(channels, 2 * levels):
            width = end - begin
            values = [field_ref[row, begin:end] for row in rows]
            slopes = dx_rows(values)
            for i in range(NODES):
                along_x, along_y = wind[i][0][:, :width], wind[i][1][:, :width]
                result = (
                    base_ref[rows[i], begin:end]
                    + mixed_ref[rows[i], begin:end]
                    - (along_x * slopes[i] + along_y * dsub(values[i], table))
                )
                out_ref[rows[i], begin:end] = sub_average(result) if average else result


def to_bf16(value):
    return value.astype(jnp.bfloat16)


def mix_all(field, mix):
    return jnp.dot(to_bf16(field), mix, preferred_element_type=jnp.float32)


def begin_kernel(size_x, size_y, levels, state, wind, mix, partial, to_left, to_right, mixed):
    channels = state.shape[1]
    mixed[...] = mix_all(state[...], mix[...])
    local_update(state, state, mixed, wind, partial, size_x, size_y, levels, True)
    average_rows(partial, size_x, size_y)
    for out, column, near, row in ((to_left, 0, 0, 0), (to_right, size_y - 1, size_y - NODES, 3)):
        slope = None
        for j in range(NODES):
            value = column_of(partial, near + j, size_x, size_y)
            term = DERIV[row][j] * value
            slope = term if slope is None else slope + term
        out[:, 0:channels] = column_of(partial, column, size_x, size_y)
        out[:, channels : 2 * channels] = slope
        out[:, 2 * channels : 3 * channels] = column_of(state, column, size_x, size_y)
        out[:, 3 * channels : 3 * channels + 2 * levels] = column_of(
            wind, column, size_x, size_y
        )


def column_of(ref, y, size_x, size_y):
    return jnp.concatenate(
        [ref[x * size_y + y : x * size_y + y + 1, :] for x in range(size_x)], axis=0
    )


def column_parts(message, channels, levels):
    return (
        message[:, 0:channels],
        message[:, channels : 2 * channels],
        message[:, 2 * channels : 3 * channels],
        message[:, 3 * channels : 3 * channels + 2 * levels],
    )


def turn_kernel(
    size_x, size_y, levels, partial, state, wind, from_left, from_right, to_up, to_down, field, line
):
    channels = state.shape[1]
    left_value, left_slope, left_state, left_wind = column_parts(from_left, channels, levels)
    right_value, right_slope, right_state, right_wind = column_parts(from_right, channels, levels)
    first_column = column_of(partial, 0, size_x, size_y)
    last_column = column_of(partial, size_y - 1, size_x, size_y)
    left_change = 0.5 * (left_value - first_column)
    right_change = 0.5 * (right_value - last_column)
    left_slope = left_slope - LAST * left_change
    right_slope = right_slope - FIRST * right_change
    for x in range(size_x):
        row = pl.ds(x * size_y, size_y)
        field[row, :] = edge_rows(
            partial[row, :], left_change[x : x + 1], right_change[x : x + 1]
        )
    span = 2 * channels + 2 * levels
    pieces = span // (2 * levels)
    for out, x, near, kind in ((to_up, 0, 0, 0), (to_down, size_x - 1, size_x - NODES, 3)):
        row = pl.ds(x * size_y, size_y)
        slope = None
        for j in range(NODES):
            term = DERIV[kind][j] * field[pl.ds((near + j) * size_y, size_y), :]
            slope = term if slope is None else slope + term
        along_x, _ = full_winds(wind[row, :], levels, channels)
        out[:, 0:channels] = field[row, :]
        out[:, channels : 2 * channels] = state[row, :] - along_x * slope
        out[:, 2 * channels : span] = wind[row, :]
        corners = (
            (left_slope, left_state, left_wind, slope[0:1]),
            (right_slope, right_state, right_wind, slope[size_y - 1 : size_y]),
        )
        for side, (side_slope, side_state, side_wind, corner_slope) in enumerate(corners):
            pair = side_wind[x : x + 1]
            corner_x, _ = full_winds(pair, levels, channels)
            line[side : side + 1, 0:channels] = side_slope[x : x + 1]
            line[side : side + 1, channels : 2 * channels] = (
                side_state[x : x + 1] - corner_x * corner_slope
            )
            line[side : side + 1, 2 * channels : span] = pair
            for piece in range(pieces):
                at = side * pieces + piece
                out[at : at + 1, span : span + 2 * levels] = line[
                    side : side + 1, piece * 2 * levels : (piece + 1) * 2 * levels
                ]
        used = 2 * pieces
        if used < size_y:
            out[used:size_y, span : span + 2 * levels] = jnp.zeros(
                (size_y - used, 2 * levels), jnp.float32
            )


def cloud_run(states, forcing, mix, tendency, columns, group):
    slots = forcing.shape[0]
    means = {}
    totals = {}
    for step in range(SUB):
        for begin in range(0, slots, group):
            span = pl.ds(begin * columns, group * columns)
            mixed = mix_all(states[span, :], mix[...])
            for slot in range(begin, begin + group):
                rows = pl.ds(slot * columns, columns)
                value = states[rows, :]
                push = forcing[slot : slot + 1, :]
                if step == 0:
                    mean = jnp.mean(value, axis=0, keepdims=True)
                else:
                    mean = means[slot]
                near = slice((slot - begin) * columns, (slot - begin + 1) * columns)
                spread = pltpu.roll(value, 1, 0) + pltpu.roll(value, columns - 1, 0) - 2.0 * value
                value = value + CRM_STEP * (
                    jnp.tanh(mixed[near]) + DIFFUSION * spread + (push - mean)
                )
                states[rows, :] = value
                mean = jnp.mean(value, axis=0, keepdims=True)
                means[slot] = mean
                totals[slot] = mean - push if step == 0 else totals[slot] + (mean - push)
    if tendency is not None:
        for slot in range(slots):
            tendency[slot : slot + 1, :] = totals[slot] / SUB


def home_kernel(
    size_x, size_y, levels, columns, groups, *refs
):
    (
        rank, field, state, wind, mix, cloud_mix, from_left, from_right, from_up, from_down,
        gather, spread, occupied, own_clouds,
    ) = refs[:14]
    clouds = refs[14 : 14 + groups - 1]
    out, to_left, to_right = refs[14 + groups - 1 : 17 + groups - 1]
    sends = refs[17 + groups - 1]
    mixed, work, total, reduced, forcing, tendency, cloud = refs[18 + groups - 1 :]
    channels = state.shape[1]
    slots = gather.shape[0]
    capacity = slots // groups
    span = 2 * channels + 2 * levels
    pieces = span // (2 * levels)
    last_row = pl.ds((size_x - 1) * size_y, size_y)
    first_row = pl.ds(0, size_y)
    cloud[pl.ds(0, capacity * columns), :] = (
        own_clouds[pl.ds(rank[0] * capacity * columns, capacity * columns), :].astype(jnp.float32)
    )
    for k in range(1, groups):
        cloud[pl.ds(k * capacity * columns, capacity * columns), :] = clouds[k - 1][...]
    up_change = 0.5 * (from_up[:, 0:channels] - field[first_row, :])
    down_change = 0.5 * (from_down[:, 0:channels] - field[last_row, :])
    work[...] = field[...]
    work[first_row, :] = field[first_row, :] + up_change
    work[last_row, :] = field[last_row, :] + down_change
    mixed[...] = mix_all(work[...], mix[...])
    local_update(state, work, mixed, wind, total, size_x, size_y, levels, True)
    table = sublane_coefficients(8, channels)
    corner = {}
    for name, message in (("up", from_up), ("down", from_down)):
        for side in range(2):
            line = jnp.concatenate(
                [
                    message[side * pieces + p : side * pieces + p + 1, span : span + 2 * levels]
                    for p in range(pieces)
                ],
                axis=1,
            )
            corner[name, side] = (
                line[:, 0:channels],
                line[:, channels : 2 * channels],
                line[:, 2 * channels : span],
            )
    side_slopes = []
    for side, (message, y, factor) in enumerate(
        ((from_left, 0, LAST), (from_right, size_y - 1, FIRST))
    ):
        value, slope, side_state, side_wind = column_parts(message, channels, levels)
        column = column_of(work, y, size_x, size_y)
        slope = slope - factor * (value - column_of(field, y, size_x, size_y))
        slope = edge_rows(
            slope,
            0.5 * (corner["up", side][0] - slope[0:1]),
            0.5 * (corner["down", side][0] - slope[size_x - 1 : size_x]),
        )
        side_slopes.append(slope)
        along_x, along_y = full_winds(side_wind, levels, channels)
        beyond = (
            side_state
            + column_of(mixed, y, size_x, size_y)
            - (along_x * dsub(column, table) + along_y * slope)
        )
        for x in range(size_x):
            at = slice(x * size_y + y, x * size_y + y + 1)
            total[at, :] = 0.5 * (total[at, :] + beyond[x : x + 1])
    for name, message, row, change, factor, x in (
        ("up", from_up, first_row, up_change, LAST, 0),
        ("down", from_down, last_row, down_change, FIRST, size_x - 1),
    ):
        along_x, along_y = full_winds(message[:, 2 * channels : span], levels, channels)
        slope_y = dsub(work[row, :], table)
        beyond = (
            message[:, channels : 2 * channels]
            + mixed[row, :]
            + factor * along_x * change
            - along_y * slope_y
        )
        beyond = sub_average(beyond)
        ends = []
        for side, y in ((0, 0), (1, size_y - 1)):
            _, part, pair = corner[name, side]
            corner_x, corner_y = full_winds(pair, levels, channels)
            value = (
                part
                + mixed[pl.ds(x * size_y + y, 1), :]
                + factor * corner_x * change[y : y + 1]
                - corner_y * side_slopes[side][x : x + 1]
            )
            ends.append(0.5 * (value - beyond[y : y + 1]))
        beyond = edge_rows(beyond, ends[0], ends[1])
        total[row, :] = 0.5 * (total[row, :] + beyond)
    average_rows(total, size_x, size_y)
    for element in range(size_x // NODES):
        value = None
        for i in range(NODES):
            term = float(QUADRATURE[i]) * total[pl.ds((NODES * element + i) * size_y, size_y), :]
            value = term if value is None else value + term
        reduced[pl.ds(element * size_y, size_y), :] = value
    forcing[...] = jnp.dot(
        gather[...], reduced[...], precision=HIGHEST, preferred_element_type=jnp.float32
    )
    mixed[...] = mix_all(total[...], mix[...])
    local_update(total, total, mixed, wind, work, size_x, size_y, levels, False)
    cloud_run(cloud, forcing, cloud_mix, tendency, columns, capacity if slots % 4 else 4)
    tend = tendency[...]
    change = COUPLING * (tend + mix_all(tend, mix[...]))
    reduced[...] = jnp.dot(
        spread[...], change, precision=HIGHEST, preferred_element_type=jnp.float32
    )
    for x in range(size_x):
        row = pl.ds(x * size_y, size_y)
        element = pl.ds((x // NODES) * size_y, size_y)
        out[row, :] = sub_average(work[row, :] + reduced[element, :])
    average_rows(out, size_x, size_y)
    for ref, y, block in ((to_left, 0, 1), (to_right, size_y - 1, groups - 1)):
        ref[0:size_x, 0:channels] = column_of(out, y, size_x, size_y)
        rows = pl.ds(block * capacity, capacity)
        ref[size_x : size_x + capacity, 0:channels] = forcing[rows, :]
        ref[size_x : size_x + capacity, channels : channels + 1] = occupied[rows, :]
    sends[:, 0:channels] = forcing[...]
    sends[:, channels : channels + 1] = occupied[...]


def last_turn_kernel(size_x, size_y, partial, from_left, from_right, to_up, to_down, field):
    channels = partial.shape[1]
    left = 0.5 * (
        from_left[0:size_x, 0:channels] - column_of(partial, 0, size_x, size_y)
    )
    right = 0.5 * (
        from_right[0:size_x, 0:channels] - column_of(partial, size_y - 1, size_x, size_y)
    )
    for x in range(size_x):
        row = pl.ds(x * size_y, size_y)
        field[row, :] = edge_rows(partial[row, :], left[x : x + 1], right[x : x + 1])
    to_up[...] = field[pl.ds(0, size_y), :]
    to_down[...] = field[pl.ds((size_x - 1) * size_y, size_y), :]


def finish_kernel(field, from_up, from_down, out):
    other = jnp.where(pl.program_id(0) == 0, from_up[...], from_down[...])
    out[...] = 0.5 * (field[...] + other)


def owner_kernel(columns, groups, *refs):
    rank, states, mix = refs[:3]
    forcings = refs[3 : 3 + groups]
    out, cloud, forcing = refs[3 + groups :]
    channels = states.shape[1]
    slots = forcing.shape[0]
    capacity = slots // groups
    block = capacity * columns
    for k in range(groups):
        place = lax.rem(rank[0] + k, groups)
        start = pl.multiple_of(place * block, block)
        cloud[pl.ds(k * block, block), :] = states[pl.ds(start, block), :].astype(jnp.float32)
        forcing[pl.ds(k * capacity, capacity), :] = forcings[k][:, 0:channels]
    cloud_run(cloud, forcing, mix, None, columns, capacity if slots % 4 else 4)
    for k in range(groups):
        place = lax.rem(rank[0] + k, groups)
        for slot in range(capacity):
            start = pl.multiple_of(place * block + slot * columns, columns)
            used = forcings[k][slot : slot + 1, channels : channels + 1] > 0.5
            rows = pl.ds((k * capacity + slot) * columns, columns)
            old = states[pl.ds(start, columns), :].astype(jnp.float32)
            out[pl.ds(start, columns), :] = to_bf16(jnp.where(used, cloud[rows, :], old))


def widen_kernel(groups, rank, states, *outs):
    block = outs[0].shape[0]
    for k in range(1, groups):
        place = lax.rem(rank[0] + k, groups)
        start = pl.multiple_of(place * block, block)
        outs[k - 1][...] = states[pl.ds(start, block), :].astype(jnp.float32)


VMEM_GRANT = 12 * 2**20
VMEM = pltpu.MemorySpace.VMEM
SMEM = pltpu.MemorySpace.SMEM


def call(kernel, outs, scratch, *args, smem=()):
    specs = [
        pl.BlockSpec(memory_space=SMEM if index in smem else VMEM) for index in range(len(args))
    ]
    shapes = [jax.ShapeDtypeStruct(shape, dtype) for shape, dtype in outs]
    return pl.pallas_call(
        kernel,
        out_shape=shapes,
        in_specs=specs,
        out_specs=[pl.BlockSpec(memory_space=VMEM)] * len(shapes),
        scratch_shapes=[pltpu.VMEM(shape, dtype) for shape, dtype in scratch],
        compiler_params=pltpu.CompilerParams(vmem_limit_bytes=VMEM_GRANT),
    )(*args)


def shift(value, axis, offset):
    count = lax.axis_size(axis)
    return lax.ppermute(value, axis, [(i, (i + offset) % count) for i in range(count)])


def on_device(state, wind, dyn_mix, owner, crm_state, crm_mix):
    f32 = jnp.float32
    size_x, size_y, channels = state.shape
    levels = wind.shape[2] // 2
    nodes = size_x * size_y
    groups = lax.axis_size("crm")
    slots, columns = crm_state.shape[:2]
    capacity = slots // groups
    elements_x, elements_y = size_x // NODES, size_y // NODES
    rank = lax.axis_index("crm").astype(jnp.int32).reshape(1)
    state = state.reshape(nodes, channels)
    wind = wind.reshape(nodes, 2 * levels)
    clouds = crm_state.reshape(slots * columns, channels)

    owners = owner[:, 0]
    onehot = (owners[:, None] == jnp.arange(groups, dtype=jnp.int32)[None, :]).astype(jnp.int32)
    earlier = jnp.cumsum(onehot, axis=0) - onehot
    position_rank = jnp.sum(earlier * onehot, axis=1)
    slot_index = ((rank[0] - owners) % groups) * capacity + position_rank
    selector = (slot_index[None, :] == jnp.arange(slots, dtype=jnp.int32)[:, None]).astype(f32)
    occupied = jnp.sum(selector, axis=1, keepdims=True)
    spread = jnp.repeat(selector, NODES, axis=1)
    weights = jnp.asarray(np.tile(QUADRATURE / 4.0, elements_x * elements_y), f32)
    gather = spread * weights[None, :]
    spread = spread.T

    column_message = ((size_x, 3 * channels + 2 * levels), f32)
    grid = ((nodes, channels), f32)
    partial, to_left, to_right = call(
        functools.partial(begin_kernel, size_x, size_y, levels),
        [grid, column_message, column_message],
        [grid],
        state, wind, dyn_mix,
    )
    from_right = shift(to_left, "crm", -1)
    from_left = shift(to_right, "crm", 1)
    block = ((capacity * columns, channels), f32)
    wide = call(
        functools.partial(widen_kernel, groups),
        [block] * (groups - 1), [], rank, clouds, smem=(0,),
    )
    arrived = [shift(wide[k - 1], "crm", k) for k in range(1, groups)]
    span = 2 * channels + 2 * levels
    row_message = ((size_y, span + 2 * levels), f32)
    to_up, to_down, field = call(
        functools.partial(turn_kernel, size_x, size_y, levels),
        [row_message, row_message, grid],
        [((8, span), f32)],
        partial, state, wind, from_left, from_right,
    )
    from_down = shift(to_up, "elem", -1)
    from_up = shift(to_down, "elem", 1)
    edge = ((size_x + capacity, channels + 1), f32)
    partial, to_left, to_right, sends = call(
        functools.partial(home_kernel, size_x, size_y, levels, columns, groups),
        [grid, edge, edge, ((slots, channels + 1), f32)],
        [
            grid, grid, grid,
            ((elements_x * size_y, channels), f32),
            ((slots, channels), f32),
            ((slots, channels), f32),
            ((slots * columns, channels), f32),
        ],
        rank, field, state, wind, dyn_mix, crm_mix, from_left, from_right, from_up, from_down,
        gather, spread, occupied, clouds, *arrived,
        smem=(0,),
    )
    from_right = shift(to_left, "crm", -1)
    from_left = shift(to_right, "crm", 1)
    blocks = [sends[k * capacity : (k + 1) * capacity] for k in range(groups)]
    forcings = [blocks[0], from_right[size_x:]]
    forcings += [shift(blocks[k], "crm", -k) for k in range(2, groups - 1)]
    forcings += [from_left[size_x:]]
    to_up, to_down, field = call(
        functools.partial(last_turn_kernel, size_x, size_y),
        [((size_y, channels), f32), ((size_y, channels), f32), grid],
        [],
        partial, from_left, from_right,
    )
    from_down = shift(to_up, "elem", -1)
    from_up = shift(to_down, "elem", 1)
    (crm_next,) = call(
        functools.partial(owner_kernel, columns, groups),
        [((slots * columns, channels), crm_state.dtype)],
        [((slots * columns, channels), f32), ((slots, channels), f32)],
        rank, clouds, crm_mix, *forcings,
        smem=(0,),
    )
    row = pl.BlockSpec((size_y, channels), lambda i: (i * (size_x - 1), 0))
    whole = pl.BlockSpec((size_y, channels), lambda i: (0, 0))
    third = pl.pallas_call(
        finish_kernel,
        grid=(2,),
        out_shape=jax.ShapeDtypeStruct((nodes, channels), f32),
        in_specs=[row, whole, whole],
        out_specs=row,
        input_output_aliases={0: 0},
        compiler_params=pltpu.CompilerParams(vmem_limit_bytes=VMEM_GRANT),
    )(field, from_up, from_down)
    return (
        third.reshape(size_x, size_y, channels),
        crm_next.reshape(slots, columns, channels),
    )


def solution(mesh):
    return jax.shard_map(
        on_device,
        mesh=mesh,
        in_specs=(
            P("elem", "crm", None),
            P("elem", "crm", None),
            P(),
            P(("elem", "crm"), None),
            P(("elem", "crm"), None, None),
            P(),
        ),
        out_specs=(P("elem", "crm", None), P(("elem", "crm"), None, None)),
        check_vma=False,
    )
```

```python
import functools

import jax
import jax.numpy as jnp
import numpy as np
from jax import lax
from jax.experimental import pallas as pl
from jax.experimental.pallas import tpu as pltpu
from jax.sharding import PartitionSpec as P


SUB = 4
HIGHEST = lax.Precision.HIGHEST
CRM_STEP = 0.5
DIFFUSION = 0.2
COUPLING = 0.5
NODES = 4


def gll_derivative():
    points = np.array([-1.0, -1.0 / np.sqrt(5.0), 1.0 / np.sqrt(5.0), 1.0])
    barycentric = np.array(
        [
            1.0 / np.prod([points[i] - points[j] for j in range(NODES) if j != i])
            for i in range(NODES)
        ]
    )
    derivative = np.zeros((NODES, NODES))
    for i in range(NODES):
        for j in range(NODES):
            if j != i:
                derivative[i, j] = barycentric[j] / barycentric[i] / (points[i] - points[j])
        derivative[i, i] = -np.sum(derivative[i])
    return derivative


DERIV = [[float(value) for value in row] for row in gll_derivative().astype(np.float32)]
FIRST, LAST = DERIV[0][0], DERIV[3][3]
QUADRATURE = np.array([1.0, 5.0, 5.0, 1.0]) / 6.0


def lane_tiles(channels, width):
    return [(at, min(at + width, channels)) for at in range(0, channels, width)]


def winds(pair, levels):
    along_x, along_y = pair[:, :levels], pair[:, levels:]
    return (
        jnp.concatenate([along_x, along_x], axis=1),
        jnp.concatenate([along_y, along_y], axis=1),
    )


def full_winds(pair, levels, channels):
    along_x, along_y = winds(pair, levels)
    count = -(-channels // (2 * levels))
    return (
        jnp.concatenate([along_x] * count, axis=1)[:, :channels],
        jnp.concatenate([along_y] * count, axis=1)[:, :channels],
    )


def dx_rows(rows):
    out = []
    for i in range(NODES):
        total = None
        for j in range(NODES):
            if DERIV[i][j] != 0.0 and not (i == j and abs(DERIV[i][j]) < 1e-6):
                term = DERIV[i][j] * rows[j]
                total = term if total is None else total + term
        out.append(total)
    return out


def sublane_coefficients(rows, width):
    position = lax.broadcasted_iota(jnp.int32, (rows, width), 0) & 3
    table = []
    for shift in range(-3, 4):
        value = jnp.zeros((rows, width), jnp.float32)
        for at in range(NODES):
            if 0 <= at + shift < NODES:
                value = jnp.where(position == at, DERIV[at][at + shift], value)
        table.append(value)
    return table


def dsub(field, table):
    width = field.shape[1]
    blocks = []
    for at in range(0, field.shape[0], 8):
        part = field[at : at + 8]
        total = None
        for index, shift in enumerate(range(-3, 4)):
            moved = part if shift == 0 else pltpu.roll(part, (-shift) % 8, 0)
            term = table[index][:, :width] * moved
            total = term if total is None else total + term
        blocks.append(total)
    return blocks[0] if len(blocks) == 1 else jnp.concatenate(blocks, axis=0)


def sub_average(field):
    rows = field.shape[0]
    position = lax.broadcasted_iota(jnp.int32, field.shape, 0)
    phase = position & 3
    upper = (phase == 3) & (position < rows - 1)
    lower = (phase == 0) & (position > 0)
    ahead = pltpu.roll(field, rows - 1, 0)
    behind = pltpu.roll(field, 1, 0)
    partner = jnp.where(upper, ahead, jnp.where(lower, behind, field))
    return 0.5 * (field + partner)


def average_rows(ref, size_x, size_y):
    for at in range(NODES - 1, size_x - 1, NODES):
        low, high = pl.ds(at * size_y, size_y), pl.ds((at + 1) * size_y, size_y)
        mean = 0.5 * (ref[low, :] + ref[high, :])
        ref[low, :] = mean
        ref[high, :] = mean


def end_rows(rows, first, last):
    shape = (rows, first.shape[1])
    position = lax.broadcasted_iota(jnp.int32, shape, 0)
    return jnp.where(position == 0, first, jnp.where(position == rows - 1, last, 0.0))


def edge_rows(rows, first, last):
    position = lax.broadcasted_iota(jnp.int32, rows.shape, 0)
    count = rows.shape[0]
    return rows + jnp.where(
        position == 0, first, jnp.where(position == count - 1, last, 0.0)
    )


def local_update(base_ref, field_ref, mixed_ref, wind_ref, out_ref, size_x, size_y, levels, average):
    channels = field_ref.shape[1]
    table = sublane_coefficients(8, 2 * levels)
    for element in range(size_x // NODES):
        rows = [pl.ds((NODES * element + i) * size_y, size_y) for i in range(NODES)]
        wind = [winds(wind_ref[row, :], levels) for row in rows]
        for begin, end in lane_tiles(channels, 2 * levels):
            width = end - begin
            values = [field_ref[row, begin:end] for row in rows]
            slopes = dx_rows(values)
            for i in range(NODES):
                along_x, along_y = wind[i][0][:, :width], wind[i][1][:, :width]
                result = (
                    base_ref[rows[i], begin:end]
                    + mixed_ref[rows[i], begin:end]
                    - (along_x * slopes[i] + along_y * dsub(values[i], table))
                )
                out_ref[rows[i], begin:end] = sub_average(result) if average else result


def to_bf16(value):
    return value.astype(jnp.bfloat16)


def mix_all(field, mix):
    return jnp.dot(to_bf16(field), mix, preferred_element_type=jnp.float32)


def column_of(ref, y, size_x, size_y):
    return jnp.concatenate(
        [ref[x * size_y + y : x * size_y + y + 1, :] for x in range(size_x)], axis=0
    )


def column_parts(message, channels, levels):
    return (
        message[:, 0:channels],
        message[:, channels : 2 * channels],
        message[:, 2 * channels : 3 * channels],
        message[:, 3 * channels : 3 * channels + 2 * levels],
    )


def is_even(rank):
    return (rank[0] & 1) == 0


def begin_kernel(size_x, size_y, levels, rank, state_in, wind_in, mix_in, partial, to_a, to_b,
                 state, wind, mix, mixed, message, arrivals):
    channels = state.shape[1]
    copies = [
        pltpu.make_async_copy(source, target, arrivals.at[index])
        for index, (source, target) in enumerate(
            ((state_in, state), (mix_in, mix), (wind_in, wind))
        )
    ]
    for copy in copies:
        copy.start()
    copies[0].wait()
    copies[1].wait()
    mixed[...] = mix_all(state[...], mix[...])
    copies[2].wait()
    local_update(state, state, mixed, wind, partial, size_x, size_y, levels, True)
    average_rows(partial, size_x, size_y)
    to_left, to_right = message.at[0], message.at[1]
    for out, column, near, row in ((to_left, 0, 0, 0), (to_right, size_y - 1, size_y - NODES, 3)):
        values = [column_of(partial, near + j, size_x, size_y) for j in range(NODES)]
        slope = None
        for j in range(NODES):
            term = DERIV[row][j] * values[j]
            slope = term if slope is None else slope + term
        out[:, 0:channels] = values[row]
        out[:, channels : 2 * channels] = slope
        out[:, 2 * channels : 3 * channels] = column_of(state, column, size_x, size_y)
        out[:, 3 * channels : 3 * channels + 2 * levels] = column_of(wind, column, size_x, size_y)
    even = is_even(rank)
    to_a[...] = jnp.where(even, message[1], message[0])
    to_b[...] = jnp.where(even, message[0], message[1])


def in_order(rank, from_a, from_b):
    even = is_even(rank)
    first, second = from_a[...], from_b[...]
    return jnp.where(even, second, first), jnp.where(even, first, second)


def side_changes(size_x, size_y, partial, from_left, from_right):
    channels = partial.shape[1]
    return (
        0.5 * (from_left[0:size_x, 0:channels] - column_of(partial, 0, size_x, size_y)),
        0.5 * (from_right[0:size_x, 0:channels] - column_of(partial, size_y - 1, size_x, size_y)),
    )


def turn_kernel(size_x, size_y, levels, rank, place, partial, state, wind, from_a, from_b,
                to_a, to_b, line, message):
    channels = state.shape[1]
    from_left, from_right = in_order(rank, from_a, from_b)
    to_up, to_down = message.at[0], message.at[1]
    left_value, left_slope, left_state, left_wind = column_parts(from_left, channels, levels)
    right_value, right_slope, right_state, right_wind = column_parts(from_right, channels, levels)
    span = 2 * channels + 2 * levels
    pieces = span // (2 * levels)
    for out, x, near, kind in ((to_up, 0, 0, 0), (to_down, size_x - 1, size_x - NODES, 3)):
        slope = None
        for j in range(NODES):
            value = partial[pl.ds((near + j) * size_y, size_y), :]
            at = near + j
            left = 0.5 * (left_value[at : at + 1] - value[0:1])
            right = 0.5 * (right_value[at : at + 1] - value[size_y - 1 : size_y])
            value = edge_rows(value, left, right)
            if at == x:
                out[:, 0:channels] = value
                changes = (left, right)
            term = DERIV[kind][j] * value
            slope = term if slope is None else slope + term
        row = pl.ds(x * size_y, size_y)
        along_x, _ = full_winds(wind[row, :], levels, channels)
        out[:, channels : 2 * channels] = state[row, :] - along_x * slope
        out[:, 2 * channels : span] = wind[row, :]
        corners = (
            (left_slope[x : x + 1] - LAST * changes[0], left_state, left_wind, slope[0:1]),
            (
                right_slope[x : x + 1] - FIRST * changes[1],
                right_state,
                right_wind,
                slope[size_y - 1 : size_y],
            ),
        )
        for side, (side_slope, side_state, side_wind, corner_slope) in enumerate(corners):
            pair = side_wind[x : x + 1]
            corner_x, _ = full_winds(pair, levels, channels)
            line[side : side + 1, 0:channels] = side_slope
            line[side : side + 1, channels : 2 * channels] = (
                side_state[x : x + 1] - corner_x * corner_slope
            )
            line[side : side + 1, 2 * channels : span] = pair
            for piece in range(pieces):
                at = side * pieces + piece
                out[at : at + 1, span : span + 2 * levels] = line[
                    side : side + 1, piece * 2 * levels : (piece + 1) * 2 * levels
                ]
        used = 2 * pieces
        if used < size_y:
            out[used:size_y, span : span + 2 * levels] = jnp.zeros(
                (size_y - used, 2 * levels), jnp.float32
            )
    even = is_even(place)
    to_a[...] = jnp.where(even, message[1], message[0])
    to_b[...] = jnp.where(even, message[0], message[1])


def ready_kernel(size_x, size_y, levels, capacity, rank, owner, partial, state, wind, mix,
                 from_a, from_b, field, mixed, total, sides, onehot):
    channels = state.shape[1]
    from_left, from_right = in_order(rank, from_a, from_b)
    shape = onehot.shape
    parts = 8 // capacity
    lanes = lax.broadcasted_iota(jnp.int32, shape, 1) >> 2
    named = jnp.zeros(shape, jnp.int32)
    for c in range(owner.shape[0]):
        named = jnp.where(lanes == c, owner[c], named)
    position = jnp.zeros(shape, jnp.int32)
    for c in range(owner.shape[0]):
        position = position + jnp.where((lanes > c) & (named == owner[c]), 1, 0)
    offset = rank[0] ^ named
    slot = (offset * capacity + position) * parts
    rows = lax.broadcasted_iota(jnp.int32, shape, 0)
    onehot[...] = jnp.where((rows >= slot) & (rows < slot + parts), 1.0, 0.0)
    left, right = side_changes(size_x, size_y, partial, from_left, from_right)
    for x in range(size_x):
        row = pl.ds(x * size_y, size_y)
        field[row, :] = edge_rows(partial[row, :], left[x : x + 1], right[x : x + 1])
    mixed[...] = mix_all(field[...], mix[...])
    local_update(state, field, mixed, wind, total, size_x, size_y, levels, True)
    table = sublane_coefficients(8, channels)
    for side, (message, y, change, factor) in enumerate(
        ((from_left, 0, left, LAST), (from_right, size_y - 1, right, FIRST))
    ):
        _, slope, side_state, side_wind = column_parts(message, channels, levels)
        slope = slope - factor * change
        along_x, along_y = full_winds(side_wind, levels, channels)
        beyond = (
            side_state
            + column_of(mixed, y, size_x, size_y)
            - (
                along_x * dsub(column_of(field, y, size_x, size_y), table)
                + along_y * slope
            )
        )
        sides[side, 0] = beyond
        sides[side, 1] = slope
        sides[side, 2] = along_x
        sides[side, 3] = along_y


def part_roll(value, parts, by):
    by = by % parts
    if by == 0:
        return value
    part = lax.broadcasted_iota(jnp.int32, value.shape, 0) & (parts - 1)
    return jnp.where(
        part < parts - by, pltpu.roll(value, 8 - by, 0), pltpu.roll(value, parts - by, 0)
    )


def part_sum(value, parts):
    total = value
    for by in range(1, parts):
        total = total + part_roll(value, parts, by)
    return total


def packing(rows, channels):
    full, rest = channels // 128, channels % 128
    assert rest in (0, 64)
    return full, rest, full * rows + (rows // 2 if rest else 0)


def pack(tile, channels, out, rows):
    full, rest, _ = packing(rows, channels)
    count = rows // 8
    for t in range(count):
        for lane in range(full):
            out[lane * rows + 8 * t : lane * rows + 8 * t + 8, :] = tile(t, lane)
    if rest:
        for t in range(count // 2):
            out[full * rows + 8 * t : full * rows + 8 * t + 8, :] = jnp.concatenate(
                [tile(t, full)[:, :rest], tile(t + count // 2, full)[:, :rest]], axis=1
            )


def unpack(message, channels, out, start, rows):
    full, rest, _ = packing(rows, channels)
    for lane in range(full):
        out[start : start + rows, lane * 128 : lane * 128 + 128] = message[
            lane * rows : (lane + 1) * rows, :
        ]
    if rest:
        half = rows // 2
        tail = message[full * rows : full * rows + half, :]
        out[start : start + half, full * 128 : channels] = tail[:, :rest]
        out[start + half : start + rows, full * 128 : channels] = tail[:, rest:]


def interleave(states, start, channels, turned, rows):
    for lane, (begin, end) in enumerate(lane_tiles(channels, 128)):
        turned[lane, 0:rows, 0 : end - begin] = states[pl.ds(start, rows), begin:end].astype(
            jnp.float32
        )

    def tile(t, lane):
        return turned[lane, pl.ds(t, 8, stride=rows // 8), :]

    return tile


def widen_kernel(groups, rank, states, *refs):
    own, near = refs[:2]
    pairs = refs[2 : 1 + groups // 2]
    turned = refs[-1]
    rows, channels = own.shape
    length = near.shape[0]
    for k in range(groups):
        start = pl.multiple_of((rank[0] ^ k) * rows, rows)
        tile = interleave(states, start, channels, turned.at[k], rows)
        if k == 0:
            for t in range(rows // 8):
                for lane, (begin, end) in enumerate(lane_tiles(channels, 128)):
                    own[8 * t : 8 * t + 8, begin:end] = tile(t, lane)[:, : end - begin]
        elif k == 1:
            pack(tile, channels, near, rows)
        else:
            at = (k & 1) * length
            pack(tile, channels, pairs[k // 2 - 1].at[at : at + length], rows)


def cloud_run(states, forcing, mix, rows, parts, tendency, finals):
    blocks = states.shape[0] // rows
    count = rows // 8
    columns = count * parts
    means, totals = {}, {}
    for step in range(SUB):
        last = step == SUB - 1
        for begin in range(0, blocks, 2):
            group = range(begin, min(begin + 2, blocks))
            mixed = mix_all(states[begin * rows : (group[-1] + 1) * rows, :], mix[...])
            for block in group:
                push = forcing[8 * block : 8 * block + 8, :]

                def read(t):
                    at = block * rows + 8 * t
                    return states[at : at + 8, :]

                if step == 0:
                    total = read(0)
                    for t in range(1, count):
                        total = total + read(t)
                    means[block] = part_sum(total, parts) * (1.0 / columns)
                gain = CRM_STEP * (push - means[block])
                keep = not last or block in finals
                total = None
                if keep:
                    start = read(0)
                    behind, here = part_roll(read(count - 1), parts, -1), start
                for t in range(count):
                    at = (block - begin) * rows + 8 * t
                    turn = jnp.tanh(mixed[at : at + 8])
                    total = turn if total is None else total + turn
                    if keep:
                        ahead = read(t + 1) if t + 1 < count else part_roll(start, parts, 1)
                        states[block * rows + 8 * t : block * rows + 8 * t + 8, :] = (
                            (1.0 - 2.0 * CRM_STEP * DIFFUSION) * here
                            + CRM_STEP * DIFFUSION * (behind + ahead)
                            + CRM_STEP * turn
                            + gain
                        )
                        behind, here = here, ahead
                if tendency is not None:
                    mean = means[block] + part_sum(total, parts) * (CRM_STEP / columns) + gain
                    totals[block] = mean - push if step == 0 else totals[block] + (mean - push)
                    means[block] = mean
                elif not last:
                    means[block] = (
                        means[block] + part_sum(total, parts) * (CRM_STEP / columns) + gain
                    )
    if tendency is not None:
        for block in range(blocks):
            tendency[8 * block : 8 * block + 8, :] = totals[block] * (1.0 / SUB)


def settle(states, start, used, parts, turned, old, old_start, out, out_start, rows):
    channels = states.shape[1]
    count = rows // 8
    for lane, (begin, end) in enumerate(lane_tiles(channels, 128)):
        width = end - begin
        for t in range(count):
            value = states[start + 8 * t : start + 8 * t + 8, begin:end]
            if width < 128:
                value = jnp.concatenate([value, jnp.zeros((8, 128 - width), jnp.float32)], axis=1)
            turned[lane, pl.ds(t, 8, stride=count), :] = value
        for slot in range(8 // parts):
            at = slot * count * parts
            span = count * parts
            flag = used[slot * parts : slot * parts + 1, :] > 0.5
            before = old[pl.ds(old_start + at, span), begin:end].astype(jnp.float32)
            after = turned[lane, at : at + span, 0:width]
            out[pl.ds(out_start + at, span), begin:end] = jnp.where(flag, after, before).astype(
                jnp.bfloat16
            )


def second_kernel(size_x, size_y, levels, place, field, second, known, sides, onehot, wind, mix,
                  from_a, from_b, work, forcing, mixed, total, reduced):
    from_up, from_down = in_order(place, from_a, from_b)
    channels = field.shape[1]
    span = 2 * channels + 2 * levels
    pieces = span // (2 * levels)
    last_row = pl.ds((size_x - 1) * size_y, size_y)
    first_row = pl.ds(0, size_y)
    small = sublane_coefficients(8, channels)
    ups = 0.5 * (from_up[:, 0:channels] - field[first_row, :])
    downs = 0.5 * (from_down[:, 0:channels] - field[last_row, :])
    remixed = mix_all(
        jnp.concatenate([field[first_row, :] + ups, field[last_row, :] + downs], axis=0), mix[...]
    )
    new_mixed = (remixed[0:size_y], remixed[size_y : 2 * size_y])
    total[...] = second[...]
    edge_mixed = []
    for index, (x, near, end, change) in enumerate(
        ((0, 0, 0, ups), (size_x - 1, size_x - NODES, 3, downs))
    ):
        edge = pl.ds(x * size_y, size_y)
        edge_mixed.append(new_mixed[index] - known[edge, :])
        for i in range(NODES):
            row = pl.ds((near + i) * size_y, size_y)
            along_x, along_y = full_winds(wind[row, :], levels, channels)
            value = -DERIV[i][end] * (along_x * change)
            if near + i == x:
                value = value + edge_mixed[index] - along_y * dsub(change, small)
            total[row, :] = total[row, :] + sub_average(value)
    corner = {}
    for name, message in enumerate((from_up, from_down)):
        for side in range(2):
            line = jnp.concatenate(
                [
                    message[side * pieces + p : side * pieces + p + 1, span : span + 2 * levels]
                    for p in range(pieces)
                ],
                axis=1,
            )
            corner[name, side] = (
                line[:, 0:channels],
                line[:, channels : 2 * channels],
                line[:, 2 * channels : span],
            )
    edge_slopes = {}
    for side, y in ((0, 0), (1, size_y - 1)):
        slope = sides[side, 1]
        pick = slice(y, y + 1)
        new_first = 0.5 * (corner[0, side][0] + slope[0:1])
        new_last = 0.5 * (corner[1, side][0] + slope[size_x - 1 : size_x])
        edge_slopes[0, side], edge_slopes[1, side] = new_first, new_last
        slope_change = end_rows(
            size_x, new_first - slope[0:1], new_last - slope[size_x - 1 : size_x]
        )
        column_change = end_rows(size_x, ups[pick], downs[pick])
        mixed_change = end_rows(size_x, edge_mixed[0][pick], edge_mixed[1][pick])
        beyond = (
            sides[side, 0]
            + mixed_change
            - (sides[side, 2] * dsub(column_change, small) + sides[side, 3] * slope_change)
        )
        for x in range(size_x):
            at = slice(x * size_y + y, x * size_y + y + 1)
            total[at, :] = 0.5 * (total[at, :] + beyond[x : x + 1])
    for name, message, row, change, factor in (
        (0, from_up, first_row, ups, LAST),
        (1, from_down, last_row, downs, FIRST),
    ):
        along_x, along_y = full_winds(message[:, 2 * channels : span], levels, channels)
        beyond = (
            message[:, channels : 2 * channels]
            + new_mixed[name]
            + factor * along_x * change
            - along_y * dsub(field[row, :] + change, small)
        )
        beyond = sub_average(beyond)
        ends = []
        for side, y in ((0, 0), (1, size_y - 1)):
            _, part, pair = corner[name, side]
            corner_x, corner_y = full_winds(pair, levels, channels)
            value = (
                part
                + new_mixed[name][y : y + 1]
                + factor * corner_x * change[y : y + 1]
                - corner_y * edge_slopes[name, side]
            )
            ends.append(0.5 * (value - beyond[y : y + 1]))
        beyond = edge_rows(beyond, ends[0], ends[1])
        total[row, :] = 0.5 * (total[row, :] + beyond)
    average_rows(total, size_x, size_y)
    for element in range(size_x // NODES):
        value = None
        for i in range(NODES):
            term = float(QUADRATURE[i]) * total[pl.ds((NODES * element + i) * size_y, size_y), :]
            value = term if value is None else value + term
        reduced[pl.ds(element * size_y, size_y), :] = value
    phase = lax.broadcasted_iota(jnp.int32, onehot.shape, 1) & 3
    weight = jnp.where(
        (phase == 0) | (phase == 3), float(QUADRATURE[0] / 4.0), float(QUADRATURE[1] / 4.0)
    )
    forcing[...] = jnp.dot(
        onehot[...] * weight, reduced[...], precision=HIGHEST, preferred_element_type=jnp.float32
    )
    mixed[...] = mix_all(total[...], mix[...])
    local_update(total, total, mixed, wind, work, size_x, size_y, levels, False)


def home_kernel(size_x, size_y, groups, capacity, *refs):
    rank, work, forcing, onehot, mix, cloud_mix, own, near, far = refs[:9]
    pairs = refs[9 : 8 + groups // 2]
    out, to_a, to_b, sends, own_final = refs[8 + groups // 2 : 13 + groups // 2]
    reduced, tendency, cloud, message = refs[13 + groups // 2 :]
    channels = work.shape[1]
    parts = 8 // capacity
    rows = own.shape[0]
    length = near.shape[0]
    cloud[0:rows, :] = own[...]
    unpack(near, channels, cloud, rows, rows)
    for m in range(1, groups // 2):
        unpack(pairs[m - 1].at[0:length], channels, cloud, 2 * m * rows, rows)
        unpack(
            far.at[(m - 1) * length : m * length], channels, cloud, (2 * m + 1) * rows, rows
        )
    cloud_run(cloud, forcing, cloud_mix, rows, parts, tendency, (0,))
    own_final[...] = cloud[0:rows, :]
    tend = tendency[...]
    change = COUPLING * (tend + mix_all(tend, mix[...]))
    part = lax.broadcasted_iota(jnp.int32, onehot.shape, 0) & (parts - 1)
    reduced[...] = lax.dot_general(
        jnp.where(part == 0, onehot[...], 0.0),
        change,
        (((0,), (0,)), ((), ())),
        precision=HIGHEST,
        preferred_element_type=jnp.float32,
    )
    for x in range(size_x):
        row = pl.ds(x * size_y, size_y)
        element = pl.ds((x // NODES) * size_y, size_y)
        out[row, :] = sub_average(work[row, :] + reduced[element, :])
    average_rows(out, size_x, size_y)
    occupied = jnp.max(onehot[...], axis=1, keepdims=True)
    sends[:, 0:channels] = forcing[...]
    sends[:, channels : channels + 1] = occupied
    message[0] = column_of(out, 0, size_x, size_y)
    message[1] = column_of(out, size_y - 1, size_x, size_y)
    even = is_even(rank)
    to_a[0:size_x, 0:channels] = jnp.where(even, message[1], message[0])
    to_b[0:size_x, 0:channels] = jnp.where(even, message[0], message[1])
    to_a[size_x : size_x + 8, :] = sends[8:16, :]
    to_b[size_x : size_x + 8, :] = sends[8 * groups - 8 : 8 * groups, :]


def last_turn_kernel(size_x, size_y, rank, place, partial, from_a, from_b, to_a, to_b, ends):
    channels = partial.shape[1]
    from_left, from_right = in_order(rank, from_a, from_b)
    for index, x in enumerate((0, size_x - 1)):
        value = partial[x * size_y : (x + 1) * size_y, :]
        ends[index] = edge_rows(
            value,
            0.5 * (from_left[x : x + 1, 0:channels] - value[0:1]),
            0.5 * (from_right[x : x + 1, 0:channels] - value[size_y - 1 : size_y]),
        )
    even = is_even(place)
    to_a[...] = jnp.where(even, ends[1], ends[0])
    to_b[...] = jnp.where(even, ends[0], ends[1])


def owner_kernel(size_x, size_y, groups, capacity, *refs):
    rank, partial, from_a, from_b, states, mix, own_final, sends, near = refs[:9]
    pairs = refs[9 : 8 + groups // 2]
    forcings = refs[8 + groups // 2 : 7 + groups // 2 + groups]
    fields, out, field, cloud, forcing, turned, ready, done = refs[7 + groups // 2 + groups :]
    channels = partial.shape[1]
    parts = 8 // capacity
    rows = own_final.shape[0]
    length = near.shape[0]
    from_left, from_right = in_order(rank, from_a, from_b)
    left, right = side_changes(size_x, size_y, partial, from_left, from_right)
    for x in range(size_x):
        row = pl.ds(x * size_y, size_y)
        field[row, :] = edge_rows(partial[row, :], left[x : x + 1], right[x : x + 1])
    copies = [pltpu.make_async_copy(field, fields, done.at[groups])]
    copies[0].start()
    unpack(near, channels, cloud, 0, rows)
    forcing[0:8, :] = forcings[0][:, 0:channels]
    for k in range(2, groups):
        at = (k & 1) * length
        unpack(pairs[k // 2 - 1].at[at : at + length], channels, cloud, (k - 1) * rows, rows)
        forcing[8 * (k - 1) : 8 * k, :] = forcings[k - 1][:, 0:channels]
    cloud_run(cloud, forcing, mix, rows, parts, None, tuple(range(groups - 1)))
    for k in range(groups):
        start = pl.multiple_of((rank[0] ^ k) * rows, rows)
        source, at = (cloud, (k - 1) * rows) if k else (own_final, 0)
        flags = (forcings[k - 1] if k else sends)[0:8, channels : channels + 1]
        settle(source, at, flags, parts, turned.at[k], states, start, ready.at[k], 0, rows)
        copy = pltpu.make_async_copy(ready.at[k], out.at[pl.ds(start, rows), :], done.at[k])
        copy.start()
        copies.append(copy)
    for copy in copies:
        copy.wait()


def finish_kernel(size_x, size_y, place, fields_in, mine_a, mine_b, from_a, from_b,
                  fields, rows, done):
    even = is_even(place)
    last = size_x - 1
    copies = []
    for index, (mine, other, x) in enumerate(
        (
            (mine_a, from_a, jnp.where(even, last, 0)),
            (mine_b, from_b, jnp.where(even, 0, last)),
        )
    ):
        rows[index] = 0.5 * (mine[...] + other[...])
        start = pl.multiple_of(x * size_y, size_y)
        copy = pltpu.make_async_copy(
            rows.at[index], fields.at[pl.ds(start, size_y), :], done.at[index]
        )
        copy.start()
        copies.append(copy)
    for copy in copies:
        copy.wait()


VMEM_GRANT = 12 * 2**20
VMEM = pltpu.MemorySpace.VMEM
SMEM = pltpu.MemorySpace.SMEM
DMA = pltpu.SemaphoreType.DMA


def call(kernel, outs, scratch, *args, smem=(), far=(), far_out=(), aliases=None):
    def space(index, remote):
        if index in smem and not remote:
            return pl.BlockSpec(memory_space=SMEM)
        if index in (far_out if remote else far):
            return pl.BlockSpec(memory_space=pltpu.MemorySpace.HBM)
        return pl.BlockSpec(memory_space=VMEM)

    args = [
        pltpu.with_memory_space_constraint(arg, pltpu.MemorySpace.HBM) if index in far else arg
        for index, arg in enumerate(args)
    ]
    return pl.pallas_call(
        kernel,
        out_shape=[jax.ShapeDtypeStruct(shape, dtype) for shape, dtype in outs],
        in_specs=[space(index, False) for index in range(len(args))],
        out_specs=[space(index, True) for index in range(len(outs))],
        scratch_shapes=[
            item if not isinstance(item, tuple) else pltpu.VMEM(*item) for item in scratch
        ],
        input_output_aliases=aliases or {},
        compiler_params=pltpu.CompilerParams(vmem_limit_bytes=VMEM_GRANT),
    )(*args)


def lower_pairs(count):
    return [(i, i ^ 1) for i in range(count)]


def upper_pairs(count):
    return [(i, (i + 1) % count if i & 1 else (i - 1) % count) for i in range(count)]


def ring(to_a, to_b, axis):
    count = lax.axis_size(axis)
    from_b = lax.ppermute(to_b, axis, upper_pairs(count))
    from_a = lax.ppermute(to_a, axis, lower_pairs(count))
    return from_a, from_b


def on_device(state, wind, dyn_mix, owner, crm_state, crm_mix):
    f32 = jnp.float32
    size_x, size_y, channels = state.shape
    levels = wind.shape[2] // 2
    nodes = size_x * size_y
    groups = lax.axis_size("crm")
    slots, columns = crm_state.shape[:2]
    capacity = slots // groups
    rows = capacity * columns
    elements = size_x // NODES
    lane_count = len(lane_tiles(channels, 128))
    rank = lax.axis_index("crm").astype(jnp.int32).reshape(1)
    place = lax.axis_index("elem").astype(jnp.int32).reshape(1)
    state = state.reshape(nodes, channels)
    wind = wind.reshape(nodes, 2 * levels)
    clouds = crm_state.reshape(slots * columns, channels)
    owners = owner.reshape(owner.shape[0])
    grid = ((nodes, channels), f32)
    xor = [[(i, i ^ k) for i in range(groups)] for k in range(groups)]

    column_message = ((size_x, 3 * channels + 2 * levels), f32)
    partial, to_a, to_b = call(
        functools.partial(begin_kernel, size_x, size_y, levels),
        [grid, column_message, column_message],
        [
            grid, ((nodes, 2 * levels), f32), (dyn_mix.shape, dyn_mix.dtype), grid,
            ((2,) + column_message[0], f32), DMA((3,)),
        ],
        rank, state, wind, dyn_mix,
        smem=(0,), far=(1, 2, 3),
    )
    column_a, column_b = ring(to_a, to_b, "crm")

    length = packing(rows, channels)[2]
    own, near, *pairs = call(
        functools.partial(widen_kernel, groups),
        [((rows, channels), f32), ((length, 128), f32)]
        + [((2 * length, 128), f32)] * (groups // 2 - 1),
        [((groups, lane_count, rows, 128), f32)],
        rank, clouds,
        smem=(0,),
    )
    pairs_in = [lax.ppermute(pairs[m - 1], "crm", xor[2 * m]) for m in range(1, groups // 2)]
    near_in = lax.ppermute(near, "crm", xor[1])

    span = 2 * channels + 2 * levels
    row_message = ((size_y, span + 2 * levels), f32)
    to_a, to_b = call(
        functools.partial(turn_kernel, size_x, size_y, levels),
        [row_message, row_message],
        [((8, span), f32), ((2,) + row_message[0], f32)],
        rank, place, partial, state, wind, column_a, column_b,
        smem=(0, 1),
    )
    row_a, row_b = ring(to_a, to_b, "elem")
    field, known, total, sides, onehot = call(
        functools.partial(ready_kernel, size_x, size_y, levels, capacity),
        [
            grid, grid, grid, ((2, 4, size_x, channels), f32),
            ((8 * groups, elements * size_y), f32),
        ],
        [],
        rank, owners, partial, state, wind, dyn_mix, column_a, column_b,
        smem=(0, 1),
    )
    far_in = lax.ppermute(
        jnp.concatenate([value[length:] for value in pairs_in], axis=0), "crm", xor[1]
    )
    work, forcing = call(
        functools.partial(second_kernel, size_x, size_y, levels),
        [grid, ((8 * groups, channels), f32)],
        [grid, grid, ((elements * size_y, channels), f32)],
        place, field, total, known, sides, onehot, wind, dyn_mix, row_a, row_b,
        smem=(0,),
    )
    edge = ((size_x + 8, channels + 1), f32)
    partial, to_a, to_b, sends, own_final = call(
        functools.partial(home_kernel, size_x, size_y, groups, capacity),
        [grid, edge, edge, ((8 * groups, channels + 1), f32), ((rows, channels), f32)],
        [
            ((elements * size_y, channels), f32),
            ((8 * groups, channels), f32),
            ((groups * rows, channels), f32),
            ((2, size_x, channels), f32),
        ],
        rank, work, forcing, onehot, dyn_mix, crm_mix, own, near_in, far_in, *pairs_in,
        smem=(0,),
    )

    column_a, column_b = ring(to_a, to_b, "crm")
    rides = groups - 1 if all(i ^ j == groups - 1 for i, j in upper_pairs(groups)) else 0
    forcings = []
    for k in range(1, groups):
        if k == 1:
            forcings.append(column_a[size_x:])
        elif k == rides:
            forcings.append(column_b[size_x:])
        else:
            forcings.append(lax.ppermute(sends[8 * k : 8 * k + 8], "crm", xor[k]))
    mine_a, mine_b = call(
        functools.partial(last_turn_kernel, size_x, size_y),
        [((size_y, channels), f32)] * 2,
        [((2, size_y, channels), f32)],
        rank, place, partial, column_a, column_b,
        smem=(0, 1),
    )
    row_a, row_b = ring(mine_a, mine_b, "elem")
    fields, crm_next = call(
        functools.partial(owner_kernel, size_x, size_y, groups, capacity),
        [grid, ((slots * columns, channels), clouds.dtype)],
        [
            grid,
            (((groups - 1) * rows, channels), f32),
            ((8 * (groups - 1), channels), f32),
            ((groups, lane_count, rows, 128), f32),
            ((groups, rows, channels), clouds.dtype),
            DMA((groups + 1,)),
        ],
        rank, partial, column_a, column_b, clouds, crm_mix, own_final, sends, near,
        *pairs, *forcings,
        smem=(0,),
        far_out=(0, 1),
    )
    (third,) = call(
        functools.partial(finish_kernel, size_x, size_y),
        [grid],
        [((2, size_y, channels), f32), DMA((2,))],
        place, fields, mine_a, mine_b, row_a, row_b,
        smem=(0,), far=(1,), far_out=(0,), aliases={1: 0},
    )
    return (
        third.reshape(size_x, size_y, channels),
        crm_next.reshape(slots, columns, channels),
    )


def solution(mesh):
    return jax.shard_map(
        on_device,
        mesh=mesh,
        in_specs=(
            P("elem", "crm", None),
            P("elem", "crm", None),
            P(),
            P(("elem", "crm"), None),
            P(("elem", "crm"), None, None),
            P(),
        ),
        out_specs=(P("elem", "crm", None), P(("elem", "crm"), None, None)),
        check_vma=False,
    )
```

```python
import functools

import jax
import jax.numpy as jnp
import numpy as np
from jax import lax
from jax.experimental import pallas as pl
from jax.experimental.pallas import tpu as pltpu
from jax.sharding import PartitionSpec as P


SUB = 4
CRM_STEP = 0.5
DIFFUSION = 0.2
COUPLING = 0.5
NODES = 4


def gll_derivative():
    points = np.array([-1.0, -1.0 / np.sqrt(5.0), 1.0 / np.sqrt(5.0), 1.0])
    barycentric = np.array(
        [
            1.0 / np.prod([points[i] - points[j] for j in range(NODES) if j != i])
            for i in range(NODES)
        ]
    )
    derivative = np.zeros((NODES, NODES))
    for i in range(NODES):
        for j in range(NODES):
            if j != i:
                derivative[i, j] = barycentric[j] / barycentric[i] / (points[i] - points[j])
        derivative[i, i] = -np.sum(derivative[i])
    return derivative


DERIV = [[float(value) for value in row] for row in gll_derivative().astype(np.float32)]
FIRST, LAST = DERIV[0][0], DERIV[3][3]
QUADRATURE = np.array([1.0, 5.0, 5.0, 1.0]) / 6.0


def lane_tiles(channels, width):
    return [(at, min(at + width, channels)) for at in range(0, channels, width)]


def winds(pair, levels):
    along_x, along_y = pair[:, :levels], pair[:, levels:]
    return (
        jnp.concatenate([along_x, along_x], axis=1),
        jnp.concatenate([along_y, along_y], axis=1),
    )


def full_winds(pair, levels, channels):
    along_x, along_y = winds(pair, levels)
    count = -(-channels // (2 * levels))
    return (
        jnp.concatenate([along_x] * count, axis=1)[:, :channels],
        jnp.concatenate([along_y] * count, axis=1)[:, :channels],
    )


def dx_rows(rows):
    out = []
    for i in range(NODES):
        total = None
        for j in range(NODES):
            if DERIV[i][j] != 0.0 and not (i == j and abs(DERIV[i][j]) < 1e-6):
                term = DERIV[i][j] * rows[j]
                total = term if total is None else total + term
        out.append(total)
    return out


def sublane_coefficients(width):
    position = lax.broadcasted_iota(jnp.int32, (8, width), 0) & 3
    table = []
    for move in range(NODES):
        value = jnp.zeros((8, width), jnp.float32)
        for at in range(NODES):
            value = jnp.where(position == at, DERIV[at][(at + move) % NODES], value)
        table.append((value, position < NODES - move))
    return table


def dsub(field, table):
    width = field.shape[1]
    blocks = []
    for at in range(0, field.shape[0], 8):
        part = field[at : at + 8]
        total = table[0][0][:, :width] * part
        for move in range(1, NODES):
            moved = jnp.where(
                table[move][1][:, :width],
                pltpu.roll(part, 8 - move, 0),
                pltpu.roll(part, NODES - move, 0),
            )
            total = total + table[move][0][:, :width] * moved
        blocks.append(total)
    return blocks[0] if len(blocks) == 1 else jnp.concatenate(blocks, axis=0)


def sub_average(field):
    rows = field.shape[0]
    position = lax.broadcasted_iota(jnp.int32, field.shape, 0)
    phase = position & 3
    upper = (phase == 3) & (position < rows - 1)
    lower = (phase == 0) & (position > 0)
    ahead = pltpu.roll(field, rows - 1, 0)
    behind = pltpu.roll(field, 1, 0)
    partner = jnp.where(upper, ahead, jnp.where(lower, behind, field))
    return 0.5 * (field + partner)


def average_rows(ref, size_x, size_y):
    for at in range(NODES - 1, size_x - 1, NODES):
        low, high = pl.ds(at * size_y, size_y), pl.ds((at + 1) * size_y, size_y)
        mean = 0.5 * (ref[low, :] + ref[high, :])
        ref[low, :] = mean
        ref[high, :] = mean


def end_rows(rows, first, last):
    shape = (rows, first.shape[1])
    position = lax.broadcasted_iota(jnp.int32, shape, 0)
    return jnp.where(position == 0, first, jnp.where(position == rows - 1, last, 0.0))


def edge_rows(rows, first, last):
    position = lax.broadcasted_iota(jnp.int32, rows.shape, 0)
    count = rows.shape[0]
    return rows + jnp.where(
        position == 0, first, jnp.where(position == count - 1, last, 0.0)
    )


def local_update(base_ref, field_ref, mix, wind_ref, out_ref, size_x, size_y, levels, average,
                 mixed_ref=None):
    channels = field_ref.shape[1]
    table = sublane_coefficients(2 * levels)
    strip = NODES * size_y
    for element in range(size_x // NODES):
        whole = pl.ds(element * strip, strip)
        mixed = mix_all(field_ref[whole, :], mix)
        if mixed_ref is not None:
            mixed_ref[whole, :] = mixed
        rows = [pl.ds((NODES * element + i) * size_y, size_y) for i in range(NODES)]
        wind = [winds(wind_ref[row, :], levels) for row in rows]
        for begin, end in lane_tiles(channels, 2 * levels):
            width = end - begin
            values = [field_ref[row, begin:end] for row in rows]
            slopes = dx_rows(values)
            for i in range(NODES):
                along_x, along_y = wind[i][0][:, :width], wind[i][1][:, :width]
                base = values[i] if base_ref is field_ref else base_ref[rows[i], begin:end]
                result = (
                    base
                    + mixed[i * size_y : (i + 1) * size_y, begin:end]
                    - (along_x * slopes[i] + along_y * dsub(values[i], table))
                )
                out_ref[rows[i], begin:end] = sub_average(result) if average else result


def to_bf16(value):
    return value.astype(jnp.bfloat16)


def mix_all(field, mix):
    return jnp.dot(to_bf16(field), mix, preferred_element_type=jnp.float32)


def column_of(ref, y, size_x, size_y):
    return jnp.concatenate(
        [ref[x * size_y + y : x * size_y + y + 1, :] for x in range(size_x)], axis=0
    )


def column_parts(message, channels, levels):
    return (
        message[:, 0:channels],
        message[:, channels : 2 * channels],
        message[:, 2 * channels : 3 * channels],
        message[:, 3 * channels : 3 * channels + 2 * levels],
    )


def select_rows(chosen, values):
    high = to_bf16(values)
    rest = values - high.astype(jnp.float32)
    middle = to_bf16(rest)
    low = to_bf16(rest - middle.astype(jnp.float32))
    return jnp.dot(
        jnp.concatenate([chosen] * 3, axis=1),
        jnp.concatenate([high, middle, low], axis=0),
        preferred_element_type=jnp.float32,
    )


def is_even(rank):
    return (rank[0] & 1) == 0


def begin_kernel(size_x, size_y, levels, rank, state_in, wind_in, mix_in, partial, to_a, to_b,
                 state, wind, mix, message, arrivals):
    channels = state.shape[1]
    copies = [
        pltpu.make_async_copy(source, target, arrivals.at[index])
        for index, (source, target) in enumerate(
            ((state_in, state), (mix_in, mix), (wind_in, wind))
        )
    ]
    for copy in copies:
        copy.start()
    for copy in copies:
        copy.wait()
    local_update(state, state, mix[...], wind, partial, size_x, size_y, levels, True)
    average_rows(partial, size_x, size_y)
    to_left, to_right = message.at[0], message.at[1]
    for out, column, near, row in ((to_left, 0, 0, 0), (to_right, size_y - 1, size_y - NODES, 3)):
        values = [column_of(partial, near + j, size_x, size_y) for j in range(NODES)]
        slope = None
        for j in range(NODES):
            term = DERIV[row][j] * values[j]
            slope = term if slope is None else slope + term
        out[:, 0:channels] = values[row]
        out[:, channels : 2 * channels] = slope
        out[:, 2 * channels : 3 * channels] = column_of(state, column, size_x, size_y)
        out[:, 3 * channels : 3 * channels + 2 * levels] = column_of(wind, column, size_x, size_y)
    even = is_even(rank)
    to_a[...] = jnp.where(even, message[1], message[0])
    to_b[...] = jnp.where(even, message[0], message[1])


def in_order(rank, from_a, from_b):
    even = is_even(rank)
    first, second = from_a[...], from_b[...]
    return jnp.where(even, second, first), jnp.where(even, first, second)


def side_changes(size_x, size_y, partial, from_left, from_right):
    channels = partial.shape[1]
    return (
        0.5 * (from_left[0:size_x, 0:channels] - column_of(partial, 0, size_x, size_y)),
        0.5 * (from_right[0:size_x, 0:channels] - column_of(partial, size_y - 1, size_x, size_y)),
    )


def turn_kernel(size_x, size_y, levels, rank, place, partial, state, wind, from_a, from_b,
                to_a, to_b, line, message):
    channels = state.shape[1]
    from_left, from_right = in_order(rank, from_a, from_b)
    to_up, to_down = message.at[0], message.at[1]
    left_value, left_slope, left_state, left_wind = column_parts(from_left, channels, levels)
    right_value, right_slope, right_state, right_wind = column_parts(from_right, channels, levels)
    span = 2 * channels + 2 * levels
    pieces = span // (2 * levels)
    for out, x, near, kind in ((to_up, 0, 0, 0), (to_down, size_x - 1, size_x - NODES, 3)):
        slope = None
        for j in range(NODES):
            value = partial[pl.ds((near + j) * size_y, size_y), :]
            at = near + j
            left = 0.5 * (left_value[at : at + 1] - value[0:1])
            right = 0.5 * (right_value[at : at + 1] - value[size_y - 1 : size_y])
            value = edge_rows(value, left, right)
            if at == x:
                out[:, 0:channels] = value
                changes = (left, right)
            term = DERIV[kind][j] * value
            slope = term if slope is None else slope + term
        row = pl.ds(x * size_y, size_y)
        along_x, _ = full_winds(wind[row, :], levels, channels)
        out[:, channels : 2 * channels] = state[row, :] - along_x * slope
        out[:, 2 * channels : span] = wind[row, :]
        corners = (
            (left_slope[x : x + 1] - LAST * changes[0], left_state, left_wind, slope[0:1]),
            (
                right_slope[x : x + 1] - FIRST * changes[1],
                right_state,
                right_wind,
                slope[size_y - 1 : size_y],
            ),
        )
        for side, (side_slope, side_state, side_wind, corner_slope) in enumerate(corners):
            pair = side_wind[x : x + 1]
            corner_x, _ = full_winds(pair, levels, channels)
            line[side : side + 1, 0:channels] = side_slope
            line[side : side + 1, channels : 2 * channels] = (
                side_state[x : x + 1] - corner_x * corner_slope
            )
            line[side : side + 1, 2 * channels : span] = pair
            for piece in range(pieces):
                at = side * pieces + piece
                out[at : at + 1, span : span + 2 * levels] = line[
                    side : side + 1, piece * 2 * levels : (piece + 1) * 2 * levels
                ]
        used = 2 * pieces
        if used < size_y:
            out[used:size_y, span : span + 2 * levels] = jnp.zeros(
                (size_y - used, 2 * levels), jnp.float32
            )
    even = is_even(place)
    to_a[...] = jnp.where(even, message[1], message[0])
    to_b[...] = jnp.where(even, message[0], message[1])


def ready_kernel(size_x, size_y, levels, capacity, rank, owner, partial, state, wind, mix,
                 from_a, from_b, field, mixed, total, sides, gather, spread):
    channels = state.shape[1]
    from_left, from_right = in_order(rank, from_a, from_b)
    parts = 8 // capacity
    for out, node_axis in ((gather, 1), (spread, 0)):
        columns = lax.broadcasted_iota(jnp.int32, out.shape, node_axis) >> 2
        named = jnp.zeros(out.shape, jnp.int32)
        for c in range(owner.shape[0]):
            named = jnp.where(columns == c, owner[c], named)
        position = jnp.zeros(out.shape, jnp.int32)
        for c in range(owner.shape[0]):
            position = position + jnp.where((columns > c) & (named == owner[c]), 1, 0)
        slot = ((rank[0] ^ named) * capacity + position) * parts
        rows = lax.broadcasted_iota(jnp.int32, out.shape, 1 - node_axis)
        count = parts if node_axis else 1
        out[...] = jnp.where((rows >= slot) & (rows < slot + count), 1.0, 0.0).astype(jnp.bfloat16)
    left, right = side_changes(size_x, size_y, partial, from_left, from_right)
    for x in range(size_x):
        row = pl.ds(x * size_y, size_y)
        field[row, :] = edge_rows(partial[row, :], left[x : x + 1], right[x : x + 1])
    local_update(state, field, mix[...], wind, total, size_x, size_y, levels, True, mixed)
    table = sublane_coefficients(channels)
    for side, (message, y, change, factor) in enumerate(
        ((from_left, 0, left, LAST), (from_right, size_y - 1, right, FIRST))
    ):
        _, slope, side_state, side_wind = column_parts(message, channels, levels)
        slope = slope - factor * change
        along_x, along_y = full_winds(side_wind, levels, channels)
        beyond = (
            side_state
            + column_of(mixed, y, size_x, size_y)
            - (
                along_x * dsub(column_of(field, y, size_x, size_y), table)
                + along_y * slope
            )
        )
        sides[side, 0] = beyond
        sides[side, 1] = slope
        sides[side, 2] = along_x
        sides[side, 3] = along_y


def part_roll(value, parts, by):
    by = by % parts
    if by == 0:
        return value
    part = lax.broadcasted_iota(jnp.int32, value.shape, 0) & (parts - 1)
    return jnp.where(
        part < parts - by, pltpu.roll(value, 8 - by, 0), pltpu.roll(value, parts - by, 0)
    )


def part_sum(value, parts):
    total = value
    for by in range(1, parts):
        total = total + part_roll(value, parts, by)
    return total


def packing(rows, channels):
    full, rest = channels // 128, channels % 128
    assert rest in (0, 64)
    return full, rest, full * rows + (rows // 2 if rest else 0)


def pack(tile, channels, out, rows):
    full, rest, _ = packing(rows, channels)
    count = rows // 8
    for t in range(count):
        for lane in range(full):
            out[lane * rows + 8 * t : lane * rows + 8 * t + 8, :] = tile(t, lane)
    if rest:
        for t in range(count // 2):
            out[full * rows + 8 * t : full * rows + 8 * t + 8, :] = jnp.concatenate(
                [tile(t, full)[:, :rest], tile(t + count // 2, full)[:, :rest]], axis=1
            )


def unpack(message, channels, out, start, rows):
    full, rest, _ = packing(rows, channels)
    for lane in range(full):
        out[start : start + rows, lane * 128 : lane * 128 + 128] = message[
            lane * rows : (lane + 1) * rows, :
        ]
    if rest:
        half = rows // 2
        tail = message[full * rows : full * rows + half, :]
        out[start : start + half, full * 128 : channels] = tail[:, :rest]
        out[start + half : start + rows, full * 128 : channels] = tail[:, rest:]


def interleave(states, start, channels, turned, rows):
    for lane, (begin, end) in enumerate(lane_tiles(channels, 128)):
        value = states[pl.ds(start, rows), begin:end].astype(jnp.float32)
        turned[lane, 0:rows, 0 : end - begin] = value + value

    def tile(t, lane):
        return turned[lane, pl.ds(t, 8, stride=rows // 8), :]

    return tile


def widen_kernel(groups, rank, states, *refs):
    own, near = refs[:2]
    pairs = refs[2 : 1 + groups // 2]
    turned = refs[-1]
    rows, channels = own.shape
    length = near.shape[0]
    for k in range(groups):
        start = pl.multiple_of((rank[0] ^ k) * rows, rows)
        tile = interleave(states, start, channels, turned.at[k], rows)
        if k == 0:
            for t in range(rows // 8):
                for lane, (begin, end) in enumerate(lane_tiles(channels, 128)):
                    own[8 * t : 8 * t + 8, begin:end] = tile(t, lane)[:, : end - begin]
        elif k == 1:
            pack(tile, channels, near, rows)
        else:
            at = (k & 1) * length
            pack(tile, channels, pairs[k // 2 - 1].at[at : at + length], rows)


def cloud_run(states, blocks, forcing, mix, rows, parts, tendency, finals):
    count = rows // 8
    columns = count * parts
    half = mix[...] * 0.5
    means, totals = {}, {}
    for step in range(SUB):
        last = step == SUB - 1
        for begin in range(0, len(blocks), 2):
            group = range(begin, min(begin + 2, len(blocks)))
            mixed = mix_all(states[begin * rows : (group[-1] + 1) * rows, :], half)
            for block in group:
                push = forcing[8 * blocks[block] : 8 * blocks[block] + 8, :]

                def read(t):
                    at = block * rows + 8 * t
                    return states[at : at + 8, :]

                if step == 0:
                    total = read(0)
                    for t in range(1, count):
                        total = total + read(t)
                    means[block] = part_sum(total, parts) * (0.5 / columns)
                gain = 2.0 * CRM_STEP * (push - means[block])
                keep = not last or block in finals
                total = None
                if keep:
                    start = read(0)
                    behind, here = part_roll(read(count - 1), parts, -1), start
                for t in range(count):
                    at = (block - begin) * rows + 8 * t
                    turn = jnp.tanh(mixed[at : at + 8])
                    total = turn if total is None else total + turn
                    if keep:
                        ahead = read(t + 1) if t + 1 < count else part_roll(start, parts, 1)
                        states[block * rows + 8 * t : block * rows + 8 * t + 8, :] = (
                            (1.0 - 2.0 * CRM_STEP * DIFFUSION) * here
                            + CRM_STEP * DIFFUSION * (behind + ahead)
                        ) + ((2.0 * CRM_STEP) * turn + gain)
                        behind, here = here, ahead
                if tendency is not None or not last:
                    mean = (
                        means[block] + part_sum(total, parts) * (CRM_STEP / columns) + 0.5 * gain
                    )
                    means[block] = mean
                    if tendency is not None:
                        totals[block] = (
                            mean - push if step == 0 else totals[block] + (mean - push)
                        )
    if tendency is not None:
        for block in range(len(blocks)):
            tendency[8 * block : 8 * block + 8, :] = totals[block] * (1.0 / SUB)


def settle(states, start, used, parts, turned, old, old_start, out, out_start, rows):
    channels = states.shape[1]
    count = rows // 8
    for lane, (begin, end) in enumerate(lane_tiles(channels, 128)):
        width = end - begin
        for t in range(count):
            value = 0.5 * states[start + 8 * t : start + 8 * t + 8, begin:end]
            if width < 128:
                value = jnp.concatenate([value, jnp.zeros((8, 128 - width), jnp.float32)], axis=1)
            turned[lane, pl.ds(t, 8, stride=count), :] = value
        for slot in range(8 // parts):
            at = slot * count * parts
            span = count * parts
            flag = used[slot * parts : slot * parts + 1, :] > 0.5
            before = old[pl.ds(old_start + at, span), begin:end].astype(jnp.float32)
            after = turned[lane, at : at + span, 0:width]
            out[pl.ds(out_start + at, span), begin:end] = jnp.where(flag, after, before).astype(
                jnp.bfloat16
            )


def second_kernel(size_x, size_y, levels, place, field, second, known, sides, gather, wind, mix,
                  from_a, from_b, work, forcing, total, reduced):
    from_up, from_down = in_order(place, from_a, from_b)
    channels = field.shape[1]
    span = 2 * channels + 2 * levels
    pieces = span // (2 * levels)
    last_row = pl.ds((size_x - 1) * size_y, size_y)
    first_row = pl.ds(0, size_y)
    small = sublane_coefficients(channels)
    ups = 0.5 * (from_up[:, 0:channels] - field[first_row, :])
    downs = 0.5 * (from_down[:, 0:channels] - field[last_row, :])
    remixed = mix_all(
        jnp.concatenate([field[first_row, :] + ups, field[last_row, :] + downs], axis=0), mix[...]
    )
    new_mixed = (remixed[0:size_y], remixed[size_y : 2 * size_y])
    total[...] = second[...]
    edge_mixed = []
    for index, (x, near, end, change) in enumerate(
        ((0, 0, 0, ups), (size_x - 1, size_x - NODES, 3, downs))
    ):
        edge = pl.ds(x * size_y, size_y)
        edge_mixed.append(new_mixed[index] - known[edge, :])
        for i in range(NODES):
            row = pl.ds((near + i) * size_y, size_y)
            along_x, along_y = full_winds(wind[row, :], levels, channels)
            value = -DERIV[i][end] * (along_x * change)
            if near + i == x:
                value = value + edge_mixed[index] - along_y * dsub(change, small)
            total[row, :] = total[row, :] + sub_average(value)
    corner = {}
    for name, message in enumerate((from_up, from_down)):
        for side in range(2):
            line = jnp.concatenate(
                [
                    message[side * pieces + p : side * pieces + p + 1, span : span + 2 * levels]
                    for p in range(pieces)
                ],
                axis=1,
            )
            corner[name, side] = (
                line[:, 0:channels],
                line[:, channels : 2 * channels],
                line[:, 2 * channels : span],
            )
    edge_slopes = {}
    for side, y in ((0, 0), (1, size_y - 1)):
        slope = sides[side, 1]
        pick = slice(y, y + 1)
        new_first = 0.5 * (corner[0, side][0] + slope[0:1])
        new_last = 0.5 * (corner[1, side][0] + slope[size_x - 1 : size_x])
        edge_slopes[0, side], edge_slopes[1, side] = new_first, new_last
        slope_change = end_rows(
            size_x, new_first - slope[0:1], new_last - slope[size_x - 1 : size_x]
        )
        column_change = end_rows(size_x, ups[pick], downs[pick])
        mixed_change = end_rows(size_x, edge_mixed[0][pick], edge_mixed[1][pick])
        beyond = (
            sides[side, 0]
            + mixed_change
            - (sides[side, 2] * dsub(column_change, small) + sides[side, 3] * slope_change)
        )
        for x in range(size_x):
            at = slice(x * size_y + y, x * size_y + y + 1)
            total[at, :] = 0.5 * (total[at, :] + beyond[x : x + 1])
    for name, message, row, change, factor in (
        (0, from_up, first_row, ups, LAST),
        (1, from_down, last_row, downs, FIRST),
    ):
        along_x, along_y = full_winds(message[:, 2 * channels : span], levels, channels)
        beyond = (
            message[:, channels : 2 * channels]
            + new_mixed[name]
            + factor * along_x * change
            - along_y * dsub(field[row, :] + change, small)
        )
        beyond = sub_average(beyond)
        ends = []
        for side, y in ((0, 0), (1, size_y - 1)):
            _, part, pair = corner[name, side]
            corner_x, corner_y = full_winds(pair, levels, channels)
            value = (
                part
                + new_mixed[name][y : y + 1]
                + factor * corner_x * change[y : y + 1]
                - corner_y * edge_slopes[name, side]
            )
            ends.append(0.5 * (value - beyond[y : y + 1]))
        beyond = edge_rows(beyond, ends[0], ends[1])
        total[row, :] = 0.5 * (total[row, :] + beyond)
    average_rows(total, size_x, size_y)
    phase = lax.broadcasted_iota(jnp.int32, (size_y, channels), 0) & 3
    weight = jnp.where(
        (phase == 0) | (phase == 3), float(QUADRATURE[0] / 4.0), float(QUADRATURE[1] / 4.0)
    )
    for element in range(size_x // NODES):
        value = None
        for i in range(NODES):
            term = float(QUADRATURE[i]) * total[pl.ds((NODES * element + i) * size_y, size_y), :]
            value = term if value is None else value + term
        reduced[pl.ds(element * size_y, size_y), :] = weight * value
    forcing[...] = select_rows(gather[...], reduced[...])
    local_update(total, total, mix[...], wind, work, size_x, size_y, levels, False)


def home_kernel(size_x, size_y, groups, capacity, *refs):
    rank, work, forcing, gather, spread, mix, cloud_mix, own, near, far = refs[:10]
    pairs = refs[10 : 9 + groups // 2]
    out, to_a, to_b, sends, own_final = refs[9 + groups // 2 : 14 + groups // 2]
    reduced, tendency, cloud, message = refs[14 + groups // 2 :]
    channels = work.shape[1]
    parts = 8 // capacity
    rows = own.shape[0]
    length = near.shape[0]
    cloud[0:rows, :] = own[...]
    unpack(near, channels, cloud, rows, rows)
    for m in range(1, groups // 2):
        unpack(pairs[m - 1].at[0:length], channels, cloud, 2 * m * rows, rows)
        unpack(
            far.at[(m - 1) * length : m * length], channels, cloud, (2 * m + 1) * rows, rows
        )
    cloud_run(
        cloud, range(groups), forcing, cloud_mix, rows, parts, tendency, (0,)
    )
    own_final[...] = cloud[0:rows, :]
    tend = tendency[...]
    change = COUPLING * (tend + mix_all(tend, mix[...]))
    reduced[...] = select_rows(spread[...], change)
    for x in range(size_x):
        row = pl.ds(x * size_y, size_y)
        element = pl.ds((x // NODES) * size_y, size_y)
        out[row, :] = sub_average(work[row, :] + reduced[element, :])
    average_rows(out, size_x, size_y)
    occupied = jnp.max(gather[...].astype(jnp.float32), axis=1, keepdims=True)
    sends[:, 0:channels] = forcing[...]
    sends[:, channels : channels + 1] = occupied
    message[0] = column_of(out, 0, size_x, size_y)
    message[1] = column_of(out, size_y - 1, size_x, size_y)
    even = is_even(rank)
    to_a[0:size_x, 0:channels] = jnp.where(even, message[1], message[0])
    to_b[0:size_x, 0:channels] = jnp.where(even, message[0], message[1])
    to_a[size_x : size_x + 8, :] = sends[8:16, :]
    to_b[size_x : size_x + 8, :] = sends[8 * groups - 8 : 8 * groups, :]


def last_turn_kernel(size_x, size_y, rank, place, partial, from_a, from_b, to_a, to_b, ends):
    channels = partial.shape[1]
    from_left, from_right = in_order(rank, from_a, from_b)
    for index, x in enumerate((0, size_x - 1)):
        value = partial[x * size_y : (x + 1) * size_y, :]
        ends[index] = edge_rows(
            value,
            0.5 * (from_left[x : x + 1, 0:channels] - value[0:1]),
            0.5 * (from_right[x : x + 1, 0:channels] - value[size_y - 1 : size_y]),
        )
    even = is_even(place)
    to_a[...] = jnp.where(even, ends[1], ends[0])
    to_b[...] = jnp.where(even, ends[0], ends[1])


def owner_kernel(size_x, size_y, groups, capacity, *refs):
    rank, partial, from_a, from_b, states, mix, own_final, sends, near = refs[:9]
    pairs = refs[9 : 8 + groups // 2]
    forcings = refs[8 + groups // 2 : 7 + groups // 2 + groups]
    fields, out, field, cloud, forcing, turned, ready, done = refs[7 + groups // 2 + groups :]
    channels = partial.shape[1]
    parts = 8 // capacity
    rows = own_final.shape[0]
    length = near.shape[0]
    from_left, from_right = in_order(rank, from_a, from_b)
    left, right = side_changes(size_x, size_y, partial, from_left, from_right)
    for x in range(size_x):
        row = pl.ds(x * size_y, size_y)
        field[row, :] = edge_rows(partial[row, :], left[x : x + 1], right[x : x + 1])
    copies = [pltpu.make_async_copy(field, fields, done.at[groups])]
    copies[0].start()
    unpack(near, channels, cloud, 0, rows)
    forcing[0:8, :] = forcings[0][:, 0:channels]
    for k in range(2, groups):
        at = (k & 1) * length
        unpack(pairs[k // 2 - 1].at[at : at + length], channels, cloud, (k - 1) * rows, rows)
        forcing[8 * (k - 1) : 8 * k, :] = forcings[k - 1][:, 0:channels]
    blocks = tuple(range(groups - 1))
    cloud_run(cloud, blocks, forcing, mix, rows, parts, None, blocks)
    for k in range(groups):
        start = pl.multiple_of((rank[0] ^ k) * rows, rows)
        source, at = (cloud, (k - 1) * rows) if k else (own_final, 0)
        flags = (forcings[k - 1] if k else sends)[0:8, channels : channels + 1]
        settle(source, at, flags, parts, turned.at[k], states, start, ready.at[k], 0, rows)
        copy = pltpu.make_async_copy(ready.at[k], out.at[pl.ds(start, rows), :], done.at[k])
        copy.start()
        copies.append(copy)
    for copy in copies:
        copy.wait()


def finish_kernel(size_x, size_y, place, fields_in, mine_a, mine_b, from_a, from_b,
                  fields, rows, done):
    even = is_even(place)
    last = size_x - 1
    copies = []
    for index, (mine, other, x) in enumerate(
        (
            (mine_a, from_a, jnp.where(even, last, 0)),
            (mine_b, from_b, jnp.where(even, 0, last)),
        )
    ):
        rows[index] = 0.5 * (mine[...] + other[...])
        start = pl.multiple_of(x * size_y, size_y)
        copy = pltpu.make_async_copy(
            rows.at[index], fields.at[pl.ds(start, size_y), :], done.at[index]
        )
        copy.start()
        copies.append(copy)
    for copy in copies:
        copy.wait()


VMEM_GRANT = 12 * 2**20
VMEM = pltpu.MemorySpace.VMEM
SMEM = pltpu.MemorySpace.SMEM
DMA = pltpu.SemaphoreType.DMA


def call(kernel, outs, scratch, *args, smem=(), far=(), far_out=(), aliases=None):
    def space(index, remote):
        if index in smem and not remote:
            return pl.BlockSpec(memory_space=SMEM)
        if index in (far_out if remote else far):
            return pl.BlockSpec(memory_space=pltpu.MemorySpace.HBM)
        return pl.BlockSpec(memory_space=VMEM)

    args = [
        pltpu.with_memory_space_constraint(arg, pltpu.MemorySpace.HBM) if index in far else arg
        for index, arg in enumerate(args)
    ]
    return pl.pallas_call(
        kernel,
        out_shape=[jax.ShapeDtypeStruct(shape, dtype) for shape, dtype in outs],
        in_specs=[space(index, False) for index in range(len(args))],
        out_specs=[space(index, True) for index in range(len(outs))],
        scratch_shapes=[
            item if not isinstance(item, tuple) else pltpu.VMEM(*item) for item in scratch
        ],
        input_output_aliases=aliases or {},
        compiler_params=pltpu.CompilerParams(vmem_limit_bytes=VMEM_GRANT),
    )(*args)


def lower_pairs(count):
    return [(i, i ^ 1) for i in range(count)]


def upper_pairs(count):
    return [(i, (i + 1) % count if i & 1 else (i - 1) % count) for i in range(count)]


def ring(to_a, to_b, axis):
    count = lax.axis_size(axis)
    from_b = lax.ppermute(to_b, axis, upper_pairs(count))
    from_a = lax.ppermute(to_a, axis, lower_pairs(count))
    return from_a, from_b


def on_device(state, wind, dyn_mix, owner, crm_state, crm_mix):
    f32 = jnp.float32
    size_x, size_y, channels = state.shape
    levels = wind.shape[2] // 2
    nodes = size_x * size_y
    groups = lax.axis_size("crm")
    slots, columns = crm_state.shape[:2]
    capacity = slots // groups
    rows = capacity * columns
    elements = size_x // NODES
    lane_count = len(lane_tiles(channels, 128))
    rank = lax.axis_index("crm").astype(jnp.int32).reshape(1)
    place = lax.axis_index("elem").astype(jnp.int32).reshape(1)
    state = state.reshape(nodes, channels)
    wind = wind.reshape(nodes, 2 * levels)
    clouds = crm_state.reshape(slots * columns, channels)
    owners = owner.reshape(owner.shape[0])
    grid = ((nodes, channels), f32)
    xor = [[(i, i ^ k) for i in range(groups)] for k in range(groups)]

    column_message = ((size_x, 3 * channels + 2 * levels), f32)
    partial, to_a, to_b = call(
        functools.partial(begin_kernel, size_x, size_y, levels),
        [grid, column_message, column_message],
        [
            grid, ((nodes, 2 * levels), f32), (dyn_mix.shape, dyn_mix.dtype),
            ((2,) + column_message[0], f32), DMA((3,)),
        ],
        rank, state, wind, dyn_mix,
        smem=(0,), far=(1, 2, 3),
    )
    column_a, column_b = ring(to_a, to_b, "crm")

    length = packing(rows, channels)[2]
    own, near, *pairs = call(
        functools.partial(widen_kernel, groups),
        [((rows, channels), f32), ((length, 128), f32)]
        + [((2 * length, 128), f32)] * (groups // 2 - 1),
        [((groups, lane_count, rows, 128), f32)],
        rank, clouds,
        smem=(0,),
    )
    pairs_in = [lax.ppermute(pairs[m - 1], "crm", xor[2 * m]) for m in range(1, groups // 2)]
    near_in = lax.ppermute(near, "crm", xor[1])

    span = 2 * channels + 2 * levels
    row_message = ((size_y, span + 2 * levels), f32)
    to_a, to_b = call(
        functools.partial(turn_kernel, size_x, size_y, levels),
        [row_message, row_message],
        [((8, span), f32), ((2,) + row_message[0], f32)],
        rank, place, partial, state, wind, column_a, column_b,
        smem=(0, 1),
    )
    row_a, row_b = ring(to_a, to_b, "elem")
    field, known, total, sides, gather, spread = call(
        functools.partial(ready_kernel, size_x, size_y, levels, capacity),
        [
            grid, grid, grid, ((2, 4, size_x, channels), f32),
            ((8 * groups, elements * size_y), jnp.bfloat16),
            ((elements * size_y, 8 * groups), jnp.bfloat16),
        ],
        [],
        rank, owners, partial, state, wind, dyn_mix, column_a, column_b,
        smem=(0, 1),
    )
    far_in = lax.ppermute(
        jnp.concatenate([value[length:] for value in pairs_in], axis=0), "crm", xor[1]
    )
    work, forcing = call(
        functools.partial(second_kernel, size_x, size_y, levels),
        [grid, ((8 * groups, channels), f32)],
        [grid, ((elements * size_y, channels), f32)],
        place, field, total, known, sides, gather, wind, dyn_mix, row_a, row_b,
        smem=(0,),
    )
    edge = ((size_x + 8, channels + 1), f32)
    partial, to_a, to_b, sends, own_final = call(
        functools.partial(home_kernel, size_x, size_y, groups, capacity),
        [grid, edge, edge, ((8 * groups, channels + 1), f32), ((rows, channels), f32)],
        [
            ((elements * size_y, channels), f32),
            ((8 * groups, channels), f32),
            ((groups * rows, channels), f32),
            ((2, size_x, channels), f32),
        ],
        rank, work, forcing, gather, spread, dyn_mix, crm_mix, own, near_in, far_in, *pairs_in,
        smem=(0,),
    )

    column_a, column_b = ring(to_a, to_b, "crm")
    rides = groups - 1 if all(i ^ j == groups - 1 for i, j in upper_pairs(groups)) else 0
    forcings = []
    for k in range(1, groups):
        if k == 1:
            forcings.append(column_a[size_x:])
        elif k == rides:
            forcings.append(column_b[size_x:])
        else:
            forcings.append(lax.ppermute(sends[8 * k : 8 * k + 8], "crm", xor[k]))
    mine_a, mine_b = call(
        functools.partial(last_turn_kernel, size_x, size_y),
        [((size_y, channels), f32)] * 2,
        [((2, size_y, channels), f32)],
        rank, place, partial, column_a, column_b,
        smem=(0, 1),
    )
    row_a, row_b = ring(mine_a, mine_b, "elem")
    fields, crm_next = call(
        functools.partial(owner_kernel, size_x, size_y, groups, capacity),
        [grid, ((slots * columns, channels), clouds.dtype)],
        [
            grid,
            (((groups - 1) * rows, channels), f32),
            ((8 * (groups - 1), channels), f32),
            ((groups, lane_count, rows, 128), f32),
            ((groups, rows, channels), clouds.dtype),
            DMA((groups + 1,)),
        ],
        rank, partial, column_a, column_b, clouds, crm_mix, own_final, sends, near,
        *pairs, *forcings,
        smem=(0,),
        far_out=(0, 1),
    )
    (third,) = call(
        functools.partial(finish_kernel, size_x, size_y),
        [grid],
        [((2, size_y, channels), f32), DMA((2,))],
        place, fields, mine_a, mine_b, row_a, row_b,
        smem=(0,), far=(1,), far_out=(0,), aliases={1: 0},
    )
    return (
        third.reshape(size_x, size_y, channels),
        crm_next.reshape(slots, columns, channels),
    )


def solution(mesh):
    return jax.shard_map(
        on_device,
        mesh=mesh,
        in_specs=(
            P("elem", "crm", None),
            P("elem", "crm", None),
            P(),
            P(("elem", "crm"), None),
            P(("elem", "crm"), None, None),
            P(),
        ),
        out_specs=(P("elem", "crm", None), P(("elem", "crm"), None, None)),
        check_vma=False,
    )
```

```python
import functools

import jax
import jax.numpy as jnp
import numpy as np
from jax import lax
from jax.experimental import pallas as pl
from jax.experimental.pallas import tpu as pltpu
from jax.sharding import PartitionSpec as P


SUB = 4
CRM_STEP = 0.5
DIFFUSION = 0.2
COUPLING = 0.5
NODES = 4


def gll_derivative():
    points = np.array([-1.0, -1.0 / np.sqrt(5.0), 1.0 / np.sqrt(5.0), 1.0])
    barycentric = np.array(
        [
            1.0 / np.prod([points[i] - points[j] for j in range(NODES) if j != i])
            for i in range(NODES)
        ]
    )
    derivative = np.zeros((NODES, NODES))
    for i in range(NODES):
        for j in range(NODES):
            if j != i:
                derivative[i, j] = barycentric[j] / barycentric[i] / (points[i] - points[j])
        derivative[i, i] = -np.sum(derivative[i])
    return derivative


DERIV = [[float(value) for value in row] for row in gll_derivative().astype(np.float32)]
FIRST, LAST = DERIV[0][0], DERIV[3][3]
QUADRATURE = np.array([1.0, 5.0, 5.0, 1.0]) / 6.0


def lane_tiles(channels, width):
    return [(at, min(at + width, channels)) for at in range(0, channels, width)]


def winds(pair, levels):
    along_x, along_y = pair[:, :levels], pair[:, levels:]
    return (
        jnp.concatenate([along_x, along_x], axis=1),
        jnp.concatenate([along_y, along_y], axis=1),
    )


def full_winds(pair, levels, channels):
    along_x, along_y = winds(pair, levels)
    count = -(-channels // (2 * levels))
    return (
        jnp.concatenate([along_x] * count, axis=1)[:, :channels],
        jnp.concatenate([along_y] * count, axis=1)[:, :channels],
    )


def dx_rows(rows):
    out = []
    for i in range(NODES):
        total = None
        for j in range(NODES):
            if DERIV[i][j] != 0.0 and not (i == j and abs(DERIV[i][j]) < 1e-6):
                term = DERIV[i][j] * rows[j]
                total = term if total is None else total + term
        out.append(total)
    return out


def sublane_coefficients(width):
    position = lax.broadcasted_iota(jnp.int32, (8, width), 0) & 3
    table = []
    for move in range(NODES):
        value = jnp.zeros((8, width), jnp.float32)
        for at in range(NODES):
            value = jnp.where(position == at, DERIV[at][(at + move) % NODES], value)
        table.append((value, position < NODES - move))
    return table


def dsub(field, table):
    width = field.shape[1]
    blocks = []
    for at in range(0, field.shape[0], 8):
        part = field[at : at + 8]
        total = table[0][0][:, :width] * part
        for move in range(1, NODES):
            moved = jnp.where(
                table[move][1][:, :width],
                pltpu.roll(part, 8 - move, 0),
                pltpu.roll(part, NODES - move, 0),
            )
            total = total + table[move][0][:, :width] * moved
        blocks.append(total)
    return blocks[0] if len(blocks) == 1 else jnp.concatenate(blocks, axis=0)


def sub_average(field):
    rows = field.shape[0]
    position = lax.broadcasted_iota(jnp.int32, field.shape, 0)
    phase = position & 3
    upper = (phase == 3) & (position < rows - 1)
    lower = (phase == 0) & (position > 0)
    ahead = pltpu.roll(field, rows - 1, 0)
    behind = pltpu.roll(field, 1, 0)
    partner = jnp.where(upper, ahead, jnp.where(lower, behind, field))
    return 0.5 * (field + partner)


def average_rows(ref, size_x, size_y):
    for at in range(NODES - 1, size_x - 1, NODES):
        low, high = pl.ds(at * size_y, size_y), pl.ds((at + 1) * size_y, size_y)
        mean = 0.5 * (ref[low, :] + ref[high, :])
        ref[low, :] = mean
        ref[high, :] = mean


def end_rows(rows, first, last):
    shape = (rows, first.shape[1])
    position = lax.broadcasted_iota(jnp.int32, shape, 0)
    return jnp.where(position == 0, first, jnp.where(position == rows - 1, last, 0.0))


def edge_rows(rows, first, last):
    position = lax.broadcasted_iota(jnp.int32, rows.shape, 0)
    count = rows.shape[0]
    return rows + jnp.where(
        position == 0, first, jnp.where(position == count - 1, last, 0.0)
    )


def local_update(base_ref, field_ref, mix, wind_ref, out_ref, size_x, size_y, levels, average,
                 mixed_ref=None, change_ref=None):
    channels = field_ref.shape[1]
    table = sublane_coefficients(2 * levels)
    strip = NODES * size_y
    for element in range(size_x // NODES):
        whole = pl.ds(element * strip, strip)
        mixed = mix_all(field_ref[whole, :], mix)
        if mixed_ref is not None:
            mixed_ref[whole, :] = mixed
        rows = [pl.ds((NODES * element + i) * size_y, size_y) for i in range(NODES)]
        wind = [winds(wind_ref[row, :], levels) for row in rows]
        for begin, end in lane_tiles(channels, 2 * levels):
            width = end - begin
            values = [field_ref[row, begin:end] for row in rows]
            slopes = dx_rows(values)
            for i in range(NODES):
                along_x, along_y = wind[i][0][:, :width], wind[i][1][:, :width]
                base = values[i] if base_ref is field_ref else base_ref[rows[i], begin:end]
                result = (
                    base
                    + mixed[i * size_y : (i + 1) * size_y, begin:end]
                    - (along_x * slopes[i] + along_y * dsub(values[i], table))
                )
                if change_ref is not None:
                    result = result + change_ref[pl.ds(element * size_y, size_y), begin:end]
                out_ref[rows[i], begin:end] = sub_average(result) if average else result


def to_bf16(value):
    return value.astype(jnp.bfloat16)


def mix_all(field, mix):
    return jnp.dot(to_bf16(field), mix, preferred_element_type=jnp.float32)


def column_of(ref, y, size_x, size_y):
    return jnp.concatenate(
        [ref[x * size_y + y : x * size_y + y + 1, :] for x in range(size_x)], axis=0
    )


def column_parts(message, channels, levels):
    span = 2 * channels + 2 * levels
    tiles = lane_tiles(channels, 128)
    slopes = [
        jnp.concatenate(
            [
                message[end * len(tiles) + p : end * len(tiles) + p + 1, span : span + last - first]
                for p, (first, last) in enumerate(tiles)
            ],
            axis=1,
        )
        for end in range(2)
    ]
    return (
        message[:, 0:channels],
        message[:, channels : 2 * channels],
        message[:, 2 * channels : span],
        slopes,
    )


def select_rows(chosen, values):
    high = to_bf16(values)
    rest = values - high.astype(jnp.float32)
    middle = to_bf16(rest)
    low = to_bf16(rest - middle.astype(jnp.float32))
    return jnp.dot(
        jnp.concatenate([chosen] * 3, axis=1),
        jnp.concatenate([high, middle, low], axis=0),
        preferred_element_type=jnp.float32,
    )


def is_even(rank):
    return (rank[0] & 1) == 0


def begin_kernel(size_x, size_y, levels, rank, state_in, wind_in, mix_in, partial, to_a, to_b,
                 state, wind, mix, message, arrivals):
    channels = state.shape[1]
    copies = [
        pltpu.make_async_copy(source, target, arrivals.at[index])
        for index, (source, target) in enumerate(
            ((state_in, state), (mix_in, mix), (wind_in, wind))
        )
    ]
    for copy in copies:
        copy.start()
    for copy in copies:
        copy.wait()
    local_update(state, state, mix[...], wind, partial, size_x, size_y, levels, True)
    average_rows(partial, size_x, size_y)
    to_left, to_right = message.at[0], message.at[1]
    for out, column, near, row in ((to_left, 0, 0, 0), (to_right, size_y - 1, size_y - NODES, 3)):
        values = [column_of(partial, near + j, size_x, size_y) for j in range(NODES)]
        slope = None
        for j in range(NODES):
            term = DERIV[row][j] * values[j]
            slope = term if slope is None else slope + term
        pair = column_of(wind, column, size_x, size_y)
        _, along_y = full_winds(pair, levels, channels)
        span = 2 * channels + 2 * levels
        out[:, 0:channels] = values[row]
        out[:, channels : 2 * channels] = (
            column_of(state, column, size_x, size_y) - along_y * slope
        )
        out[:, 2 * channels : span] = pair
        out[:, span : span + 128] = jnp.zeros((size_x, 128), jnp.float32)
        tiles = lane_tiles(channels, 128)
        for end, x in enumerate((0, size_x - 1)):
            for piece, (first, last) in enumerate(tiles):
                at = end * len(tiles) + piece
                out[at : at + 1, span : span + last - first] = slope[x : x + 1, first:last]
    even = is_even(rank)
    to_a[...] = jnp.where(even, message[1], message[0])
    to_b[...] = jnp.where(even, message[0], message[1])


def in_order(rank, from_a, from_b):
    even = is_even(rank)
    first, second = from_a[...], from_b[...]
    return jnp.where(even, second, first), jnp.where(even, first, second)


def side_changes(size_x, size_y, partial, from_left, from_right):
    channels = partial.shape[1]
    return (
        0.5 * (from_left[0:size_x, 0:channels] - column_of(partial, 0, size_x, size_y)),
        0.5 * (from_right[0:size_x, 0:channels] - column_of(partial, size_y - 1, size_x, size_y)),
    )


def turn_kernel(size_x, size_y, levels, rank, place, partial, state, wind, from_a, from_b,
                to_a, to_b, line, message):
    channels = state.shape[1]
    from_left, from_right = in_order(rank, from_a, from_b)
    to_up, to_down = message.at[0], message.at[1]
    left_value, left_part, left_wind, left_slopes = column_parts(from_left, channels, levels)
    right_value, right_part, right_wind, right_slopes = column_parts(
        from_right, channels, levels
    )
    span = 2 * channels + 2 * levels
    pieces = span // (2 * levels)
    for end, (out, x, near, kind) in enumerate(
        ((to_up, 0, 0, 0), (to_down, size_x - 1, size_x - NODES, 3))
    ):
        slope = None
        for j in range(NODES):
            value = partial[pl.ds((near + j) * size_y, size_y), :]
            at = near + j
            left = 0.5 * (left_value[at : at + 1] - value[0:1])
            right = 0.5 * (right_value[at : at + 1] - value[size_y - 1 : size_y])
            value = edge_rows(value, left, right)
            if at == x:
                out[:, 0:channels] = value
                changes = (left, right)
            term = DERIV[kind][j] * value
            slope = term if slope is None else slope + term
        row = pl.ds(x * size_y, size_y)
        along_x, _ = full_winds(wind[row, :], levels, channels)
        out[:, channels : 2 * channels] = state[row, :] - along_x * slope
        out[:, 2 * channels : span] = wind[row, :]
        corners = (
            (left_slopes[end], LAST * changes[0], left_part, left_wind, slope[0:1]),
            (
                right_slopes[end],
                FIRST * changes[1],
                right_part,
                right_wind,
                slope[size_y - 1 : size_y],
            ),
        )
        for side, (side_slope, fix, side_part, side_wind, corner_slope) in enumerate(corners):
            pair = side_wind[x : x + 1]
            corner_x, corner_y = full_winds(pair, levels, channels)
            line[side : side + 1, 0:channels] = side_slope - fix
            line[side : side + 1, channels : 2 * channels] = (
                side_part[x : x + 1] + corner_y * side_slope - corner_x * corner_slope
            )
            line[side : side + 1, 2 * channels : span] = pair
            for piece in range(pieces):
                at = side * pieces + piece
                out[at : at + 1, span : span + 2 * levels] = line[
                    side : side + 1, piece * 2 * levels : (piece + 1) * 2 * levels
                ]
        used = 2 * pieces
        if used < size_y:
            out[used:size_y, span : span + 2 * levels] = jnp.zeros(
                (size_y - used, 2 * levels), jnp.float32
            )
    even = is_even(place)
    to_a[...] = jnp.where(even, message[1], message[0])
    to_b[...] = jnp.where(even, message[0], message[1])


def ready_kernel(size_x, size_y, levels, capacity, rank, owner, partial, state, wind, mix,
                 from_a, from_b, field, mixed, total, sides, gather, spread):
    channels = state.shape[1]
    from_left, from_right = in_order(rank, from_a, from_b)
    parts = 8 // capacity
    for out, node_axis in ((gather, 1), (spread, 0)):
        columns = lax.broadcasted_iota(jnp.int32, out.shape, node_axis) >> 2
        named = jnp.zeros(out.shape, jnp.int32)
        for c in range(owner.shape[0]):
            named = jnp.where(columns == c, owner[c], named)
        position = jnp.zeros(out.shape, jnp.int32)
        for c in range(owner.shape[0]):
            position = position + jnp.where((columns > c) & (named == owner[c]), 1, 0)
        slot = ((rank[0] ^ named) * capacity + position) * parts
        rows = lax.broadcasted_iota(jnp.int32, out.shape, 1 - node_axis)
        count = parts if node_axis else 1
        out[...] = jnp.where((rows >= slot) & (rows < slot + count), 1.0, 0.0).astype(jnp.bfloat16)
    left, right = side_changes(size_x, size_y, partial, from_left, from_right)
    for x in range(size_x):
        row = pl.ds(x * size_y, size_y)
        field[row, :] = edge_rows(partial[row, :], left[x : x + 1], right[x : x + 1])
    local_update(state, field, mix[...], wind, total, size_x, size_y, levels, True, mixed)
    table = sublane_coefficients(channels)
    for side, (message, y, change, factor) in enumerate(
        ((from_left, 0, left, LAST), (from_right, size_y - 1, right, FIRST))
    ):
        _, side_part, side_wind, slopes = column_parts(message, channels, levels)
        along_x, along_y = full_winds(side_wind, levels, channels)
        sides[side, 0] = (
            side_part
            + column_of(mixed, y, size_x, size_y)
            - along_x * dsub(column_of(field, y, size_x, size_y), table)
            + factor * (along_y * change)
        )
        sides[side, 1] = end_rows(
            size_x,
            slopes[0] - factor * change[0:1],
            slopes[1] - factor * change[size_x - 1 : size_x],
        )
        sides[side, 2] = along_x
        sides[side, 3] = along_y


def part_roll(value, parts, by):
    by = by % parts
    if by == 0:
        return value
    part = lax.broadcasted_iota(jnp.int32, value.shape, 0) & (parts - 1)
    return jnp.where(
        part < parts - by, pltpu.roll(value, 8 - by, 0), pltpu.roll(value, parts - by, 0)
    )


def part_sum(value, parts):
    total = value
    for by in range(1, parts):
        total = total + part_roll(value, parts, by)
    return total


def packing(rows, channels):
    full, rest = channels // 128, channels % 128
    assert rest in (0, 64)
    return full, rest, full * rows + (rows // 2 if rest else 0)


def pack(tile, channels, out, rows):
    full, rest, _ = packing(rows, channels)
    count = rows // 8
    for t in range(count):
        for lane in range(full):
            out[lane * rows + 8 * t : lane * rows + 8 * t + 8, :] = tile(t, lane)
    if rest:
        for t in range(count // 2):
            out[full * rows + 8 * t : full * rows + 8 * t + 8, :] = jnp.concatenate(
                [tile(t, full)[:, :rest], tile(t + count // 2, full)[:, :rest]], axis=1
            )


def unpack(message, channels, out, start, rows):
    full, rest, _ = packing(rows, channels)
    for lane in range(full):
        out[start : start + rows, lane * 128 : lane * 128 + 128] = message[
            lane * rows : (lane + 1) * rows, :
        ]
    if rest:
        half = rows // 2
        tail = message[full * rows : full * rows + half, :]
        out[start : start + half, full * 128 : channels] = tail[:, :rest]
        out[start + half : start + rows, full * 128 : channels] = tail[:, rest:]


def interleave(states, start, channels, turned, rows):
    for lane, (begin, end) in enumerate(lane_tiles(channels, 128)):
        value = states[pl.ds(start, rows), begin:end].astype(jnp.float32)
        turned[lane, 0:rows, 0 : end - begin] = value + value

    def tile(t, lane):
        return turned[lane, pl.ds(t, 8, stride=rows // 8), :]

    return tile


def widen_kernel(groups, rank, states, *refs):
    own, outs, turned = refs[0], refs[1:groups], refs[groups]
    rows, channels = own.shape
    for k in range(groups):
        start = pl.multiple_of((rank[0] ^ k) * rows, rows)
        tile = interleave(states, start, channels, turned.at[k], rows)
        if k:
            pack(tile, channels, outs[k - 1], rows)
        else:
            for t in range(rows // 8):
                for lane, (begin, end) in enumerate(lane_tiles(channels, 128)):
                    own[8 * t : 8 * t + 8, begin:end] = tile(t, lane)[:, : end - begin]


def cloud_run(states, blocks, forcing, mix, rows, parts, tendency, finals):
    count = rows // 8
    columns = count * parts
    half = mix[...] * 0.5
    means, totals = {}, {}
    for step in range(SUB):
        last = step == SUB - 1
        for begin in range(0, len(blocks), 2):
            group = range(begin, min(begin + 2, len(blocks)))
            mixed = mix_all(states[begin * rows : (group[-1] + 1) * rows, :], half)
            for block in group:
                push = forcing[8 * blocks[block] : 8 * blocks[block] + 8, :]

                def read(t):
                    at = block * rows + 8 * t
                    return states[at : at + 8, :]

                if step == 0:
                    total = read(0)
                    for t in range(1, count):
                        total = total + read(t)
                    means[block] = part_sum(total, parts) * (0.5 / columns)
                gain = 2.0 * CRM_STEP * (push - means[block])
                keep = not last or block in finals
                total = None
                if keep:
                    start = read(0)
                    behind, here = part_roll(read(count - 1), parts, -1), start
                for t in range(count):
                    at = (block - begin) * rows + 8 * t
                    turn = jnp.tanh(mixed[at : at + 8])
                    total = turn if total is None else total + turn
                    if keep:
                        ahead = read(t + 1) if t + 1 < count else part_roll(start, parts, 1)
                        states[block * rows + 8 * t : block * rows + 8 * t + 8, :] = (
                            (1.0 - 2.0 * CRM_STEP * DIFFUSION) * here
                            + CRM_STEP * DIFFUSION * (behind + ahead)
                        ) + ((2.0 * CRM_STEP) * turn + gain)
                        behind, here = here, ahead
                if tendency is not None or not last:
                    mean = (
                        means[block] + part_sum(total, parts) * (CRM_STEP / columns) + 0.5 * gain
                    )
                    means[block] = mean
                    if tendency is not None:
                        totals[block] = (
                            mean - push if step == 0 else totals[block] + (mean - push)
                        )
    if tendency is not None:
        for block in range(len(blocks)):
            tendency[8 * block : 8 * block + 8, :] = totals[block] * (1.0 / SUB)


def settle(states, start, used, parts, turned, old, old_start, out, out_start, rows):
    channels = states.shape[1]
    count = rows // 8
    for lane, (begin, end) in enumerate(lane_tiles(channels, 128)):
        width = end - begin
        for t in range(count):
            value = 0.5 * states[start + 8 * t : start + 8 * t + 8, begin:end]
            if width < 128:
                value = jnp.concatenate([value, jnp.zeros((8, 128 - width), jnp.float32)], axis=1)
            turned[lane, pl.ds(t, 8, stride=count), :] = value
        for slot in range(8 // parts):
            at = slot * count * parts
            span = count * parts
            flag = used[slot * parts : slot * parts + 1, :] > 0.5
            before = old[pl.ds(old_start + at, span), begin:end].astype(jnp.float32)
            after = turned[lane, at : at + span, 0:width]
            out[pl.ds(out_start + at, span), begin:end] = jnp.where(flag, after, before).astype(
                jnp.bfloat16
            )


def second_kernel(size_x, size_y, levels, place, field, second, known, sides, gather, wind, mix,
                  from_a, from_b, total, work, forcing, reduced):
    from_up, from_down = in_order(place, from_a, from_b)
    channels = field.shape[1]
    span = 2 * channels + 2 * levels
    pieces = span // (2 * levels)
    last_row = pl.ds((size_x - 1) * size_y, size_y)
    first_row = pl.ds(0, size_y)
    small = sublane_coefficients(channels)
    ups = 0.5 * (from_up[:, 0:channels] - field[first_row, :])
    downs = 0.5 * (from_down[:, 0:channels] - field[last_row, :])
    remixed = mix_all(
        jnp.concatenate([field[first_row, :] + ups, field[last_row, :] + downs], axis=0), mix[...]
    )
    new_mixed = (remixed[0:size_y], remixed[size_y : 2 * size_y])
    total[...] = second[...]
    edge_mixed = []
    for index, (x, near, end, change) in enumerate(
        ((0, 0, 0, ups), (size_x - 1, size_x - NODES, 3, downs))
    ):
        edge = pl.ds(x * size_y, size_y)
        edge_mixed.append(new_mixed[index] - known[edge, :])
        for i in range(NODES):
            row = pl.ds((near + i) * size_y, size_y)
            along_x, along_y = full_winds(wind[row, :], levels, channels)
            value = -DERIV[i][end] * (along_x * change)
            if near + i == x:
                value = value + edge_mixed[index] - along_y * dsub(change, small)
            total[row, :] = total[row, :] + sub_average(value)
    corner = {}
    for name, message in enumerate((from_up, from_down)):
        for side in range(2):
            line = jnp.concatenate(
                [
                    message[side * pieces + p : side * pieces + p + 1, span : span + 2 * levels]
                    for p in range(pieces)
                ],
                axis=1,
            )
            corner[name, side] = (
                line[:, 0:channels],
                line[:, channels : 2 * channels],
                line[:, 2 * channels : span],
            )
    edge_slopes = {}
    for side, y in ((0, 0), (1, size_y - 1)):
        slope = sides[side, 1]
        pick = slice(y, y + 1)
        new_first = 0.5 * (corner[0, side][0] + slope[0:1])
        new_last = 0.5 * (corner[1, side][0] + slope[size_x - 1 : size_x])
        edge_slopes[0, side], edge_slopes[1, side] = new_first, new_last
        slope_change = end_rows(
            size_x, new_first - slope[0:1], new_last - slope[size_x - 1 : size_x]
        )
        column_change = end_rows(size_x, ups[pick], downs[pick])
        mixed_change = end_rows(size_x, edge_mixed[0][pick], edge_mixed[1][pick])
        beyond = (
            sides[side, 0]
            + mixed_change
            - (sides[side, 2] * dsub(column_change, small) + sides[side, 3] * slope_change)
        )
        for x in range(size_x):
            at = slice(x * size_y + y, x * size_y + y + 1)
            total[at, :] = 0.5 * (total[at, :] + beyond[x : x + 1])
    for name, message, row, change, factor in (
        (0, from_up, first_row, ups, LAST),
        (1, from_down, last_row, downs, FIRST),
    ):
        along_x, along_y = full_winds(message[:, 2 * channels : span], levels, channels)
        beyond = (
            message[:, channels : 2 * channels]
            + new_mixed[name]
            + factor * along_x * change
            - along_y * dsub(field[row, :] + change, small)
        )
        beyond = sub_average(beyond)
        ends = []
        for side, y in ((0, 0), (1, size_y - 1)):
            _, part, pair = corner[name, side]
            corner_x, corner_y = full_winds(pair, levels, channels)
            value = (
                part
                + new_mixed[name][y : y + 1]
                + factor * corner_x * change[y : y + 1]
                - corner_y * edge_slopes[name, side]
            )
            ends.append(0.5 * (value - beyond[y : y + 1]))
        beyond = edge_rows(beyond, ends[0], ends[1])
        total[row, :] = 0.5 * (total[row, :] + beyond)
    average_rows(total, size_x, size_y)
    phase = lax.broadcasted_iota(jnp.int32, (size_y, channels), 0) & 3
    weight = jnp.where(
        (phase == 0) | (phase == 3), float(QUADRATURE[0] / 4.0), float(QUADRATURE[1] / 4.0)
    )
    for element in range(size_x // NODES):
        value = None
        for i in range(NODES):
            term = float(QUADRATURE[i]) * total[pl.ds((NODES * element + i) * size_y, size_y), :]
            value = term if value is None else value + term
        reduced[pl.ds(element * size_y, size_y), :] = weight * value
    forcing[...] = select_rows(gather[...], reduced[...])
    ends = [
        [column_of(total, near + j, size_x, size_y) for j in range(NODES)]
        for near in (0, size_y - NODES)
    ]
    remixed = mix_all(jnp.concatenate([ends[0][0], ends[1][3]], axis=0), mix[...])
    for side, (y, kind) in enumerate(((0, 0), (size_y - 1, 3))):
        slope = None
        for j in range(NODES):
            term = DERIV[kind][j] * ends[side][j]
            slope = term if slope is None else slope + term
        along_x, along_y = full_winds(column_of(wind, y, size_x, size_y), levels, channels)
        column = ends[side][kind]
        work[side] = (
            column
            + remixed[side * size_x : (side + 1) * size_x]
            - (along_x * dsub(column, small) + along_y * slope)
        )


def home_kernel(size_x, size_y, groups, capacity, *refs):
    rank, edges, forcing, gather, spread, mix, cloud_mix, own = refs[:8]
    arrived = refs[8 : 7 + groups]
    out, to_a, to_b, sends, own_final = refs[7 + groups : 12 + groups]
    tendency, cloud, message = refs[12 + groups :]
    channels = forcing.shape[1]
    parts = 8 // capacity
    rows = own.shape[0]
    cloud[0:rows, :] = own[...]
    for k in range(1, groups):
        unpack(arrived[k - 1], channels, cloud, k * rows, rows)
    cloud_run(
        cloud, range(groups), forcing, cloud_mix, rows, parts, tendency, (0,)
    )
    own_final[...] = cloud[0:rows, :]
    tend = tendency[...]
    change = COUPLING * (tend + mix_all(tend, mix[...]))
    out[...] = select_rows(spread[...], change)
    occupied = jnp.max(gather[...].astype(jnp.float32), axis=1, keepdims=True)
    sends[:, 0:channels] = forcing[...]
    sends[:, channels : channels + 1] = occupied
    for side, y in ((0, 0), (1, size_y - 1)):
        own_change = jnp.concatenate(
            [
                jnp.broadcast_to(
                    out[(x // NODES) * size_y + y : (x // NODES) * size_y + y + 1, :],
                    (NODES, channels),
                )
                for x in range(0, size_x, NODES)
            ],
            axis=0,
        )
        message[side] = sub_average(edges[side] + own_change)
    even = is_even(rank)
    to_a[0:size_x, 0:channels] = jnp.where(even, message[1], message[0])
    to_b[0:size_x, 0:channels] = jnp.where(even, message[0], message[1])
    to_a[size_x : size_x + 8, :] = sends[8:16, :]
    to_b[size_x : size_x + 8, :] = sends[8 * groups - 8 : 8 * groups, :]


def fields_kernel(size_x, size_y, levels, second, wind, mix, change, out):
    local_update(second, second, mix[...], wind, out, size_x, size_y, levels, True, None, change)
    average_rows(out, size_x, size_y)


def last_turn_kernel(size_x, size_y, rank, place, partial, from_a, from_b, to_a, to_b, ends):
    channels = partial.shape[1]
    from_left, from_right = in_order(rank, from_a, from_b)
    for index, x in enumerate((0, size_x - 1)):
        value = partial[x * size_y : (x + 1) * size_y, :]
        ends[index] = edge_rows(
            value,
            0.5 * (from_left[x : x + 1, 0:channels] - value[0:1]),
            0.5 * (from_right[x : x + 1, 0:channels] - value[size_y - 1 : size_y]),
        )
    even = is_even(place)
    to_a[...] = jnp.where(even, ends[1], ends[0])
    to_b[...] = jnp.where(even, ends[0], ends[1])


def owner_kernel(size_x, size_y, groups, capacity, *refs):
    rank, partial, from_a, from_b, states, mix, own_final, sends = refs[:8]
    wide = refs[8 : 7 + groups]
    forcings = refs[7 + groups : 6 + 2 * groups]
    fields, out, field, cloud, forcing, turned, ready, done = refs[6 + 2 * groups :]
    channels = partial.shape[1]
    parts = 8 // capacity
    rows = own_final.shape[0]
    from_left, from_right = in_order(rank, from_a, from_b)
    left, right = side_changes(size_x, size_y, partial, from_left, from_right)
    for x in range(size_x):
        row = pl.ds(x * size_y, size_y)
        field[row, :] = edge_rows(partial[row, :], left[x : x + 1], right[x : x + 1])
    copies = [pltpu.make_async_copy(field, fields, done.at[groups])]
    copies[0].start()
    for k in range(1, groups):
        unpack(wide[k - 1], channels, cloud, (k - 1) * rows, rows)
        forcing[8 * (k - 1) : 8 * k, :] = forcings[k - 1][:, 0:channels]
    blocks = tuple(range(groups - 1))
    cloud_run(cloud, blocks, forcing, mix, rows, parts, None, blocks)
    for k in range(groups):
        start = pl.multiple_of((rank[0] ^ k) * rows, rows)
        source, at = (cloud, (k - 1) * rows) if k else (own_final, 0)
        flags = (forcings[k - 1] if k else sends)[0:8, channels : channels + 1]
        settle(source, at, flags, parts, turned.at[k], states, start, ready.at[k], 0, rows)
        copy = pltpu.make_async_copy(ready.at[k], out.at[pl.ds(start, rows), :], done.at[k])
        copy.start()
        copies.append(copy)
    for copy in copies:
        copy.wait()


def finish_kernel(size_x, size_y, place, fields_in, mine_a, mine_b, from_a, from_b,
                  fields, rows, done):
    even = is_even(place)
    last = size_x - 1
    copies = []
    for index, (mine, other, x) in enumerate(
        (
            (mine_a, from_a, jnp.where(even, last, 0)),
            (mine_b, from_b, jnp.where(even, 0, last)),
        )
    ):
        rows[index] = 0.5 * (mine[...] + other[...])
        start = pl.multiple_of(x * size_y, size_y)
        copy = pltpu.make_async_copy(
            rows.at[index], fields.at[pl.ds(start, size_y), :], done.at[index]
        )
        copy.start()
        copies.append(copy)
    for copy in copies:
        copy.wait()


VMEM_GRANT = 12 * 2**20
VMEM = pltpu.MemorySpace.VMEM
SMEM = pltpu.MemorySpace.SMEM
DMA = pltpu.SemaphoreType.DMA


def call(kernel, outs, scratch, *args, smem=(), far=(), far_out=(), aliases=None):
    def space(index, remote):
        if index in smem and not remote:
            return pl.BlockSpec(memory_space=SMEM)
        if index in (far_out if remote else far):
            return pl.BlockSpec(memory_space=pltpu.MemorySpace.HBM)
        return pl.BlockSpec(memory_space=VMEM)

    args = [
        pltpu.with_memory_space_constraint(arg, pltpu.MemorySpace.HBM) if index in far else arg
        for index, arg in enumerate(args)
    ]
    return pl.pallas_call(
        kernel,
        out_shape=[jax.ShapeDtypeStruct(shape, dtype) for shape, dtype in outs],
        in_specs=[space(index, False) for index in range(len(args))],
        out_specs=[space(index, True) for index in range(len(outs))],
        scratch_shapes=[
            item if not isinstance(item, tuple) else pltpu.VMEM(*item) for item in scratch
        ],
        input_output_aliases=aliases or {},
        compiler_params=pltpu.CompilerParams(vmem_limit_bytes=VMEM_GRANT),
    )(*args)


def lower_pairs(count):
    return [(i, i ^ 1) for i in range(count)]


def upper_pairs(count):
    return [(i, (i + 1) % count if i & 1 else (i - 1) % count) for i in range(count)]


def ring(to_a, to_b, axis):
    count = lax.axis_size(axis)
    from_b = lax.ppermute(to_b, axis, upper_pairs(count))
    from_a = lax.ppermute(to_a, axis, lower_pairs(count))
    return from_a, from_b


def on_device(state, wind, dyn_mix, owner, crm_state, crm_mix):
    f32 = jnp.float32
    size_x, size_y, channels = state.shape
    levels = wind.shape[2] // 2
    nodes = size_x * size_y
    groups = lax.axis_size("crm")
    slots, columns = crm_state.shape[:2]
    capacity = slots // groups
    rows = capacity * columns
    elements = size_x // NODES
    lane_count = len(lane_tiles(channels, 128))
    rank = lax.axis_index("crm").astype(jnp.int32).reshape(1)
    place = lax.axis_index("elem").astype(jnp.int32).reshape(1)
    state = state.reshape(nodes, channels)
    wind = wind.reshape(nodes, 2 * levels)
    clouds = crm_state.reshape(slots * columns, channels)
    owners = owner.reshape(owner.shape[0])
    grid = ((nodes, channels), f32)
    xor = [[(i, i ^ k) for i in range(groups)] for k in range(groups)]

    column_message = ((size_x, 2 * channels + 2 * levels + 128), f32)
    partial, to_a, to_b = call(
        functools.partial(begin_kernel, size_x, size_y, levels),
        [grid, column_message, column_message],
        [
            grid, ((nodes, 2 * levels), f32), (dyn_mix.shape, dyn_mix.dtype),
            ((2,) + column_message[0], f32), DMA((3,)),
        ],
        rank, state, wind, dyn_mix,
        smem=(0,), far=(1, 2, 3),
    )
    column_a, column_b = ring(to_a, to_b, "crm")

    length = packing(rows, channels)[2]
    own, *wide = call(
        functools.partial(widen_kernel, groups),
        [((rows, channels), f32)] + [((length, 128), f32)] * (groups - 1),
        [((groups, lane_count, rows, 128), f32)],
        rank, clouds,
        smem=(0,),
    )
    arrived = [lax.ppermute(wide[k - 1], "crm", xor[k]) for k in range(1, groups)]

    span = 2 * channels + 2 * levels
    row_message = ((size_y, span + 2 * levels), f32)
    to_a, to_b = call(
        functools.partial(turn_kernel, size_x, size_y, levels),
        [row_message, row_message],
        [((8, span), f32), ((2,) + row_message[0], f32)],
        rank, place, partial, state, wind, column_a, column_b,
        smem=(0, 1),
    )
    row_a, row_b = ring(to_a, to_b, "elem")
    field, known, total, sides, gather, spread = call(
        functools.partial(ready_kernel, size_x, size_y, levels, capacity),
        [
            grid, grid, grid, ((2, 4, size_x, channels), f32),
            ((8 * groups, elements * size_y), jnp.bfloat16),
            ((elements * size_y, 8 * groups), jnp.bfloat16),
        ],
        [],
        rank, owners, partial, state, wind, dyn_mix, column_a, column_b,
        smem=(0, 1),
    )
    second, edges, forcing = call(
        functools.partial(second_kernel, size_x, size_y, levels),
        [grid, ((2, size_x, channels), f32), ((8 * groups, channels), f32)],
        [((elements * size_y, channels), f32)],
        place, field, total, known, sides, gather, wind, dyn_mix, row_a, row_b,
        smem=(0,),
    )
    edge = ((size_x + 8, channels + 1), f32)
    change, to_a, to_b, sends, own_final = call(
        functools.partial(home_kernel, size_x, size_y, groups, capacity),
        [((elements * size_y, channels), f32), edge, edge, ((8 * groups, channels + 1), f32), ((rows, channels), f32)],
        [
            ((8 * groups, channels), f32),
            ((groups * rows, channels), f32),
            ((2, size_x, channels), f32),
        ],
        rank, edges, forcing, gather, spread, dyn_mix, crm_mix, own, *arrived,
        smem=(0,),
    )

    column_a, column_b = ring(to_a, to_b, "crm")
    rides = groups - 1 if all(i ^ j == groups - 1 for i, j in upper_pairs(groups)) else 0
    forcings = []
    for k in range(1, groups):
        if k == 1:
            forcings.append(column_a[size_x:])
        elif k == rides:
            forcings.append(column_b[size_x:])
        else:
            forcings.append(lax.ppermute(sends[8 * k : 8 * k + 8], "crm", xor[k]))
    (partial,) = call(
        functools.partial(fields_kernel, size_x, size_y, levels),
        [grid],
        [],
        second, wind, dyn_mix, change,
    )
    mine_a, mine_b = call(
        functools.partial(last_turn_kernel, size_x, size_y),
        [((size_y, channels), f32)] * 2,
        [((2, size_y, channels), f32)],
        rank, place, partial, column_a, column_b,
        smem=(0, 1),
    )
    row_a, row_b = ring(mine_a, mine_b, "elem")
    fields, crm_next = call(
        functools.partial(owner_kernel, size_x, size_y, groups, capacity),
        [grid, ((slots * columns, channels), clouds.dtype)],
        [
            grid,
            (((groups - 1) * rows, channels), f32),
            ((8 * (groups - 1), channels), f32),
            ((groups, lane_count, rows, 128), f32),
            ((groups, rows, channels), clouds.dtype),
            DMA((groups + 1,)),
        ],
        rank, partial, column_a, column_b, clouds, crm_mix, own_final, sends,
        *wide, *forcings,
        smem=(0,),
        far_out=(0, 1),
    )
    (third,) = call(
        functools.partial(finish_kernel, size_x, size_y),
        [grid],
        [((2, size_y, channels), f32), DMA((2,))],
        place, fields, mine_a, mine_b, row_a, row_b,
        smem=(0,), far=(1,), far_out=(0,), aliases={1: 0},
    )
    return (
        third.reshape(size_x, size_y, channels),
        crm_next.reshape(slots, columns, channels),
    )


def solution(mesh):
    return jax.shard_map(
        on_device,
        mesh=mesh,
        in_specs=(
            P("elem", "crm", None),
            P("elem", "crm", None),
            P(),
            P(("elem", "crm"), None),
            P(("elem", "crm"), None, None),
            P(),
        ),
        out_specs=(P("elem", "crm", None), P(("elem", "crm"), None, None)),
        check_vma=False,
    )
```

```python
import functools

import jax
import jax.numpy as jnp
import numpy as np
from jax import lax
from jax.experimental import pallas as pl
from jax.experimental.pallas import tpu as pltpu
from jax.sharding import PartitionSpec as P


SUB = 4
CRM_STEP = 0.5
DIFFUSION = 0.2
COUPLING = 0.5
NODES = 4


def gll_derivative():
    points = np.array([-1.0, -1.0 / np.sqrt(5.0), 1.0 / np.sqrt(5.0), 1.0])
    barycentric = np.array(
        [
            1.0 / np.prod([points[i] - points[j] for j in range(NODES) if j != i])
            for i in range(NODES)
        ]
    )
    derivative = np.zeros((NODES, NODES))
    for i in range(NODES):
        for j in range(NODES):
            if j != i:
                derivative[i, j] = barycentric[j] / barycentric[i] / (points[i] - points[j])
        derivative[i, i] = -np.sum(derivative[i])
    return derivative


DERIV = [[float(value) for value in row] for row in gll_derivative().astype(np.float32)]
FIRST, LAST = DERIV[0][0], DERIV[3][3]
QUADRATURE = np.array([1.0, 5.0, 5.0, 1.0]) / 6.0


def lane_tiles(channels, width):
    return [(at, min(at + width, channels)) for at in range(0, channels, width)]


def winds(pair, levels):
    along_x, along_y = pair[:, :levels], pair[:, levels:]
    return (
        jnp.concatenate([along_x, along_x], axis=1),
        jnp.concatenate([along_y, along_y], axis=1),
    )


def full_winds(pair, levels, channels):
    along_x, along_y = winds(pair, levels)
    count = -(-channels // (2 * levels))
    return (
        jnp.concatenate([along_x] * count, axis=1)[:, :channels],
        jnp.concatenate([along_y] * count, axis=1)[:, :channels],
    )


def dx_rows(rows):
    out = []
    for i in range(NODES):
        total = None
        for j in range(NODES):
            if abs(DERIV[i][j]) > 1e-6:
                term = DERIV[i][j] * rows[j]
                total = term if total is None else total + term
        out.append(total)
    return out


def sublane_coefficients(width):
    position = lax.broadcasted_iota(jnp.int32, (8, width), 0) & 3
    table = []
    for move in range(NODES):
        value = jnp.zeros((8, width), jnp.float32)
        for at in range(NODES):
            value = jnp.where(position == at, DERIV[at][(at + move) % NODES], value)
        table.append((value, position < NODES - move))
    return table


def dsub(field, table):
    width = field.shape[1]
    blocks = []
    for at in range(0, field.shape[0], 8):
        part = field[at : at + 8]
        total = table[0][0][:, :width] * part
        for move in range(1, NODES):
            moved = jnp.where(
                table[move][1][:, :width],
                pltpu.roll(part, 8 - move, 0),
                pltpu.roll(part, NODES - move, 0),
            )
            total = total + table[move][0][:, :width] * moved
        blocks.append(total)
    return blocks[0] if len(blocks) == 1 else jnp.concatenate(blocks, axis=0)


def sub_average(field):
    rows = field.shape[0]
    position = lax.broadcasted_iota(jnp.int32, field.shape, 0)
    phase = position & 3
    upper = (phase == 3) & (position < rows - 1)
    lower = (phase == 0) & (position > 0)
    ahead = pltpu.roll(field, rows - 1, 0)
    behind = pltpu.roll(field, 1, 0)
    partner = jnp.where(upper, ahead, jnp.where(lower, behind, field))
    return 0.5 * (field + partner)


def average_rows(ref, size_x, size_y):
    for at in range(NODES - 1, size_x - 1, NODES):
        low, high = pl.ds(at * size_y, size_y), pl.ds((at + 1) * size_y, size_y)
        mean = 0.5 * (ref[low, :] + ref[high, :])
        ref[low, :] = mean
        ref[high, :] = mean


def end_rows(rows, first, last):
    shape = (rows, first.shape[1])
    position = lax.broadcasted_iota(jnp.int32, shape, 0)
    return jnp.where(position == 0, first, jnp.where(position == rows - 1, last, 0.0))


def edge_rows(rows, first, last):
    position = lax.broadcasted_iota(jnp.int32, rows.shape, 0)
    count = rows.shape[0]
    return rows + jnp.where(
        position == 0, first, jnp.where(position == count - 1, last, 0.0)
    )


def strip_derivatives(size_y):
    matrix = np.asarray(DERIV, np.float64)
    both = np.concatenate(
        [np.kron(matrix, np.eye(size_y)), np.kron(np.eye(size_y), matrix)], axis=0
    )
    high = both.astype(jnp.bfloat16)
    low = (both - high.astype(np.float64)).astype(jnp.bfloat16)
    return jnp.asarray(np.concatenate([high, high, low], axis=1))


def strip_products(field_ref, mix, slopes_ref, size_x, size_y):
    strip = NODES * size_y
    products = []
    for element in range(size_x // NODES):
        field = field_ref[pl.ds(element * strip, strip), :]
        high = to_bf16(field)
        slopes = None
        if 2 * element >= size_x // NODES:
            low = to_bf16(field - high.astype(jnp.float32))
            slopes = jnp.dot(
                slopes_ref[...],
                jnp.concatenate([high, low, high], axis=0),
                preferred_element_type=jnp.float32,
            )
        products.append((jnp.dot(high, mix, preferred_element_type=jnp.float32), slopes))
    return products


def local_update(base_ref, field_ref, products, wind_ref, out_ref, size_y, levels,
                 mixed_ref=None, change_ref=None):
    channels = out_ref.shape[1]
    strip = NODES * size_y
    table = sublane_coefficients(2 * levels)
    for element, (mixed, slopes) in enumerate(products):
        if mixed_ref is not None:
            mixed_ref[pl.ds(element * strip, strip), :] = mixed
        rows = [pl.ds((NODES * element + i) * size_y, size_y) for i in range(NODES)]
        wind = [winds(wind_ref[row, :], levels) for row in rows]
        for begin, end in lane_tiles(channels, 2 * levels):
            if slopes is None:
                values = [field_ref[row, begin:end] for row in rows]
                along = dx_rows(values)
                across = [dsub(value, table) for value in values]
            else:
                along, across = (
                    [
                        slopes[at + i * size_y : at + (i + 1) * size_y, begin:end]
                        for i in range(NODES)
                    ]
                    for at in (0, strip)
                )
            for i in range(NODES):
                wind_x, wind_y = wind[i][0][:, : end - begin], wind[i][1][:, : end - begin]
                result = (
                    base_ref[rows[i], begin:end]
                    + mixed[i * size_y : (i + 1) * size_y, begin:end]
                    - (wind_x * along[i] + wind_y * across[i])
                )
                if change_ref is not None:
                    result = result + change_ref[pl.ds(element * size_y, size_y), begin:end]
                out_ref[rows[i], begin:end] = sub_average(result)


def to_bf16(value):
    return value.astype(jnp.bfloat16)


def mix_all(field, mix):
    return jnp.dot(to_bf16(field), mix, preferred_element_type=jnp.float32)


def column_of(ref, y, size_x, size_y):
    return jnp.concatenate(
        [ref[x * size_y + y : x * size_y + y + 1, :] for x in range(size_x)], axis=0
    )


def column_parts(message, channels, levels):
    span = 2 * channels + 2 * levels
    tiles = lane_tiles(channels, 128)
    slopes = [
        jnp.concatenate(
            [
                message[end * len(tiles) + p : end * len(tiles) + p + 1, span : span + last - first]
                for p, (first, last) in enumerate(tiles)
            ],
            axis=1,
        )
        for end in range(2)
    ]
    return (
        message[:, 0:channels],
        message[:, channels : 2 * channels],
        message[:, 2 * channels : span],
        slopes,
    )


def select_rows(chosen, values):
    high = to_bf16(values)
    rest = values - high.astype(jnp.float32)
    middle = to_bf16(rest)
    low = to_bf16(rest - middle.astype(jnp.float32))
    return jnp.dot(
        jnp.concatenate([chosen] * 3, axis=1),
        jnp.concatenate([high, middle, low], axis=0),
        preferred_element_type=jnp.float32,
    )


def is_even(rank):
    return (rank[0] & 1) == 0


def begin_kernel(size_x, size_y, levels, rank, state_in, wind_in, mix_in, slopes_in,
                 partial, to_a, to_b, state, wind, mix, slopes, message, arrivals):
    channels = state.shape[1]
    copies = [
        pltpu.make_async_copy(source, target, arrivals.at[index])
        for index, (source, target) in enumerate(
            ((state_in, state), (mix_in, mix), (slopes_in, slopes), (wind_in, wind))
        )
    ]
    for copy in copies:
        copy.start()
    for copy in copies:
        copy.wait()
    products = strip_products(state, mix[...], slopes, size_x, size_y)
    local_update(state, state, products, wind, partial, size_y, levels)
    average_rows(partial, size_x, size_y)
    to_left, to_right = message.at[0], message.at[1]
    for out, column, near, row in ((to_left, 0, 0, 0), (to_right, size_y - 1, size_y - NODES, 3)):
        values = [column_of(partial, near + j, size_x, size_y) for j in range(NODES)]
        slope = None
        for j in range(NODES):
            term = DERIV[row][j] * values[j]
            slope = term if slope is None else slope + term
        pair = column_of(wind, column, size_x, size_y)
        _, along_y = full_winds(pair, levels, channels)
        span = 2 * channels + 2 * levels
        out[:, 0:channels] = values[row]
        out[:, channels : 2 * channels] = (
            column_of(state, column, size_x, size_y) - along_y * slope
        )
        out[:, 2 * channels : span] = pair
        out[:, span : span + 128] = jnp.zeros((size_x, 128), jnp.float32)
        tiles = lane_tiles(channels, 128)
        for end, x in enumerate((0, size_x - 1)):
            for piece, (first, last) in enumerate(tiles):
                at = end * len(tiles) + piece
                out[at : at + 1, span : span + last - first] = slope[x : x + 1, first:last]
    even = is_even(rank)
    to_a[...] = jnp.where(even, message[1], message[0])
    to_b[...] = jnp.where(even, message[0], message[1])


def in_order(rank, from_a, from_b):
    even = is_even(rank)
    first, second = from_a[...], from_b[...]
    return jnp.where(even, second, first), jnp.where(even, first, second)


def side_changes(size_x, size_y, partial, from_left, from_right):
    channels = partial.shape[1]
    return (
        0.5 * (from_left[0:size_x, 0:channels] - column_of(partial, 0, size_x, size_y)),
        0.5 * (from_right[0:size_x, 0:channels] - column_of(partial, size_y - 1, size_x, size_y)),
    )


def turn_kernel(size_x, size_y, levels, rank, place, partial, state, wind, from_a, from_b,
                to_a, to_b, line, message):
    channels = state.shape[1]
    from_left, from_right = in_order(rank, from_a, from_b)
    to_up, to_down = message.at[0], message.at[1]
    left_value, left_part, left_wind, left_slopes = column_parts(from_left, channels, levels)
    right_value, right_part, right_wind, right_slopes = column_parts(
        from_right, channels, levels
    )
    span = 2 * channels + 2 * levels
    pieces = span // (2 * levels)
    for end, (out, x, near, kind) in enumerate(
        ((to_up, 0, 0, 0), (to_down, size_x - 1, size_x - NODES, 3))
    ):
        slope = None
        for j in range(NODES):
            value = partial[pl.ds((near + j) * size_y, size_y), :]
            at = near + j
            left = 0.5 * (left_value[at : at + 1] - value[0:1])
            right = 0.5 * (right_value[at : at + 1] - value[size_y - 1 : size_y])
            value = edge_rows(value, left, right)
            if at == x:
                out[:, 0:channels] = value
                changes = (left, right)
            term = DERIV[kind][j] * value
            slope = term if slope is None else slope + term
        row = pl.ds(x * size_y, size_y)
        along_x, _ = full_winds(wind[row, :], levels, channels)
        out[:, channels : 2 * channels] = state[row, :] - along_x * slope
        out[:, 2 * channels : span] = wind[row, :]
        corners = (
            (left_slopes[end], LAST * changes[0], left_part, left_wind, slope[0:1]),
            (
                right_slopes[end],
                FIRST * changes[1],
                right_part,
                right_wind,
                slope[size_y - 1 : size_y],
            ),
        )
        for side, (side_slope, fix, side_part, side_wind, corner_slope) in enumerate(corners):
            pair = side_wind[x : x + 1]
            corner_x, corner_y = full_winds(pair, levels, channels)
            line[side : side + 1, 0:channels] = side_slope - fix
            line[side : side + 1, channels : 2 * channels] = (
                side_part[x : x + 1] + corner_y * side_slope - corner_x * corner_slope
            )
            line[side : side + 1, 2 * channels : span] = pair
            for piece in range(pieces):
                at = side * pieces + piece
                out[at : at + 1, span : span + 2 * levels] = line[
                    side : side + 1, piece * 2 * levels : (piece + 1) * 2 * levels
                ]
        used = 2 * pieces
        if used < size_y:
            out[used:size_y, span : span + 2 * levels] = jnp.zeros(
                (size_y - used, 2 * levels), jnp.float32
            )
    even = is_even(place)
    to_a[...] = jnp.where(even, message[1], message[0])
    to_b[...] = jnp.where(even, message[0], message[1])


def ready_kernel(size_x, size_y, levels, capacity, rank, owner_in, cloud_mix_in, partial,
                 state, wind, mix, slopes, from_a, from_b,
                 field, mixed, total, sides, gather, spread, cloud_mix, owner, arrivals):
    channels = state.shape[1]
    from_left, from_right = in_order(rank, from_a, from_b)
    copies = [
        pltpu.make_async_copy(owner_in, owner, arrivals.at[0]),
        pltpu.make_async_copy(cloud_mix_in, cloud_mix, arrivals.at[1]),
    ]
    for copy in copies:
        copy.start()
    left, right = side_changes(size_x, size_y, partial, from_left, from_right)
    for x in range(size_x):
        row = pl.ds(x * size_y, size_y)
        field[row, :] = edge_rows(partial[row, :], left[x : x + 1], right[x : x + 1])
    products = strip_products(field, mix[...], slopes, size_x, size_y)
    local_update(state, field, products, wind, total, size_y, levels, mixed)
    table = sublane_coefficients(channels)
    for side, (message, y, change, factor) in enumerate(
        ((from_left, 0, left, LAST), (from_right, size_y - 1, right, FIRST))
    ):
        _, side_part, side_wind, ends = column_parts(message, channels, levels)
        along_x, along_y = full_winds(side_wind, levels, channels)
        sides[side, 0] = (
            side_part
            + column_of(mixed, y, size_x, size_y)
            - along_x * dsub(column_of(field, y, size_x, size_y), table)
            + factor * (along_y * change)
        )
        sides[side, 1] = end_rows(
            size_x,
            ends[0] - factor * change[0:1],
            ends[1] - factor * change[size_x - 1 : size_x],
        )
        sides[side, 2] = along_x
        sides[side, 3] = along_y
    copies[0].wait()
    parts = 8 // capacity
    for out, node_axis in ((gather, 1), (spread, 0)):
        columns = lax.broadcasted_iota(jnp.int32, out.shape, node_axis) >> 2
        named = jnp.zeros(out.shape, jnp.int32)
        for c in range(owner.shape[0]):
            named = jnp.where(columns == c, owner[c], named)
        position = jnp.zeros(out.shape, jnp.int32)
        for c in range(owner.shape[0]):
            position = position + jnp.where((columns > c) & (named == owner[c]), 1, 0)
        slot = ((rank[0] ^ named) * capacity + position) * parts
        rows = lax.broadcasted_iota(jnp.int32, out.shape, 1 - node_axis)
        count = parts if node_axis else 1
        out[...] = jnp.where((rows >= slot) & (rows < slot + count), 1.0, 0.0).astype(jnp.bfloat16)
    copies[1].wait()
    cloud_mix[...] = cloud_mix[...] * 0.5


def part_roll(value, parts, by):
    by = by % parts
    if by == 0:
        return value
    part = lax.broadcasted_iota(jnp.int32, value.shape, 0) & (parts - 1)
    return jnp.where(
        part < parts - by, pltpu.roll(value, 8 - by, 0), pltpu.roll(value, parts - by, 0)
    )


def part_sum(value, parts):
    total = value
    for by in range(1, parts):
        total = total + part_roll(value, parts, by)
    return total


def packing(rows, channels):
    full, rest = channels // 128, channels % 128
    assert rest in (0, 64)
    return full, rest, full * rows + (rows // 2 if rest else 0)


def pack(tile, channels, out, rows):
    full, rest, _ = packing(rows, channels)
    count = rows // 8
    for t in range(count):
        for lane in range(full):
            out[lane * rows + 8 * t : lane * rows + 8 * t + 8, :] = tile(t, lane)
    if rest:
        for t in range(count // 2):
            out[full * rows + 8 * t : full * rows + 8 * t + 8, :] = jnp.concatenate(
                [tile(t, full)[:, :rest], tile(t + count // 2, full)[:, :rest]], axis=1
            )


def unpack(message, channels, out, start, rows):
    full, rest, _ = packing(rows, channels)
    for lane in range(full):
        out[start : start + rows, lane * 128 : lane * 128 + 128] = message[
            lane * rows : (lane + 1) * rows, :
        ]
    if rest:
        half = rows // 2
        tail = message[full * rows : full * rows + half, :]
        out[start : start + half, full * 128 : channels] = tail[:, :rest]
        out[start + half : start + rows, full * 128 : channels] = tail[:, rest:]


def interleave(states, start, channels, turned, rows):
    for lane, (begin, end) in enumerate(lane_tiles(channels, 128)):
        value = states[pl.ds(start, rows), begin:end].astype(jnp.float32)
        turned[lane, 0:rows, 0 : end - begin] = value + value

    def tile(t, lane):
        return turned[lane, pl.ds(t, 8, stride=rows // 8), :]

    return tile


def widen_kernel(groups, rank, states, *refs):
    own, outs, turned = refs[0], refs[1:groups], refs[groups]
    rows, channels = own.shape
    for k in range(groups):
        start = pl.multiple_of((rank[0] ^ k) * rows, rows)
        tile = interleave(states, start, channels, turned.at[k], rows)
        if k:
            pack(tile, channels, outs[k - 1], rows)
        else:
            for t in range(rows // 8):
                for lane, (begin, end) in enumerate(lane_tiles(channels, 128)):
                    own[8 * t : 8 * t + 8, begin:end] = tile(t, lane)[:, : end - begin]


def cloud_run(states, blocks, forcing, mix, rows, parts, tendency, finals):
    count = rows // 8
    columns = count * parts
    half = mix[...]
    means, totals = {}, {}
    for step in range(SUB):
        last = step == SUB - 1
        for begin in range(0, len(blocks), 2):
            group = range(begin, min(begin + 2, len(blocks)))
            mixed = mix_all(states[begin * rows : (group[-1] + 1) * rows, :], half)
            for block in group:
                push = forcing[8 * blocks[block] : 8 * blocks[block] + 8, :]

                def read(t):
                    at = block * rows + 8 * t
                    return states[at : at + 8, :]

                if step == 0:
                    total = read(0)
                    for t in range(1, count):
                        total = total + read(t)
                    means[block] = part_sum(total, parts) * (0.5 / columns)
                gain = 2.0 * CRM_STEP * (push - means[block])
                keep = not last or block in finals
                total = None
                if keep:
                    start = read(0)
                    behind, here = part_roll(read(count - 1), parts, -1), start
                for t in range(count):
                    at = (block - begin) * rows + 8 * t
                    turn = jnp.tanh(mixed[at : at + 8])
                    total = turn if total is None else total + turn
                    if keep:
                        ahead = read(t + 1) if t + 1 < count else part_roll(start, parts, 1)
                        states[block * rows + 8 * t : block * rows + 8 * t + 8, :] = (
                            (1.0 - 2.0 * CRM_STEP * DIFFUSION) * here
                            + CRM_STEP * DIFFUSION * (behind + ahead)
                        ) + (turn + gain)
                        behind, here = here, ahead
                if tendency is not None or not last:
                    mean = (
                        means[block] + part_sum(total, parts) * (CRM_STEP / columns) + 0.5 * gain
                    )
                    means[block] = mean
                    if tendency is not None:
                        totals[block] = (
                            mean - push if step == 0 else totals[block] + (mean - push)
                        )
    if tendency is not None:
        for block in range(len(blocks)):
            tendency[8 * block : 8 * block + 8, :] = totals[block] * (1.0 / SUB)


def settle(states, start, used, parts, turned, old, old_start, out, out_start, rows):
    channels = states.shape[1]
    count = rows // 8
    for lane, (begin, end) in enumerate(lane_tiles(channels, 128)):
        width = end - begin
        for t in range(count):
            value = 0.5 * states[start + 8 * t : start + 8 * t + 8, begin:end]
            if width < 128:
                value = jnp.concatenate([value, jnp.zeros((8, 128 - width), jnp.float32)], axis=1)
            turned[lane, pl.ds(t, 8, stride=count), :] = value
        for slot in range(8 // parts):
            at = slot * count * parts
            span = count * parts
            flag = used[slot * parts : slot * parts + 1, :] > 0.5
            before = old[pl.ds(old_start + at, span), begin:end].astype(jnp.float32)
            after = turned[lane, at : at + span, 0:width]
            out[pl.ds(out_start + at, span), begin:end] = jnp.where(flag, after, before).astype(
                jnp.bfloat16
            )


def second_kernel(size_x, size_y, levels, place, field, total_in, known, sides, gather, wind, mix,
                  from_a, from_b, total, work, forcing, reduced):
    from_up, from_down = in_order(place, from_a, from_b)
    channels = field.shape[1]
    span = 2 * channels + 2 * levels
    pieces = span // (2 * levels)
    last_row = pl.ds((size_x - 1) * size_y, size_y)
    first_row = pl.ds(0, size_y)
    small = sublane_coefficients(channels)
    ups = 0.5 * (from_up[:, 0:channels] - field[first_row, :])
    downs = 0.5 * (from_down[:, 0:channels] - field[last_row, :])
    remixed = mix_all(
        jnp.concatenate([field[first_row, :] + ups, field[last_row, :] + downs], axis=0), mix[...]
    )
    new_mixed = (remixed[0:size_y], remixed[size_y : 2 * size_y])
    edge_mixed = []
    for index, (x, near, end, change) in enumerate(
        ((0, 0, 0, ups), (size_x - 1, size_x - NODES, 3, downs))
    ):
        edge = pl.ds(x * size_y, size_y)
        edge_mixed.append(new_mixed[index] - known[edge, :])
        for i in range(NODES):
            row = pl.ds((near + i) * size_y, size_y)
            along_x, along_y = full_winds(wind[row, :], levels, channels)
            value = -DERIV[i][end] * (along_x * change)
            if near + i == x:
                value = value + edge_mixed[index] - along_y * dsub(change, small)
            total[row, :] = total[row, :] + sub_average(value)
    corner = {}
    for name, message in enumerate((from_up, from_down)):
        for side in range(2):
            line = jnp.concatenate(
                [
                    message[side * pieces + p : side * pieces + p + 1, span : span + 2 * levels]
                    for p in range(pieces)
                ],
                axis=1,
            )
            corner[name, side] = (
                line[:, 0:channels],
                line[:, channels : 2 * channels],
                line[:, 2 * channels : span],
            )
    edge_slopes = {}
    for side, y in ((0, 0), (1, size_y - 1)):
        slope = sides[side, 1]
        pick = slice(y, y + 1)
        new_first = 0.5 * (corner[0, side][0] + slope[0:1])
        new_last = 0.5 * (corner[1, side][0] + slope[size_x - 1 : size_x])
        edge_slopes[0, side], edge_slopes[1, side] = new_first, new_last
        slope_change = end_rows(
            size_x, new_first - slope[0:1], new_last - slope[size_x - 1 : size_x]
        )
        column_change = end_rows(size_x, ups[pick], downs[pick])
        mixed_change = end_rows(size_x, edge_mixed[0][pick], edge_mixed[1][pick])
        beyond = (
            sides[side, 0]
            + mixed_change
            - (sides[side, 2] * dsub(column_change, small) + sides[side, 3] * slope_change)
        )
        for x in range(size_x):
            at = slice(x * size_y + y, x * size_y + y + 1)
            total[at, :] = 0.5 * (total[at, :] + beyond[x : x + 1])
    for name, message, row, change, factor in (
        (0, from_up, first_row, ups, LAST),
        (1, from_down, last_row, downs, FIRST),
    ):
        along_x, along_y = full_winds(message[:, 2 * channels : span], levels, channels)
        beyond = (
            message[:, channels : 2 * channels]
            + new_mixed[name]
            + factor * along_x * change
            - along_y * dsub(field[row, :] + change, small)
        )
        beyond = sub_average(beyond)
        ends = []
        for side, y in ((0, 0), (1, size_y - 1)):
            _, part, pair = corner[name, side]
            corner_x, corner_y = full_winds(pair, levels, channels)
            value = (
                part
                + new_mixed[name][y : y + 1]
                + factor * corner_x * change[y : y + 1]
                - corner_y * edge_slopes[name, side]
            )
            ends.append(0.5 * (value - beyond[y : y + 1]))
        beyond = edge_rows(beyond, ends[0], ends[1])
        total[row, :] = 0.5 * (total[row, :] + beyond)
    average_rows(total, size_x, size_y)
    phase = lax.broadcasted_iota(jnp.int32, (size_y, channels), 0) & 3
    weight = jnp.where(
        (phase == 0) | (phase == 3), float(QUADRATURE[0] / 4.0), float(QUADRATURE[1] / 4.0)
    )
    for element in range(size_x // NODES):
        value = None
        for i in range(NODES):
            term = float(QUADRATURE[i]) * total[pl.ds((NODES * element + i) * size_y, size_y), :]
            value = term if value is None else value + term
        reduced[pl.ds(element * size_y, size_y), :] = weight * value
    forcing[...] = select_rows(gather[...], reduced[...])
    ends = [
        [column_of(total, near + j, size_x, size_y) for j in range(NODES)]
        for near in (0, size_y - NODES)
    ]
    remixed = mix_all(jnp.concatenate([ends[0][0], ends[1][3]], axis=0), mix[...])
    for side, (y, kind) in enumerate(((0, 0), (size_y - 1, 3))):
        slope = None
        for j in range(NODES):
            term = DERIV[kind][j] * ends[side][j]
            slope = term if slope is None else slope + term
        along_x, along_y = full_winds(column_of(wind, y, size_x, size_y), levels, channels)
        column = ends[side][kind]
        work[side] = (
            column
            + remixed[side * size_x : (side + 1) * size_x]
            - (along_x * dsub(column, small) + along_y * slope)
        )


def home_kernel(size_x, size_y, groups, capacity, *refs):
    rank, edges, forcing, gather, spread, mix, cloud_mix, own = refs[:8]
    arrived = refs[8 : 7 + groups]
    out, to_a, to_b, sends, own_final = refs[7 + groups : 12 + groups]
    tendency, cloud, message = refs[12 + groups :]
    channels = forcing.shape[1]
    parts = 8 // capacity
    rows = own.shape[0]
    cloud[0:rows, :] = own[...]
    for k in range(1, groups):
        unpack(arrived[k - 1], channels, cloud, k * rows, rows)
    cloud_run(
        cloud, range(groups), forcing, cloud_mix, rows, parts, tendency, (0,)
    )
    own_final[...] = cloud[0:rows, :]
    tend = tendency[...]
    change = COUPLING * (tend + mix_all(tend, mix[...]))
    out[...] = select_rows(spread[...], change)
    occupied = jnp.max(gather[...].astype(jnp.float32), axis=1, keepdims=True)
    sends[:, 0:channels] = forcing[...]
    sends[:, channels : channels + 1] = occupied
    for side, y in ((0, 0), (1, size_y - 1)):
        own_change = jnp.concatenate(
            [
                jnp.broadcast_to(
                    out[(x // NODES) * size_y + y : (x // NODES) * size_y + y + 1, :],
                    (NODES, channels),
                )
                for x in range(0, size_x, NODES)
            ],
            axis=0,
        )
        message[side] = sub_average(edges[side] + own_change)
    even = is_even(rank)
    to_a[0:size_x, 0:channels] = jnp.where(even, message[1], message[0])
    to_b[0:size_x, 0:channels] = jnp.where(even, message[0], message[1])
    to_a[size_x : size_x + 8, :] = sends[8:16, :]
    to_b[size_x : size_x + 8, :] = sends[8 * groups - 8 : 8 * groups, :]


def fields_kernel(size_x, size_y, levels, second, wind, mix, slopes, change, out):
    products = strip_products(second, mix[...], slopes, size_x, size_y)
    local_update(second, second, products, wind, out, size_y, levels, None, change)
    average_rows(out, size_x, size_y)


def last_turn_kernel(size_x, size_y, rank, place, partial, from_a, from_b, to_a, to_b, ends):
    channels = partial.shape[1]
    from_left, from_right = in_order(rank, from_a, from_b)
    for index, x in enumerate((0, size_x - 1)):
        value = partial[x * size_y : (x + 1) * size_y, :]
        ends[index] = edge_rows(
            value,
            0.5 * (from_left[x : x + 1, 0:channels] - value[0:1]),
            0.5 * (from_right[x : x + 1, 0:channels] - value[size_y - 1 : size_y]),
        )
    even = is_even(place)
    to_a[...] = jnp.where(even, ends[1], ends[0])
    to_b[...] = jnp.where(even, ends[0], ends[1])


def owner_kernel(size_x, size_y, groups, capacity, *refs):
    rank, partial, from_a, from_b, states, mix, own_final, sends = refs[:8]
    wide = refs[8 : 7 + groups]
    forcings = refs[7 + groups : 6 + 2 * groups]
    fields, out, field, cloud, forcing, turned, ready, done = refs[6 + 2 * groups :]
    channels = partial.shape[1]
    parts = 8 // capacity
    rows = own_final.shape[0]
    from_left, from_right = in_order(rank, from_a, from_b)
    left, right = side_changes(size_x, size_y, partial, from_left, from_right)
    for x in range(size_x):
        row = pl.ds(x * size_y, size_y)
        field[row, :] = edge_rows(partial[row, :], left[x : x + 1], right[x : x + 1])
    copies = [pltpu.make_async_copy(field, fields, done.at[groups])]
    copies[0].start()
    for k in range(1, groups):
        unpack(wide[k - 1], channels, cloud, (k - 1) * rows, rows)
        forcing[8 * (k - 1) : 8 * k, :] = forcings[k - 1][:, 0:channels]
    blocks = tuple(range(groups - 1))
    cloud_run(cloud, blocks, forcing, mix, rows, parts, None, blocks)
    for k in range(groups):
        start = pl.multiple_of((rank[0] ^ k) * rows, rows)
        source, at = (cloud, (k - 1) * rows) if k else (own_final, 0)
        flags = (forcings[k - 1] if k else sends)[0:8, channels : channels + 1]
        settle(source, at, flags, parts, turned.at[k], states, start, ready.at[k], 0, rows)
        copy = pltpu.make_async_copy(ready.at[k], out.at[pl.ds(start, rows), :], done.at[k])
        copy.start()
        copies.append(copy)
    for copy in copies:
        copy.wait()


def finish_kernel(size_x, size_y, place, fields_in, mine_a, mine_b, from_a, from_b,
                  fields, rows, done):
    even = is_even(place)
    last = size_x - 1
    copies = []
    for index, (mine, other, x) in enumerate(
        (
            (mine_a, from_a, jnp.where(even, last, 0)),
            (mine_b, from_b, jnp.where(even, 0, last)),
        )
    ):
        rows[index] = 0.5 * (mine[...] + other[...])
        start = pl.multiple_of(x * size_y, size_y)
        copy = pltpu.make_async_copy(
            rows.at[index], fields.at[pl.ds(start, size_y), :], done.at[index]
        )
        copy.start()
        copies.append(copy)
    for copy in copies:
        copy.wait()


VMEM_GRANT = 12 * 2**20
VMEM = pltpu.MemorySpace.VMEM
SMEM = pltpu.MemorySpace.SMEM
DMA = pltpu.SemaphoreType.DMA


def call(kernel, outs, scratch, *args, smem=(), far=(), far_out=(), aliases=None):
    def space(index, remote):
        if index in smem and not remote:
            return pl.BlockSpec(memory_space=SMEM)
        if index in (far_out if remote else far):
            return pl.BlockSpec(memory_space=pltpu.MemorySpace.HBM)
        return pl.BlockSpec(memory_space=VMEM)

    args = [
        pltpu.with_memory_space_constraint(arg, pltpu.MemorySpace.HBM) if index in far else arg
        for index, arg in enumerate(args)
    ]
    return pl.pallas_call(
        kernel,
        out_shape=[jax.ShapeDtypeStruct(shape, dtype) for shape, dtype in outs],
        in_specs=[space(index, False) for index in range(len(args))],
        out_specs=[space(index, True) for index in range(len(outs))],
        scratch_shapes=[
            item if not isinstance(item, tuple) else pltpu.VMEM(*item) for item in scratch
        ],
        input_output_aliases=aliases or {},
        compiler_params=pltpu.CompilerParams(vmem_limit_bytes=VMEM_GRANT),
    )(*args)


def lower_pairs(count):
    return [(i, i ^ 1) for i in range(count)]


def upper_pairs(count):
    return [(i, (i + 1) % count if i & 1 else (i - 1) % count) for i in range(count)]


def ring(to_a, to_b, axis):
    count = lax.axis_size(axis)
    from_b = lax.ppermute(to_b, axis, upper_pairs(count))
    from_a = lax.ppermute(to_a, axis, lower_pairs(count))
    return from_a, from_b


def on_device(state, wind, dyn_mix, owner, crm_state, crm_mix):
    f32 = jnp.float32
    size_x, size_y, channels = state.shape
    levels = wind.shape[2] // 2
    nodes = size_x * size_y
    groups = lax.axis_size("crm")
    slots, columns = crm_state.shape[:2]
    capacity = slots // groups
    rows = capacity * columns
    elements = size_x // NODES
    lane_count = len(lane_tiles(channels, 128))
    rank = lax.axis_index("crm").astype(jnp.int32).reshape(1)
    place = lax.axis_index("elem").astype(jnp.int32).reshape(1)
    state = state.reshape(nodes, channels)
    wind = wind.reshape(nodes, 2 * levels)
    clouds = crm_state.reshape(slots * columns, channels)
    owners = owner.reshape(owner.shape[0])
    grid = ((nodes, channels), f32)
    xor = [[(i, i ^ k) for i in range(groups)] for k in range(groups)]

    column_message = ((size_x, 2 * channels + 2 * levels + 128), f32)
    slopes = strip_derivatives(size_y)
    partial, to_a, to_b, state, wind, dyn_mix, slopes = call(
        functools.partial(begin_kernel, size_x, size_y, levels),
        [
            grid, column_message, column_message, grid, ((nodes, 2 * levels), f32),
            (dyn_mix.shape, dyn_mix.dtype), (slopes.shape, slopes.dtype),
        ],
        [((2,) + column_message[0], f32), DMA((4,))],
        rank, state, wind, dyn_mix, slopes,
        smem=(0,), far=(1, 2, 3, 4),
    )
    column_a, column_b = ring(to_a, to_b, "crm")

    length = packing(rows, channels)[2]
    own, *wide = call(
        functools.partial(widen_kernel, groups),
        [((rows, channels), f32)] + [((length, 128), f32)] * (groups - 1),
        [((groups, lane_count, rows, 128), f32)],
        rank, clouds,
        smem=(0,),
    )
    arrived = [lax.ppermute(wide[k - 1], "crm", xor[k]) for k in range(1, groups)]

    span = 2 * channels + 2 * levels
    row_message = ((size_y, span + 2 * levels), f32)
    to_a, to_b = call(
        functools.partial(turn_kernel, size_x, size_y, levels),
        [row_message, row_message],
        [((8, span), f32), ((2,) + row_message[0], f32)],
        rank, place, partial, state, wind, column_a, column_b,
        smem=(0, 1),
    )
    row_a, row_b = ring(to_a, to_b, "elem")
    field, known, total, sides, gather, spread, crm_mix = call(
        functools.partial(ready_kernel, size_x, size_y, levels, capacity),
        [
            grid, grid, grid, ((2, 4, size_x, channels), f32),
            ((8 * groups, elements * size_y), jnp.bfloat16),
            ((elements * size_y, 8 * groups), jnp.bfloat16),
            (crm_mix.shape, crm_mix.dtype),
        ],
        [pltpu.SMEM(owners.shape, owners.dtype), DMA((2,))],
        rank, owners, crm_mix, partial, state, wind, dyn_mix, slopes, column_a, column_b,
        smem=(0,), far=(1, 2),
    )
    second, edges, forcing = call(
        functools.partial(second_kernel, size_x, size_y, levels),
        [grid, ((2, size_x, channels), f32), ((8 * groups, channels), f32)],
        [((elements * size_y, channels), f32)],
        place, field, total, known, sides, gather, wind, dyn_mix, row_a, row_b,
        smem=(0,), aliases={2: 0},
    )
    edge = ((size_x + 8, channels + 1), f32)
    change, to_a, to_b, sends, own_final = call(
        functools.partial(home_kernel, size_x, size_y, groups, capacity),
        [((elements * size_y, channels), f32), edge, edge, ((8 * groups, channels + 1), f32), ((rows, channels), f32)],
        [
            ((8 * groups, channels), f32),
            ((groups * rows, channels), f32),
            ((2, size_x, channels), f32),
        ],
        rank, edges, forcing, gather, spread, dyn_mix, crm_mix, own, *arrived,
        smem=(0,),
    )

    column_a, column_b = ring(to_a, to_b, "crm")
    rides = groups - 1 if all(i ^ j == groups - 1 for i, j in upper_pairs(groups)) else 0
    forcings = []
    for k in range(1, groups):
        if k == 1:
            forcings.append(column_a[size_x:])
        elif k == rides:
            forcings.append(column_b[size_x:])
        else:
            forcings.append(lax.ppermute(sends[8 * k : 8 * k + 8], "crm", xor[k]))
    (partial,) = call(
        functools.partial(fields_kernel, size_x, size_y, levels),
        [grid],
        [],
        second, wind, dyn_mix, slopes, change,
    )
    mine_a, mine_b = call(
        functools.partial(last_turn_kernel, size_x, size_y),
        [((size_y, channels), f32)] * 2,
        [((2, size_y, channels), f32)],
        rank, place, partial, column_a, column_b,
        smem=(0, 1),
    )
    row_a, row_b = ring(mine_a, mine_b, "elem")
    fields, crm_next = call(
        functools.partial(owner_kernel, size_x, size_y, groups, capacity),
        [grid, ((slots * columns, channels), clouds.dtype)],
        [
            grid,
            (((groups - 1) * rows, channels), f32),
            ((8 * (groups - 1), channels), f32),
            ((groups, lane_count, rows, 128), f32),
            ((groups, rows, channels), clouds.dtype),
            DMA((groups + 1,)),
        ],
        rank, partial, column_a, column_b, clouds, crm_mix, own_final, sends,
        *wide, *forcings,
        smem=(0,),
        far_out=(0, 1),
    )
    (third,) = call(
        functools.partial(finish_kernel, size_x, size_y),
        [grid],
        [((2, size_y, channels), f32), DMA((2,))],
        place, fields, mine_a, mine_b, row_a, row_b,
        smem=(0,), far=(1,), far_out=(0,), aliases={1: 0},
    )
    return (
        third.reshape(size_x, size_y, channels),
        crm_next.reshape(slots, columns, channels),
    )


def solution(mesh):
    return jax.shard_map(
        on_device,
        mesh=mesh,
        in_specs=(
            P("elem", "crm", None),
            P("elem", "crm", None),
            P(),
            P(("elem", "crm"), None),
            P(("elem", "crm"), None, None),
            P(),
        ),
        out_specs=(P("elem", "crm", None), P(("elem", "crm"), None, None)),
        check_vma=False,
    )
```

```python
import functools

import jax
import jax.numpy as jnp
import numpy as np
from jax import lax
from jax.experimental import pallas as pl
from jax.experimental.pallas import tpu as pltpu
from jax.sharding import PartitionSpec as P


SUB = 4
CRM_STEP = 0.5
DIFFUSION = 0.2
COUPLING = 0.5
NODES = 4


def gll_derivative():
    points = np.array([-1.0, -1.0 / np.sqrt(5.0), 1.0 / np.sqrt(5.0), 1.0])
    barycentric = np.array(
        [
            1.0 / np.prod([points[i] - points[j] for j in range(NODES) if j != i])
            for i in range(NODES)
        ]
    )
    derivative = np.zeros((NODES, NODES))
    for i in range(NODES):
        for j in range(NODES):
            if j != i:
                derivative[i, j] = barycentric[j] / barycentric[i] / (points[i] - points[j])
        derivative[i, i] = -np.sum(derivative[i])
    return derivative


DERIV = [[float(value) for value in row] for row in gll_derivative().astype(np.float32)]
FIRST, LAST = DERIV[0][0], DERIV[3][3]
QUADRATURE = np.array([1.0, 5.0, 5.0, 1.0]) / 6.0


def lane_tiles(channels, width):
    return [(at, min(at + width, channels)) for at in range(0, channels, width)]


def winds(pair, levels):
    along_x, along_y = pair[:, :levels], pair[:, levels:]
    return (
        jnp.concatenate([along_x, along_x], axis=1),
        jnp.concatenate([along_y, along_y], axis=1),
    )


def full_winds(pair, levels, channels):
    along_x, along_y = winds(pair, levels)
    count = -(-channels // (2 * levels))
    return (
        jnp.concatenate([along_x] * count, axis=1)[:, :channels],
        jnp.concatenate([along_y] * count, axis=1)[:, :channels],
    )


def dx_rows(rows):
    out = []
    for i in range(NODES):
        total = None
        for j in range(NODES):
            if abs(DERIV[i][j]) > 1e-6:
                term = DERIV[i][j] * rows[j]
                total = term if total is None else total + term
        out.append(total)
    return out


def sublane_coefficients(width):
    position = lax.broadcasted_iota(jnp.int32, (8, width), 0) & 3
    table = []
    for move in range(NODES):
        value = jnp.zeros((8, width), jnp.float32)
        for at in range(NODES):
            value = jnp.where(position == at, DERIV[at][(at + move) % NODES], value)
        table.append((value, position < NODES - move))
    return table


def dsub(field, table):
    width = field.shape[1]
    blocks = []
    for at in range(0, field.shape[0], 8):
        part = field[at : at + 8]
        total = table[0][0][:, :width] * part
        for move in range(1, NODES):
            moved = jnp.where(
                table[move][1][:, :width],
                pltpu.roll(part, 8 - move, 0),
                pltpu.roll(part, NODES - move, 0),
            )
            total = total + table[move][0][:, :width] * moved
        blocks.append(total)
    return blocks[0] if len(blocks) == 1 else jnp.concatenate(blocks, axis=0)


def sub_average(field):
    rows = field.shape[0]
    position = lax.broadcasted_iota(jnp.int32, field.shape, 0)
    phase = position & 3
    upper = (phase == 3) & (position < rows - 1)
    lower = (phase == 0) & (position > 0)
    ahead = pltpu.roll(field, rows - 1, 0)
    behind = pltpu.roll(field, 1, 0)
    partner = jnp.where(upper, ahead, jnp.where(lower, behind, field))
    return 0.5 * (field + partner)


def average_rows(ref, size_x, size_y):
    for at in range(NODES - 1, size_x - 1, NODES):
        low, high = pl.ds(at * size_y, size_y), pl.ds((at + 1) * size_y, size_y)
        mean = 0.5 * (ref[low, :] + ref[high, :])
        ref[low, :] = mean
        ref[high, :] = mean


def end_rows(rows, first, last):
    shape = (rows, first.shape[1])
    position = lax.broadcasted_iota(jnp.int32, shape, 0)
    return jnp.where(position == 0, first, jnp.where(position == rows - 1, last, 0.0))


def edge_rows(rows, first, last):
    position = lax.broadcasted_iota(jnp.int32, rows.shape, 0)
    count = rows.shape[0]
    return rows + jnp.where(
        position == 0, first, jnp.where(position == count - 1, last, 0.0)
    )


def strip_derivatives(size_y):
    matrix = np.asarray(DERIV, np.float64)
    both = np.concatenate(
        [np.kron(matrix, np.eye(size_y)), np.kron(np.eye(size_y), matrix)], axis=0
    )
    high = both.astype(jnp.bfloat16)
    low = (both - high.astype(np.float64)).astype(jnp.bfloat16)
    return jnp.asarray(np.concatenate([high, high, low], axis=1))


def strip_products(field_ref, mix, slopes_ref, size_x, size_y):
    strip = NODES * size_y
    products = []
    for element in range(size_x // NODES):
        field = field_ref[pl.ds(element * strip, strip), :]
        high = to_bf16(field)
        slopes = None
        if 2 * element >= size_x // NODES:
            low = to_bf16(field - high.astype(jnp.float32))
            slopes = jnp.dot(
                slopes_ref[...],
                jnp.concatenate([high, low, high], axis=0),
                preferred_element_type=jnp.float32,
            )
        products.append((jnp.dot(high, mix, preferred_element_type=jnp.float32), slopes))
    return products


def local_update(base_ref, field_ref, products, wind_ref, out_ref, size_y, levels,
                 mixed_ref=None):
    channels = out_ref.shape[1]
    strip = NODES * size_y
    table = sublane_coefficients(2 * levels)
    for element, (mixed, slopes) in enumerate(products):
        if mixed_ref is not None:
            mixed_ref[pl.ds(element * strip, strip), :] = mixed
        rows = [pl.ds((NODES * element + i) * size_y, size_y) for i in range(NODES)]
        wind = [winds(wind_ref[row, :], levels) for row in rows]
        for begin, end in lane_tiles(channels, 2 * levels):
            if slopes is None:
                values = [field_ref[row, begin:end] for row in rows]
                along = dx_rows(values)
                across = [dsub(value, table) for value in values]
            else:
                along, across = (
                    [
                        slopes[at + i * size_y : at + (i + 1) * size_y, begin:end]
                        for i in range(NODES)
                    ]
                    for at in (0, strip)
                )
            for i in range(NODES):
                wind_x, wind_y = wind[i][0][:, : end - begin], wind[i][1][:, : end - begin]
                result = (
                    base_ref[rows[i], begin:end]
                    + mixed[i * size_y : (i + 1) * size_y, begin:end]
                    - (wind_x * along[i] + wind_y * across[i])
                )
                out_ref[rows[i], begin:end] = sub_average(result)


def to_bf16(value):
    return value.astype(jnp.bfloat16)


def mix_all(field, mix):
    return jnp.dot(to_bf16(field), mix, preferred_element_type=jnp.float32)


def column_of(ref, y, size_x, size_y):
    return jnp.concatenate(
        [ref[x * size_y + y : x * size_y + y + 1, :] for x in range(size_x)], axis=0
    )


def column_parts(message, channels, levels):
    span = 2 * channels + 2 * levels
    tiles = lane_tiles(channels, 128)
    slopes = [
        jnp.concatenate(
            [
                message[end * len(tiles) + p : end * len(tiles) + p + 1, span : span + last - first]
                for p, (first, last) in enumerate(tiles)
            ],
            axis=1,
        )
        for end in range(2)
    ]
    return (
        message[:, 0:channels],
        message[:, channels : 2 * channels],
        message[:, 2 * channels : span],
        slopes,
    )


def select_rows(chosen, values):
    high = to_bf16(values)
    rest = values - high.astype(jnp.float32)
    middle = to_bf16(rest)
    low = to_bf16(rest - middle.astype(jnp.float32))
    return jnp.dot(
        jnp.concatenate([chosen] * 3, axis=1),
        jnp.concatenate([high, middle, low], axis=0),
        preferred_element_type=jnp.float32,
    )


def is_even(rank):
    return (rank[0] & 1) == 0


def begin_kernel(size_x, size_y, levels, rank, state_in, wind_in, mix_in, slopes_in,
                 partial, to_a, to_b, state, wind, mix, slopes, message, arrivals):
    channels = state.shape[1]
    copies = [
        pltpu.make_async_copy(source, target, arrivals.at[index])
        for index, (source, target) in enumerate(
            ((state_in, state), (mix_in, mix), (slopes_in, slopes), (wind_in, wind))
        )
    ]
    for copy in copies:
        copy.start()
    for copy in copies:
        copy.wait()
    products = strip_products(state, mix[...], slopes, size_x, size_y)
    local_update(state, state, products, wind, partial, size_y, levels)
    average_rows(partial, size_x, size_y)
    to_left, to_right = message.at[0], message.at[1]
    for out, column, near, row in ((to_left, 0, 0, 0), (to_right, size_y - 1, size_y - NODES, 3)):
        values = [column_of(partial, near + j, size_x, size_y) for j in range(NODES)]
        slope = None
        for j in range(NODES):
            term = DERIV[row][j] * values[j]
            slope = term if slope is None else slope + term
        pair = column_of(wind, column, size_x, size_y)
        _, along_y = full_winds(pair, levels, channels)
        span = 2 * channels + 2 * levels
        out[:, 0:channels] = values[row]
        out[:, channels : 2 * channels] = (
            column_of(state, column, size_x, size_y) - along_y * slope
        )
        out[:, 2 * channels : span] = pair
        out[:, span : span + 128] = jnp.zeros((size_x, 128), jnp.float32)
        tiles = lane_tiles(channels, 128)
        for end, x in enumerate((0, size_x - 1)):
            for piece, (first, last) in enumerate(tiles):
                at = end * len(tiles) + piece
                out[at : at + 1, span : span + last - first] = slope[x : x + 1, first:last]
    even = is_even(rank)
    to_a[...] = jnp.where(even, message[1], message[0])
    to_b[...] = jnp.where(even, message[0], message[1])


def in_order(rank, from_a, from_b):
    even = is_even(rank)
    first, second = from_a[...], from_b[...]
    return jnp.where(even, second, first), jnp.where(even, first, second)


def side_changes(size_x, size_y, partial, from_left, from_right):
    channels = partial.shape[1]
    return (
        0.5 * (from_left[0:size_x, 0:channels] - column_of(partial, 0, size_x, size_y)),
        0.5 * (from_right[0:size_x, 0:channels] - column_of(partial, size_y - 1, size_x, size_y)),
    )


def turn_kernel(size_x, size_y, levels, rank, place, partial, state, wind, from_a, from_b,
                to_a, to_b, line, message):
    channels = state.shape[1]
    from_left, from_right = in_order(rank, from_a, from_b)
    to_up, to_down = message.at[0], message.at[1]
    left_value, left_part, left_wind, left_slopes = column_parts(from_left, channels, levels)
    right_value, right_part, right_wind, right_slopes = column_parts(
        from_right, channels, levels
    )
    span = 2 * channels + 2 * levels
    pieces = span // (2 * levels)
    for end, (out, x, near, kind) in enumerate(
        ((to_up, 0, 0, 0), (to_down, size_x - 1, size_x - NODES, 3))
    ):
        slope = None
        for j in range(NODES):
            value = partial[pl.ds((near + j) * size_y, size_y), :]
            at = near + j
            left = 0.5 * (left_value[at : at + 1] - value[0:1])
            right = 0.5 * (right_value[at : at + 1] - value[size_y - 1 : size_y])
            value = edge_rows(value, left, right)
            if at == x:
                out[:, 0:channels] = value
                changes = (left, right)
            term = DERIV[kind][j] * value
            slope = term if slope is None else slope + term
        row = pl.ds(x * size_y, size_y)
        along_x, _ = full_winds(wind[row, :], levels, channels)
        out[:, channels : 2 * channels] = state[row, :] - along_x * slope
        out[:, 2 * channels : span] = wind[row, :]
        corners = (
            (left_slopes[end], LAST * changes[0], left_part, left_wind, slope[0:1]),
            (
                right_slopes[end],
                FIRST * changes[1],
                right_part,
                right_wind,
                slope[size_y - 1 : size_y],
            ),
        )
        for side, (side_slope, fix, side_part, side_wind, corner_slope) in enumerate(corners):
            pair = side_wind[x : x + 1]
            corner_x, corner_y = full_winds(pair, levels, channels)
            line[side : side + 1, 0:channels] = side_slope - fix
            line[side : side + 1, channels : 2 * channels] = (
                side_part[x : x + 1] + corner_y * side_slope - corner_x * corner_slope
            )
            line[side : side + 1, 2 * channels : span] = pair
            for piece in range(pieces):
                at = side * pieces + piece
                out[at : at + 1, span : span + 2 * levels] = line[
                    side : side + 1, piece * 2 * levels : (piece + 1) * 2 * levels
                ]
        used = 2 * pieces
        if used < size_y:
            out[used:size_y, span : span + 2 * levels] = jnp.zeros(
                (size_y - used, 2 * levels), jnp.float32
            )
    even = is_even(place)
    to_a[...] = jnp.where(even, message[1], message[0])
    to_b[...] = jnp.where(even, message[0], message[1])


def ready_kernel(size_x, size_y, levels, capacity, rank, owner_in, cloud_mix_in, partial,
                 state, wind, mix, slopes, from_a, from_b,
                 field, mixed, total, sides, gather, spread, cloud_mix, owner, arrivals):
    channels = state.shape[1]
    from_left, from_right = in_order(rank, from_a, from_b)
    copies = [
        pltpu.make_async_copy(owner_in, owner, arrivals.at[0]),
        pltpu.make_async_copy(cloud_mix_in, cloud_mix, arrivals.at[1]),
    ]
    for copy in copies:
        copy.start()
    left, right = side_changes(size_x, size_y, partial, from_left, from_right)
    for x in range(size_x):
        row = pl.ds(x * size_y, size_y)
        field[row, :] = edge_rows(partial[row, :], left[x : x + 1], right[x : x + 1])
    products = strip_products(field, mix[...], slopes, size_x, size_y)
    local_update(state, field, products, wind, total, size_y, levels, mixed)
    table = sublane_coefficients(channels)
    for side, (message, y, change, factor) in enumerate(
        ((from_left, 0, left, LAST), (from_right, size_y - 1, right, FIRST))
    ):
        _, side_part, side_wind, ends = column_parts(message, channels, levels)
        along_x, along_y = full_winds(side_wind, levels, channels)
        sides[side, 0] = (
            side_part
            + column_of(mixed, y, size_x, size_y)
            - along_x * dsub(column_of(field, y, size_x, size_y), table)
            + factor * (along_y * change)
        )
        sides[side, 1] = end_rows(
            size_x,
            ends[0] - factor * change[0:1],
            ends[1] - factor * change[size_x - 1 : size_x],
        )
        sides[side, 2] = along_x
        sides[side, 3] = along_y
    copies[0].wait()
    parts = 8 // capacity
    for out, node_axis in ((gather, 1), (spread, 0)):
        columns = lax.broadcasted_iota(jnp.int32, out.shape, node_axis) >> 2
        named = jnp.zeros(out.shape, jnp.int32)
        for c in range(owner.shape[0]):
            named = jnp.where(columns == c, owner[c], named)
        position = jnp.zeros(out.shape, jnp.int32)
        for c in range(owner.shape[0]):
            position = position + jnp.where((columns > c) & (named == owner[c]), 1, 0)
        slot = ((rank[0] ^ named) * capacity + position) * parts
        rows = lax.broadcasted_iota(jnp.int32, out.shape, 1 - node_axis)
        count = parts if node_axis else 1
        out[...] = jnp.where((rows >= slot) & (rows < slot + count), 1.0, 0.0).astype(jnp.bfloat16)
    copies[1].wait()
    cloud_mix[...] = cloud_mix[...] * 0.5


def part_roll(value, parts, by):
    by = by % parts
    if by == 0:
        return value
    part = lax.broadcasted_iota(jnp.int32, value.shape, 0) & (parts - 1)
    return jnp.where(
        part < parts - by, pltpu.roll(value, 8 - by, 0), pltpu.roll(value, parts - by, 0)
    )


def part_sum(value, parts):
    total = value
    for by in range(1, parts):
        total = total + part_roll(value, parts, by)
    return total


def packing(rows, channels):
    full, rest = channels // 128, channels % 128
    assert rest in (0, 64)
    return full, rest, full * rows + (rows // 2 if rest else 0)


def pack(tile, channels, out, rows):
    full, rest, _ = packing(rows, channels)
    count = rows // 8
    for t in range(count):
        for lane in range(full):
            out[lane * rows + 8 * t : lane * rows + 8 * t + 8, :] = tile(t, lane)
    if rest:
        for t in range(count // 2):
            out[full * rows + 8 * t : full * rows + 8 * t + 8, :] = jnp.concatenate(
                [tile(t, full)[:, :rest], tile(t + count // 2, full)[:, :rest]], axis=1
            )


def unpack(message, channels, out, start, rows):
    full, rest, _ = packing(rows, channels)
    for lane in range(full):
        out[start : start + rows, lane * 128 : lane * 128 + 128] = message[
            lane * rows : (lane + 1) * rows, :
        ]
    if rest:
        half = rows // 2
        tail = message[full * rows : full * rows + half, :]
        out[start : start + half, full * 128 : channels] = tail[:, :rest]
        out[start + half : start + rows, full * 128 : channels] = tail[:, rest:]


def interleave(states, start, channels, turned, rows):
    for lane, (begin, end) in enumerate(lane_tiles(channels, 128)):
        value = states[pl.ds(start, rows), begin:end].astype(jnp.float32)
        turned[lane, 0:rows, 0 : end - begin] = value + value

    def tile(t, lane):
        return turned[lane, pl.ds(t, 8, stride=rows // 8), :]

    return tile


def widen_kernel(groups, rank, states, *refs):
    own, outs, turned = refs[0], refs[1:groups], refs[groups]
    rows, channels = own.shape
    for k in range(groups):
        start = pl.multiple_of((rank[0] ^ k) * rows, rows)
        tile = interleave(states, start, channels, turned.at[k], rows)
        if k:
            pack(tile, channels, outs[k - 1], rows)
        else:
            for t in range(rows // 8):
                for lane, (begin, end) in enumerate(lane_tiles(channels, 128)):
                    own[8 * t : 8 * t + 8, begin:end] = tile(t, lane)[:, : end - begin]


def cloud_run(states, blocks, forcing, mix, rows, parts, tendency, finals):
    count = rows // 8
    columns = count * parts
    half = mix[...]
    means, totals = {}, {}
    for step in range(SUB):
        last = step == SUB - 1
        for begin in range(0, len(blocks), 2):
            group = range(begin, min(begin + 2, len(blocks)))
            mixed = mix_all(states[begin * rows : (group[-1] + 1) * rows, :], half)
            for block in group:
                push = forcing[8 * blocks[block] : 8 * blocks[block] + 8, :]

                def read(t):
                    at = block * rows + 8 * t
                    return states[at : at + 8, :]

                if step == 0:
                    total = read(0)
                    for t in range(1, count):
                        total = total + read(t)
                    means[block] = part_sum(total, parts) * (0.5 / columns)
                gain = 2.0 * CRM_STEP * (push - means[block])
                keep = not last or block in finals
                total = None
                if keep:
                    start = read(0)
                    behind, here = part_roll(read(count - 1), parts, -1), start
                for t in range(count):
                    at = (block - begin) * rows + 8 * t
                    turn = jnp.tanh(mixed[at : at + 8])
                    total = turn if total is None else total + turn
                    if keep:
                        ahead = read(t + 1) if t + 1 < count else part_roll(start, parts, 1)
                        states[block * rows + 8 * t : block * rows + 8 * t + 8, :] = (
                            (1.0 - 2.0 * CRM_STEP * DIFFUSION) * here
                            + CRM_STEP * DIFFUSION * (behind + ahead)
                        ) + (turn + gain)
                        behind, here = here, ahead
                if tendency is not None or not last:
                    mean = (
                        means[block] + part_sum(total, parts) * (CRM_STEP / columns) + 0.5 * gain
                    )
                    means[block] = mean
                    if tendency is not None:
                        totals[block] = (
                            mean - push if step == 0 else totals[block] + (mean - push)
                        )
    if tendency is not None:
        for block in range(len(blocks)):
            tendency[8 * block : 8 * block + 8, :] = totals[block] * (1.0 / SUB)


def settle(states, start, used, parts, turned, old, old_start, out, out_start, rows):
    channels = states.shape[1]
    count = rows // 8
    for lane, (begin, end) in enumerate(lane_tiles(channels, 128)):
        width = end - begin
        for t in range(count):
            value = 0.5 * states[start + 8 * t : start + 8 * t + 8, begin:end]
            if width < 128:
                value = jnp.concatenate([value, jnp.zeros((8, 128 - width), jnp.float32)], axis=1)
            turned[lane, pl.ds(t, 8, stride=count), :] = value
        for slot in range(8 // parts):
            at = slot * count * parts
            span = count * parts
            flag = used[slot * parts : slot * parts + 1, :] > 0.5
            before = old[pl.ds(old_start + at, span), begin:end].astype(jnp.float32)
            after = turned[lane, at : at + span, 0:width]
            out[pl.ds(out_start + at, span), begin:end] = jnp.where(flag, after, before).astype(
                jnp.bfloat16
            )


def second_kernel(size_x, size_y, levels, place, field, total_in, known, sides, gather, wind, mix,
                  from_a, from_b, total, work, forcing, reduced):
    from_up, from_down = in_order(place, from_a, from_b)
    channels = field.shape[1]
    span = 2 * channels + 2 * levels
    pieces = span // (2 * levels)
    last_row = pl.ds((size_x - 1) * size_y, size_y)
    first_row = pl.ds(0, size_y)
    small = sublane_coefficients(channels)
    ups = 0.5 * (from_up[:, 0:channels] - field[first_row, :])
    downs = 0.5 * (from_down[:, 0:channels] - field[last_row, :])
    remixed = mix_all(
        jnp.concatenate([field[first_row, :] + ups, field[last_row, :] + downs], axis=0), mix[...]
    )
    new_mixed = (remixed[0:size_y], remixed[size_y : 2 * size_y])
    edge_mixed = []
    for index, (x, near, end, change) in enumerate(
        ((0, 0, 0, ups), (size_x - 1, size_x - NODES, 3, downs))
    ):
        edge = pl.ds(x * size_y, size_y)
        edge_mixed.append(new_mixed[index] - known[edge, :])
        for i in range(NODES):
            row = pl.ds((near + i) * size_y, size_y)
            along_x, along_y = full_winds(wind[row, :], levels, channels)
            value = -DERIV[i][end] * (along_x * change)
            if near + i == x:
                value = value + edge_mixed[index] - along_y * dsub(change, small)
            total[row, :] = total[row, :] + sub_average(value)
    corner = {}
    for name, message in enumerate((from_up, from_down)):
        for side in range(2):
            line = jnp.concatenate(
                [
                    message[side * pieces + p : side * pieces + p + 1, span : span + 2 * levels]
                    for p in range(pieces)
                ],
                axis=1,
            )
            corner[name, side] = (
                line[:, 0:channels],
                line[:, channels : 2 * channels],
                line[:, 2 * channels : span],
            )
    edge_slopes = {}
    for side, y in ((0, 0), (1, size_y - 1)):
        slope = sides[side, 1]
        pick = slice(y, y + 1)
        new_first = 0.5 * (corner[0, side][0] + slope[0:1])
        new_last = 0.5 * (corner[1, side][0] + slope[size_x - 1 : size_x])
        edge_slopes[0, side], edge_slopes[1, side] = new_first, new_last
        slope_change = end_rows(
            size_x, new_first - slope[0:1], new_last - slope[size_x - 1 : size_x]
        )
        column_change = end_rows(size_x, ups[pick], downs[pick])
        mixed_change = end_rows(size_x, edge_mixed[0][pick], edge_mixed[1][pick])
        beyond = (
            sides[side, 0]
            + mixed_change
            - (sides[side, 2] * dsub(column_change, small) + sides[side, 3] * slope_change)
        )
        for x in range(size_x):
            at = slice(x * size_y + y, x * size_y + y + 1)
            total[at, :] = 0.5 * (total[at, :] + beyond[x : x + 1])
    for name, message, row, change, factor in (
        (0, from_up, first_row, ups, LAST),
        (1, from_down, last_row, downs, FIRST),
    ):
        along_x, along_y = full_winds(message[:, 2 * channels : span], levels, channels)
        beyond = (
            message[:, channels : 2 * channels]
            + new_mixed[name]
            + factor * along_x * change
            - along_y * dsub(field[row, :] + change, small)
        )
        beyond = sub_average(beyond)
        ends = []
        for side, y in ((0, 0), (1, size_y - 1)):
            _, part, pair = corner[name, side]
            corner_x, corner_y = full_winds(pair, levels, channels)
            value = (
                part
                + new_mixed[name][y : y + 1]
                + factor * corner_x * change[y : y + 1]
                - corner_y * edge_slopes[name, side]
            )
            ends.append(0.5 * (value - beyond[y : y + 1]))
        beyond = edge_rows(beyond, ends[0], ends[1])
        total[row, :] = 0.5 * (total[row, :] + beyond)
    average_rows(total, size_x, size_y)
    phase = lax.broadcasted_iota(jnp.int32, (size_y, channels), 0) & 3
    weight = jnp.where(
        (phase == 0) | (phase == 3), float(QUADRATURE[0] / 4.0), float(QUADRATURE[1] / 4.0)
    )
    for element in range(size_x // NODES):
        value = None
        for i in range(NODES):
            term = float(QUADRATURE[i]) * total[pl.ds((NODES * element + i) * size_y, size_y), :]
            value = term if value is None else value + term
        reduced[pl.ds(element * size_y, size_y), :] = weight * value
    forcing[...] = select_rows(gather[...], reduced[...])
    for side, (y, near, kind) in enumerate(((0, 0, 0), (size_y - 1, size_y - NODES, 3))):
        values = [column_of(total, near + j, size_x, size_y) for j in range(NODES)]
        slope = None
        for j in range(NODES):
            term = DERIV[kind][j] * values[j]
            slope = term if slope is None else slope + term
        along_x, along_y = full_winds(column_of(wind, y, size_x, size_y), levels, channels)
        work[side, 0] = values[kind]
        work[side, 1] = along_x * dsub(values[kind], small) + along_y * slope


def home_kernel(size_x, size_y, groups, capacity, *refs):
    rank, edges, forcing, gather, spread, mix, cloud_mix, own = refs[:8]
    arrived = refs[8 : 7 + groups]
    out, to_a, to_b, sends, own_final = refs[7 + groups : 12 + groups]
    tendency, cloud, message = refs[12 + groups :]
    channels = forcing.shape[1]
    parts = 8 // capacity
    rows = own.shape[0]
    cloud[0:rows, :] = own[...]
    for k in range(1, groups):
        unpack(arrived[k - 1], channels, cloud, k * rows, rows)
    cloud_run(
        cloud, range(groups), forcing, cloud_mix, rows, parts, tendency, (0,)
    )
    own_final[...] = cloud[0:rows, :]
    tend = tendency[...]
    out[...] = select_rows(spread[...], COUPLING * tend)
    occupied = jnp.max(gather[...].astype(jnp.float32), axis=1, keepdims=True)
    sends[:, 0:channels] = forcing[...]
    sends[:, channels : channels + 1] = occupied
    coupled = []
    for side, y in ((0, 0), (1, size_y - 1)):
        half = [
            jnp.broadcast_to(
                out[(x // NODES) * size_y + y : (x // NODES) * size_y + y + 1, :],
                (NODES, channels),
            )
            for x in range(0, size_x, NODES)
        ]
        coupled.append(edges[side, 0] + jnp.concatenate(half, axis=0))
    mixed = mix_all(jnp.concatenate(coupled, axis=0), mix[...])
    for side in range(2):
        message[side] = sub_average(
            coupled[side] + mixed[side * size_x : (side + 1) * size_x] - edges[side, 1]
        )
    even = is_even(rank)
    to_a[0:size_x, 0:channels] = jnp.where(even, message[1], message[0])
    to_b[0:size_x, 0:channels] = jnp.where(even, message[0], message[1])
    to_a[size_x : size_x + 8, :] = sends[8:16, :]
    to_b[size_x : size_x + 8, :] = sends[8 * groups - 8 : 8 * groups, :]


def fields_kernel(size_x, size_y, levels, second, wind, mix, slopes, half, out, coupled):
    for x in range(size_x):
        row = pl.ds(x * size_y, size_y)
        coupled[row, :] = second[row, :] + half[pl.ds(x // NODES * size_y, size_y), :]
    products = strip_products(coupled, mix[...], slopes, size_x, size_y)
    local_update(coupled, coupled, products, wind, out, size_y, levels)
    average_rows(out, size_x, size_y)


def last_turn_kernel(size_x, size_y, rank, place, partial, from_a, from_b, to_a, to_b, ends):
    channels = partial.shape[1]
    from_left, from_right = in_order(rank, from_a, from_b)
    for index, x in enumerate((0, size_x - 1)):
        value = partial[x * size_y : (x + 1) * size_y, :]
        ends[index] = edge_rows(
            value,
            0.5 * (from_left[x : x + 1, 0:channels] - value[0:1]),
            0.5 * (from_right[x : x + 1, 0:channels] - value[size_y - 1 : size_y]),
        )
    even = is_even(place)
    to_a[...] = jnp.where(even, ends[1], ends[0])
    to_b[...] = jnp.where(even, ends[0], ends[1])


def owner_kernel(size_x, size_y, groups, capacity, *refs):
    rank, partial, from_a, from_b, states, mix, own_final, sends = refs[:8]
    wide = refs[8 : 7 + groups]
    forcings = refs[7 + groups : 6 + 2 * groups]
    fields, out, field, cloud, forcing, turned, ready, done = refs[6 + 2 * groups :]
    channels = partial.shape[1]
    parts = 8 // capacity
    rows = own_final.shape[0]
    from_left, from_right = in_order(rank, from_a, from_b)
    left, right = side_changes(size_x, size_y, partial, from_left, from_right)
    for x in range(size_x):
        row = pl.ds(x * size_y, size_y)
        field[row, :] = edge_rows(partial[row, :], left[x : x + 1], right[x : x + 1])
    copies = [pltpu.make_async_copy(field, fields, done.at[groups])]
    copies[0].start()
    for k in range(1, groups):
        unpack(wide[k - 1], channels, cloud, (k - 1) * rows, rows)
        forcing[8 * (k - 1) : 8 * k, :] = forcings[k - 1][:, 0:channels]
    blocks = tuple(range(groups - 1))
    cloud_run(cloud, blocks, forcing, mix, rows, parts, None, blocks)
    for k in range(groups):
        start = pl.multiple_of((rank[0] ^ k) * rows, rows)
        source, at = (cloud, (k - 1) * rows) if k else (own_final, 0)
        flags = (forcings[k - 1] if k else sends)[0:8, channels : channels + 1]
        settle(source, at, flags, parts, turned.at[k], states, start, ready.at[k], 0, rows)
        copy = pltpu.make_async_copy(ready.at[k], out.at[pl.ds(start, rows), :], done.at[k])
        copy.start()
        copies.append(copy)
    for copy in copies:
        copy.wait()


def finish_kernel(size_x, size_y, place, fields_in, mine_a, mine_b, from_a, from_b,
                  fields, rows, done):
    even = is_even(place)
    last = size_x - 1
    copies = []
    for index, (mine, other, x) in enumerate(
        (
            (mine_a, from_a, jnp.where(even, last, 0)),
            (mine_b, from_b, jnp.where(even, 0, last)),
        )
    ):
        rows[index] = 0.5 * (mine[...] + other[...])
        start = pl.multiple_of(x * size_y, size_y)
        copy = pltpu.make_async_copy(
            rows.at[index], fields.at[pl.ds(start, size_y), :], done.at[index]
        )
        copy.start()
        copies.append(copy)
    for copy in copies:
        copy.wait()


VMEM_GRANT = 12 * 2**20
VMEM = pltpu.MemorySpace.VMEM
SMEM = pltpu.MemorySpace.SMEM
DMA = pltpu.SemaphoreType.DMA


def call(kernel, outs, scratch, *args, smem=(), far=(), far_out=(), aliases=None):
    def space(index, remote):
        if index in smem and not remote:
            return pl.BlockSpec(memory_space=SMEM)
        if index in (far_out if remote else far):
            return pl.BlockSpec(memory_space=pltpu.MemorySpace.HBM)
        return pl.BlockSpec(memory_space=VMEM)

    args = [
        pltpu.with_memory_space_constraint(arg, pltpu.MemorySpace.HBM) if index in far else arg
        for index, arg in enumerate(args)
    ]
    return pl.pallas_call(
        kernel,
        out_shape=[jax.ShapeDtypeStruct(shape, dtype) for shape, dtype in outs],
        in_specs=[space(index, False) for index in range(len(args))],
        out_specs=[space(index, True) for index in range(len(outs))],
        scratch_shapes=[
            item if not isinstance(item, tuple) else pltpu.VMEM(*item) for item in scratch
        ],
        input_output_aliases=aliases or {},
        compiler_params=pltpu.CompilerParams(vmem_limit_bytes=VMEM_GRANT),
    )(*args)


def lower_pairs(count):
    return [(i, i ^ 1) for i in range(count)]


def upper_pairs(count):
    return [(i, (i + 1) % count if i & 1 else (i - 1) % count) for i in range(count)]


def ring(to_a, to_b, axis):
    count = lax.axis_size(axis)
    from_b = lax.ppermute(to_b, axis, upper_pairs(count))
    from_a = lax.ppermute(to_a, axis, lower_pairs(count))
    return from_a, from_b


def on_device(state, wind, dyn_mix, owner, crm_state, crm_mix):
    f32 = jnp.float32
    size_x, size_y, channels = state.shape
    levels = wind.shape[2] // 2
    nodes = size_x * size_y
    groups = lax.axis_size("crm")
    slots, columns = crm_state.shape[:2]
    capacity = slots // groups
    rows = capacity * columns
    elements = size_x // NODES
    lane_count = len(lane_tiles(channels, 128))
    rank = lax.axis_index("crm").astype(jnp.int32).reshape(1)
    place = lax.axis_index("elem").astype(jnp.int32).reshape(1)
    state = state.reshape(nodes, channels)
    wind = wind.reshape(nodes, 2 * levels)
    clouds = crm_state.reshape(slots * columns, channels)
    owners = owner.reshape(owner.shape[0])
    grid = ((nodes, channels), f32)
    xor = [[(i, i ^ k) for i in range(groups)] for k in range(groups)]

    column_message = ((size_x, 2 * channels + 2 * levels + 128), f32)
    slopes = strip_derivatives(size_y)
    partial, to_a, to_b, state, wind, dyn_mix, slopes = call(
        functools.partial(begin_kernel, size_x, size_y, levels),
        [
            grid, column_message, column_message, grid, ((nodes, 2 * levels), f32),
            (dyn_mix.shape, dyn_mix.dtype), (slopes.shape, slopes.dtype),
        ],
        [((2,) + column_message[0], f32), DMA((4,))],
        rank, state, wind, dyn_mix, slopes,
        smem=(0,), far=(1, 2, 3, 4),
    )
    column_a, column_b = ring(to_a, to_b, "crm")

    length = packing(rows, channels)[2]
    own, *wide = call(
        functools.partial(widen_kernel, groups),
        [((rows, channels), f32)] + [((length, 128), f32)] * (groups - 1),
        [((groups, lane_count, rows, 128), f32)],
        rank, clouds,
        smem=(0,),
    )
    arrived = [lax.ppermute(wide[k - 1], "crm", xor[k]) for k in range(1, groups)]

    span = 2 * channels + 2 * levels
    row_message = ((size_y, span + 2 * levels), f32)
    to_a, to_b = call(
        functools.partial(turn_kernel, size_x, size_y, levels),
        [row_message, row_message],
        [((8, span), f32), ((2,) + row_message[0], f32)],
        rank, place, partial, state, wind, column_a, column_b,
        smem=(0, 1),
    )
    row_a, row_b = ring(to_a, to_b, "elem")
    field, known, total, sides, gather, spread, crm_mix = call(
        functools.partial(ready_kernel, size_x, size_y, levels, capacity),
        [
            grid, grid, grid, ((2, 4, size_x, channels), f32),
            ((8 * groups, elements * size_y), jnp.bfloat16),
            ((elements * size_y, 8 * groups), jnp.bfloat16),
            (crm_mix.shape, crm_mix.dtype),
        ],
        [pltpu.SMEM(owners.shape, owners.dtype), DMA((2,))],
        rank, owners, crm_mix, partial, state, wind, dyn_mix, slopes, column_a, column_b,
        smem=(0,), far=(1, 2),
    )
    second, edges, forcing = call(
        functools.partial(second_kernel, size_x, size_y, levels),
        [grid, ((2, 2, size_x, channels), f32), ((8 * groups, channels), f32)],
        [((elements * size_y, channels), f32)],
        place, field, total, known, sides, gather, wind, dyn_mix, row_a, row_b,
        smem=(0,), aliases={2: 0},
    )
    edge = ((size_x + 8, channels + 1), f32)
    half, to_a, to_b, sends, own_final = call(
        functools.partial(home_kernel, size_x, size_y, groups, capacity),
        [((elements * size_y, channels), f32), edge, edge, ((8 * groups, channels + 1), f32), ((rows, channels), f32)],
        [
            ((8 * groups, channels), f32),
            ((groups * rows, channels), f32),
            ((2, size_x, channels), f32),
        ],
        rank, edges, forcing, gather, spread, dyn_mix, crm_mix, own, *arrived,
        smem=(0,),
    )

    column_a, column_b = ring(to_a, to_b, "crm")
    rides = groups - 1 if all(i ^ j == groups - 1 for i, j in upper_pairs(groups)) else 0
    forcings = []
    for k in range(1, groups):
        if k == 1:
            forcings.append(column_a[size_x:])
        elif k == rides:
            forcings.append(column_b[size_x:])
        else:
            forcings.append(lax.ppermute(sends[8 * k : 8 * k + 8], "crm", xor[k]))
    (partial,) = call(
        functools.partial(fields_kernel, size_x, size_y, levels),
        [grid],
        [grid],
        second, wind, dyn_mix, slopes, half,
    )
    mine_a, mine_b = call(
        functools.partial(last_turn_kernel, size_x, size_y),
        [((size_y, channels), f32)] * 2,
        [((2, size_y, channels), f32)],
        rank, place, partial, column_a, column_b,
        smem=(0, 1),
    )
    row_a, row_b = ring(mine_a, mine_b, "elem")
    fields, crm_next = call(
        functools.partial(owner_kernel, size_x, size_y, groups, capacity),
        [grid, ((slots * columns, channels), clouds.dtype)],
        [
            grid,
            (((groups - 1) * rows, channels), f32),
            ((8 * (groups - 1), channels), f32),
            ((groups, lane_count, rows, 128), f32),
            ((groups, rows, channels), clouds.dtype),
            DMA((groups + 1,)),
        ],
        rank, partial, column_a, column_b, clouds, crm_mix, own_final, sends,
        *wide, *forcings,
        smem=(0,),
        far_out=(0, 1),
    )
    (third,) = call(
        functools.partial(finish_kernel, size_x, size_y),
        [grid],
        [((2, size_y, channels), f32), DMA((2,))],
        place, fields, mine_a, mine_b, row_a, row_b,
        smem=(0,), far=(1,), far_out=(0,), aliases={1: 0},
    )
    return (
        third.reshape(size_x, size_y, channels),
        crm_next.reshape(slots, columns, channels),
    )


def solution(mesh):
    return jax.shard_map(
        on_device,
        mesh=mesh,
        in_specs=(
            P("elem", "crm", None),
            P("elem", "crm", None),
            P(),
            P(("elem", "crm"), None),
            P(("elem", "crm"), None, None),
            P(),
        ),
        out_specs=(P("elem", "crm", None), P(("elem", "crm"), None, None)),
        check_vma=False,
    )
```
